256 devices in a mesh: dp: 64 (over y_lo, z, x), chan: 4 (over y_hi, core).
Axes of the slice: x: 4, y: 4 (y_hi: 2, y_lo: 2; y = y_hi * 2 + y_lo), z: 8, core: 2. Of those that a mesh axis runs over, the one named last changes fastest.
Arguments:
- inputs: bfloat16 [512, 128, 512], P(('dp', 'chan')), may hold values from -6 to 6
- cotangent: bfloat16 [512, 128, 512], P(('dp', 'chan')), may hold values from -24 to 24
- expand_w: bfloat16 [512, 2048], P(None, 'chan'), may hold values from -0.25 to 0.25
- expand_b: float32 [2048], P('chan'), may hold values from -3 to 3
- depth_k: float32 [25, 2048], P(None, 'chan'), may hold values from -1.25 to 1.25
- depth_b: float32 [2048], P('chan'), may hold values from -3 to 3
- project_w: bfloat16 [2048, 512], P('chan'), may hold values from -0.125 to 0.125
Outputs:
- input_grad: bfloat16 [512, 128, 512], P(('dp', 'chan'))
- expand_w_grad: float32 [512, 2048], P(None, 'chan')
- expand_b_grad: float32 [2048], P('chan')
- depth_k_grad: float32 [25, 2048], P(None, 'chan')
- depth_b_grad: float32 [2048], P('chan')
- project_w_grad: float32 [2048, 512], P('chan')
The draws below stay inside these ranges and needn't reach their ends.
All inputs are finite; a program needn't handle non-finite values.
Results may differ from the reference program's by a relative error of at most 0.007.
Values may be sent and summed in bfloat16 or wider, within the bound.
A program may use at most 64 MiB of HBM per device.

```python
import jax
import jax.numpy as jnp
from jax import lax

C = 512
H = 2048
WIDTH = 128
ROWS = 512


def spiked(values, own_key, source, target, blocks, factor):
    def block_of(dim):
        return (jnp.arange(values.shape[dim]) // (values.shape[dim] // blocks)).reshape((-1,) + (1,) * (values.ndim - 1 - dim))

    first = jax.random.permutation(own_key, blocks)[block_of(target)]
    far = (block_of(target) + blocks // 2) % blocks
    return jnp.where((block_of(source) == first) | (block_of(source) == far), factor * values, values)


def shard_levels(own_key, dims, pieces, low, top_value):
    def one(axis_at, parts):
        draws = jax.random.uniform(jax.random.fold_in(jax.random.fold_in(own_key, 6), axis_at), (parts,), jnp.float32, low / len(pieces), top_value / len(pieces))
        return jnp.repeat(jnp.exp(draws), dims[axis_at] // parts).reshape((-1,) + (1,) * (len(dims) - axis_at - 1))

    gain = one(*pieces[0])
    for cut in pieces[1:]:
        gain = gain * one(*cut)
    return gain


def scatter_about(own_key, shape, width, limit, split=(), kind=jnp.bfloat16):
    loudness = shard_levels(own_key, shape, split, -0.22, 0.18) if split else 1.0
    drawn = jax.random.normal(own_key, shape, jnp.float32) * width * loudness
    return jnp.minimum(jnp.maximum(drawn, -limit), limit).astype(kind)


def gaussian_with(stream_key, shape, scale, reach, split, heavy, kind=jnp.bfloat16):
    values = scale * jax.random.normal(stream_key, shape, jnp.float32)
    if split:
        values = values * shard_levels(stream_key, shape, split, -0.22, 0.18)
    return jnp.clip(spiked(values, jax.random.fold_in(stream_key, 3), *heavy), -reach, reach).astype(kind)


def setup_inputs(seed: int = 0) -> dict:
    seeds = jax.random.split(jax.random.key(seed), 8)
    return {
        "inputs": scatter_about(seeds[0], (ROWS, WIDTH, C), 1.0, 6.0, ((0, 256),)),
        "cotangent": gaussian_with(seeds[1], (ROWS, WIDTH, C), 1.0, 24.0, ((0, 256),), (0, 2, 256, 6.0)),
        "expand_w": scatter_about(seeds[2], (C, H), C ** -0.5, 0.25, ((1, 4),)),
        "expand_b": scatter_about(seeds[3], (H,), 0.5, 3.0, ((0, 4),), jnp.float32),
        "depth_k": scatter_about(seeds[4], (25, H), 25 ** -0.5, 1.25, ((1, 4),), jnp.float32),
        "depth_b": scatter_about(seeds[5], (H,), 0.5, 3.0, ((0, 4),), jnp.float32),
        "project_w": scatter_about(seeds[6], (H, C), H ** -0.5, 0.125, ((0, 4),)),
    }


def gelu_parts(pre):
    cdf = 0.5 * (1.0 + lax.erf(pre * 0.7071067811865476))
    dens = jnp.exp(-0.5 * pre * pre) * 0.3989422804014327
    return pre * cdf, cdf + pre * dens


def reference(inputs, cotangent, expand_w, expand_b, depth_k, depth_b, project_w):
    blocks = 4
    hblk = H // blocks
    nrows = inputs.shape[0]
    ncols = inputs.shape[1]
    flat_inputs = inputs.reshape(nrows * ncols, C)
    flat_cotan = cotangent.reshape(nrows * ncols, C)
    stack_w1 = expand_w.reshape(C, blocks, hblk).transpose(1, 0, 2)
    stack_b1 = expand_b.reshape(blocks, hblk)
    stack_k = depth_k.reshape(25, blocks, hblk).transpose(1, 0, 2)
    stack_bd = depth_b.reshape(blocks, hblk)
    stack_w2 = project_w.reshape(blocks, hblk, C)

    def one_block(total, weights):
        w_one, b_one, kernel, b_two, w_two = weights
        pre_one = jnp.dot(flat_inputs, w_one, preferred_element_type=jnp.float32).reshape(nrows, ncols, hblk) + b_one
        hidden, slope_one = gelu_parts(pre_one)
        hidden = hidden.astype(jnp.bfloat16)
        padded = jnp.pad(hidden, ((2, 2), (2, 2), (0, 0))).astype(jnp.float32)
        pre_two = jnp.zeros((nrows, ncols, hblk), jnp.float32) + b_two
        for row_tap in range(5):
            for col_tap in range(5):
                pre_two = pre_two + kernel[5 * row_tap + col_tap] * padded[row_tap:row_tap + nrows, col_tap:col_tap + ncols]
        mixed, slope_two = gelu_parts(pre_two)
        mixed = mixed.astype(jnp.bfloat16).reshape(nrows * ncols, hblk)
        grad_w2 = jnp.dot(mixed.T, flat_cotan, preferred_element_type=jnp.float32)
        grad_mixed = jnp.dot(flat_cotan, w_two.T, preferred_element_type=jnp.float32).reshape(nrows, ncols, hblk)
        grad_pre = (grad_mixed * slope_two).astype(jnp.bfloat16)
        grad_pre_f = grad_pre.astype(jnp.float32)
        grad_bd = jnp.sum(grad_pre_f, axis=(0, 1))
        grad_pad = jnp.pad(grad_pre_f, ((2, 2), (2, 2), (0, 0)))
        taps = []
        grad_hidden = jnp.zeros((nrows, ncols, hblk), jnp.float32)
        for row_tap in range(5):
            for col_tap in range(5):
                taps.append(jnp.sum(padded[row_tap:row_tap + nrows, col_tap:col_tap + ncols] * grad_pre_f, axis=(0, 1)))
                grad_hidden = grad_hidden + kernel[5 * row_tap + col_tap] * grad_pad[4 - row_tap:4 - row_tap + nrows, 4 - col_tap:4 - col_tap + ncols]
        grad_k = jnp.stack(taps, axis=0)
        grad_act = (grad_hidden * slope_one).astype(jnp.bfloat16).reshape(nrows * ncols, hblk)
        grad_b1 = jnp.sum(grad_act.astype(jnp.float32), axis=0)
        grad_w1 = jnp.dot(flat_inputs.T, grad_act, preferred_element_type=jnp.float32)
        partial_value = jnp.dot(grad_act, w_one.T, preferred_element_type=jnp.float32)
        return total + partial_value, (grad_w1, grad_b1, grad_k, grad_bd, grad_w2)

    start_total = jnp.zeros((nrows * ncols, C), jnp.float32)
    total, grads = lax.scan(one_block, start_total, (stack_w1, stack_b1, stack_k, stack_bd, stack_w2))
    grad_w1, grad_b1, grad_k, grad_bd, grad_w2 = grads
    input_grad = (flat_cotan.astype(jnp.float32) + total).astype(jnp.bfloat16).reshape(nrows, ncols, C)
    return (input_grad,
            grad_w1.transpose(1, 0, 2).reshape(C, H),
            grad_b1.reshape(H),
            grad_k.transpose(1, 0, 2).reshape(25, H),
            grad_bd.reshape(H),
            grad_w2.reshape(H, C))
```

```python
import jax
import jax.numpy as jnp
from jax import lax
from jax.sharding import Mesh, PartitionSpec as P

ROW_AXES = ("y_lo", "z", "x")
CHAN_AXES = ("y_hi", "core")


def extended(block, sides, width):
    for axis, dim in sides:
        count = 1
        for name in axis:
            count *= lax.axis_size(name)
        forward = [(i, i + 1) for i in range(count - 1)]
        backward = [(target, source) for source, target in forward]
        low = lax.ppermute(
            lax.slice_in_dim(block, block.shape[dim] - width, None, axis=dim), axis, forward
        )
        high = lax.ppermute(lax.slice_in_dim(block, 0, width, axis=dim), axis, backward)
        block = jnp.concatenate([low, block, high], axis=dim)
    return block


def gelu_parts(pre):
    cdf = 0.5 * (1.0 + lax.erf(pre * 0.7071067811865476))
    dens = jnp.exp(-0.5 * pre * pre) * 0.3989422804014327
    return (pre * cdf, cdf + pre * dens)


def ring_reduce_scatter(flat, axis):
    count = lax.axis_size(axis)
    index = lax.axis_index(axis)
    half = flat.shape[0] // 2
    parts = []
    for piece, step in ((flat[:half], 1), (flat[half:], -1)):
        blocks = piece.reshape(count, -1, piece.shape[-1])
        pairs = [(k, (k + step) % count) for k in range(count)]
        acc = blocks[(index - step) % count]
        for hop in range(1, count):
            acc = lax.ppermute(acc, axis, pairs)
            acc = acc + blocks[(index - step * (hop + 1)) % count]
        parts.append(acc)
    return jnp.concatenate(parts, axis=0)


def ring_all_gather(flat, axis):
    count = lax.axis_size(axis)
    index = lax.axis_index(axis)
    half = flat.shape[0] // 2
    parts = []
    for piece, step in ((flat[:half], 1), (flat[half:], -1)):
        pairs = [(k, (k + step) % count) for k in range(count)]
        got = [piece]
        for hop in range(1, count):
            got.append(lax.ppermute(got[-1], axis, pairs))
        if step == 1:
            order = jnp.stack(got[::-1], axis=0)
            start = (count - index - 1) % count
        else:
            order = jnp.stack(got, axis=0)
            start = (count - index) % count
        doubled = jnp.concatenate([order, order], axis=0)
        picked = lax.dynamic_slice_in_dim(doubled, start, count, axis=0)
        parts.append(picked.reshape(-1, piece.shape[-1]))
    return jnp.concatenate(parts, axis=0)


def row_group_sum(terms):
    width = terms[0].shape[-1]
    flat = jnp.concatenate([t.reshape(-1, width) for t in terms], axis=0)
    rows = flat.shape[0]
    quantum = 64
    padded_rows = -(-rows // quantum) * quantum
    flat = jnp.pad(flat, ((0, padded_rows - rows), (0, 0)))
    flat = ring_reduce_scatter(flat, "x")
    flat = ring_reduce_scatter(flat, "z")
    flat = flat + lax.ppermute(flat, "y_lo", [(0, 1), (1, 0)])
    flat = ring_all_gather(flat, "z")
    flat = ring_all_gather(flat, "x")
    out = []
    at = 0
    for t in terms:
        size = t.size // width
        out.append(flat[at : at + size].reshape(t.shape))
        at += size
    return out


def shards(inputs, cotangent, expand_w, expand_b, depth_k, depth_b, project_w):
    rows_in, rows_cot = (
        lax.all_gather(inputs, CHAN_AXES, axis=0, tiled=True),
        lax.all_gather(cotangent, CHAN_AXES, axis=0, tiled=True),
    )
    nrows, ncols, cin = rows_in.shape
    hslice = expand_w.shape[1]
    flat_inputs = rows_in.reshape(nrows * ncols, cin)
    flat_cotan = rows_cot.reshape(nrows * ncols, cin)
    pre_one = (
        jnp.dot(flat_inputs, expand_w, preferred_element_type=jnp.float32).reshape(
            nrows, ncols, hslice
        )
        + expand_b
    )
    hidden, slope_one = gelu_parts(pre_one)
    hidden = hidden.astype(jnp.bfloat16)
    rimmed = extended(hidden, ((ROW_AXES, 0),), 2)
    padded = jnp.pad(rimmed, ((0, 0), (2, 2), (0, 0))).astype(jnp.float32)
    pre_two = jnp.zeros((nrows, ncols, hslice), jnp.float32) + depth_b
    for row_tap in range(5):
        for col_tap in range(5):
            pre_two = (
                pre_two
                + depth_k[5 * row_tap + col_tap]
                * padded[row_tap : row_tap + nrows, col_tap : col_tap + ncols]
            )
    mixed, slope_two = gelu_parts(pre_two)
    mixed = mixed.astype(jnp.bfloat16).reshape(nrows * ncols, hslice)
    grad_w2 = jnp.dot(mixed.T, flat_cotan, preferred_element_type=jnp.float32)
    grad_mixed = jnp.dot(flat_cotan, project_w.T, preferred_element_type=jnp.float32).reshape(
        nrows, ncols, hslice
    )
    grad_pre = (grad_mixed * slope_two).astype(jnp.bfloat16)
    grad_pre_f = grad_pre.astype(jnp.float32)
    grad_bd = jnp.sum(grad_pre_f, axis=(0, 1))
    grad_rimmed = extended(grad_pre, ((ROW_AXES, 0),), 2)
    grad_pad = jnp.pad(grad_rimmed, ((0, 0), (2, 2), (0, 0))).astype(jnp.float32)
    taps = []
    grad_hidden = jnp.zeros((nrows, ncols, hslice), jnp.float32)
    for row_tap in range(5):
        for col_tap in range(5):
            taps.append(
                jnp.sum(
                    padded[row_tap : row_tap + nrows, col_tap : col_tap + ncols] * grad_pre_f,
                    axis=(0, 1),
                )
            )
            grad_hidden = (
                grad_hidden
                + depth_k[5 * row_tap + col_tap]
                * grad_pad[4 - row_tap : 4 - row_tap + nrows, 4 - col_tap : 4 - col_tap + ncols]
            )
    grad_k = jnp.stack(taps, axis=0)
    grad_act = (grad_hidden * slope_one).astype(jnp.bfloat16)
    flat_act = grad_act.reshape(nrows * ncols, hslice)
    grad_b1 = jnp.sum(flat_act.astype(jnp.float32), axis=0)
    grad_w1 = jnp.dot(flat_inputs.T, flat_act, preferred_element_type=jnp.float32)
    summed = row_group_sum([grad_w1, grad_b1[None], grad_k, grad_bd[None], grad_w2])
    summed[1] = summed[1][0]
    summed[3] = summed[3][0]
    own_part = lax.psum_scatter(
        jnp.einsum("rwh,ch->rwc", grad_act, expand_w, preferred_element_type=jnp.float32),
        CHAN_AXES,
        scatter_dimension=0,
        tiled=True,
    )
    input_grad = (cotangent.astype(jnp.float32) + own_part).astype(jnp.bfloat16)
    return (input_grad, summed[0], summed[1], summed[2], summed[3], summed[4])


def solution(mesh):
    fine = Mesh(mesh.devices.reshape(2, 8, 4, 2, 2), ROW_AXES + CHAN_AXES)
    rows = ROW_AXES + CHAN_AXES
    in_specs = (
        P(rows, None, None),
        P(rows, None, None),
        P(None, CHAN_AXES),
        P(CHAN_AXES),
        P(None, CHAN_AXES),
        P(CHAN_AXES),
        P(CHAN_AXES, None),
    )
    out_specs = (
        P(rows, None, None),
        P(None, CHAN_AXES),
        P(CHAN_AXES),
        P(None, CHAN_AXES),
        P(CHAN_AXES),
        P(CHAN_AXES, None),
    )
    return jax.shard_map(shards, mesh=fine, in_specs=in_specs, out_specs=out_specs, check_vma=False)
```

```python
import jax
import jax.numpy as jnp
from jax import lax
from jax.experimental import pallas as pl
from jax.experimental.pallas import tpu as pltpu
from jax.sharding import Mesh, PartitionSpec as P

MESH_ID = pl.DeviceIdType.MESH
ALL_AXES = ("y_lo", "z", "x", "y_hi", "core")
ROW_AXES = ("y_lo", "z", "x")
CHAN_AXES = ("y_hi", "core")


def _sum_kernel(nx, nz, data, out, xs, zs, ys, sems):
    (xsend, xrecv, zsend, zrecv, ysend, yrecv, gzsend, gzrecv, gxsend, gxrecv) = sems
    coords = [lax.axis_index(a) for a in ALL_AXES]
    iy, iz, ix = coords[0], coords[1], coords[2]

    def dev(y=None, z=None, x=None):
        c = list(coords)
        if y is not None:
            c[0] = y
        if z is not None:
            c[1] = z
        if x is not None:
            c[2] = x
        return tuple(c)

    x_next = [dev(x=lax.rem(ix + 1, nx)), dev(x=lax.rem(ix + nx - 1, nx))]
    z_next = [dev(z=lax.rem(iz + 1, nz)), dev(z=lax.rem(iz + nz - 1, nz))]
    partner = dev(y=1 - iy)

    barrier = pltpu.get_barrier_semaphore()
    for d in (x_next[0], x_next[1], z_next[0], z_next[1], partner):
        pl.semaphore_signal(barrier, inc=1, device_id=d, device_id_type=MESH_ID)
    pl.semaphore_wait(barrier, 5)

    rows = data.shape[0]
    half = rows // 2
    bx = half // nx
    bz = bx // nz
    steps = (1, -1)

    def xblock(h, k):
        return pl.ds(pl.multiple_of(h * half + lax.rem(k + 4 * nx, nx) * bx, 8), bx)

    def zblock(k):
        return pl.ds(pl.multiple_of(lax.rem(k + 4 * nz, nz) * bz, 8), bz)

    def oblock(h, kx, kz):
        at = h * half + lax.rem(kx + 4 * nx, nx) * bx + lax.rem(kz + 4 * nz, nz) * bz
        return pl.ds(pl.multiple_of(at, 8), bz)

    def obig(h, kx):
        return pl.ds(pl.multiple_of(h * half + lax.rem(kx + 4 * nx, nx) * bx, 8), bx)

    for s in range(nx - 1):
        copies = []
        for h in range(2):
            sg = steps[h]
            src = data.at[xblock(h, ix - sg)] if s == 0 else xs.at[h, s - 1]
            c = pltpu.make_async_remote_copy(
                src_ref=src, dst_ref=xs.at[h, s], send_sem=xsend.at[h * nx + s],
                recv_sem=xrecv.at[h * nx + s], device_id=x_next[h], device_id_type=MESH_ID)
            c.start()
            copies.append(c)
        for h in range(2):
            sg = steps[h]
            copies[h].wait_recv()
            xs[h, s] = xs[h, s] + data[xblock(h, ix - sg * (s + 2))]
            copies[h].wait_send()
    last = nx - 2
    for s in range(nz - 1):
        copies = []
        for h in range(2):
            sg = steps[h]
            src = xs.at[h, last, zblock(iz - sg)] if s == 0 else zs.at[h, s - 1]
            c = pltpu.make_async_remote_copy(
                src_ref=src, dst_ref=zs.at[h, s], send_sem=zsend.at[h * nz + s],
                recv_sem=zrecv.at[h * nz + s], device_id=z_next[h], device_id_type=MESH_ID)
            c.start()
            copies.append(c)
        for h in range(2):
            sg = steps[h]
            copies[h].wait_recv()
            zs[h, s] = zs[h, s] + xs[h, last, zblock(iz - sg * (s + 2))]
            copies[h].wait_send()
    zl = nz - 2
    c = pltpu.make_async_remote_copy(
        src_ref=zs.at[:, zl], dst_ref=ys, send_sem=ysend.at[0], recv_sem=yrecv.at[0],
        device_id=partner, device_id_type=MESH_ID)
    c.start()
    c.wait_recv()
    for h in range(2):
        out[oblock(h, ix, iz)] = zs[h, zl] + ys[h]
    c.wait_send()
    for s in range(nz - 1):
        copies = []
        for h in range(2):
            sg = steps[h]
            loc = oblock(h, ix, iz - sg * s)
            c = pltpu.make_async_remote_copy(
                src_ref=out.at[loc], dst_ref=out.at[loc], send_sem=gzsend.at[h * nz + s],
                recv_sem=gzrecv.at[h * nz + s], device_id=z_next[h], device_id_type=MESH_ID)
            c.start()
            copies.append(c)
        for h in range(2):
            copies[h].wait_recv()
            copies[h].wait_send()
    for s in range(nx - 1):
        copies = []
        for h in range(2):
            sg = steps[h]
            loc = obig(h, ix - sg * s)
            c = pltpu.make_async_remote_copy(
                src_ref=out.at[loc], dst_ref=out.at[loc], send_sem=gxsend.at[h * nx + s],
                recv_sem=gxrecv.at[h * nx + s], device_id=x_next[h], device_id_type=MESH_ID)
            c.start()
            copies.append(c)
        for h in range(2):
            copies[h].wait_recv()
            copies[h].wait_send()


def row_group_allreduce(flat, nx, nz):
    rows, cols = flat.shape
    half = rows // 2
    bx = half // nx
    bz = bx // nz
    sems = [pltpu.SemaphoreType.DMA((2 * nx,)), pltpu.SemaphoreType.DMA((2 * nx,)),
            pltpu.SemaphoreType.DMA((2 * nz,)), pltpu.SemaphoreType.DMA((2 * nz,)),
            pltpu.SemaphoreType.DMA((1,)), pltpu.SemaphoreType.DMA((1,)),
            pltpu.SemaphoreType.DMA((2 * nz,)), pltpu.SemaphoreType.DMA((2 * nz,)),
            pltpu.SemaphoreType.DMA((2 * nx,)), pltpu.SemaphoreType.DMA((2 * nx,))]

    def body(data, out, xs, zs, ys, *s):
        _sum_kernel(nx, nz, data, out, xs, zs, ys, s)

    return pl.pallas_call(
        body,
        out_shape=jax.ShapeDtypeStruct((rows, cols), jnp.float32),
        in_specs=[pl.BlockSpec(memory_space=pltpu.VMEM)],
        out_specs=pl.BlockSpec(memory_space=pltpu.VMEM),
        scratch_shapes=[
            pltpu.VMEM((2, nx - 1, bx, cols), jnp.float32),
            pltpu.VMEM((2, nz - 1, bz, cols), jnp.float32),
            pltpu.VMEM((2, bz, cols), jnp.float32),
        ] + sems,
        compiler_params=pltpu.CompilerParams(collective_id=0, has_side_effects=True,
                                             vmem_limit_bytes=48 * 1024 * 1024),
    )(flat)


def extended(block, sides, width):
    for axis, dim in sides:
        count = 1
        for name in axis:
            count *= lax.axis_size(name)
        forward = [(i, i + 1) for i in range(count - 1)]
        backward = [(target, source) for source, target in forward]
        low = lax.ppermute(
            lax.slice_in_dim(block, block.shape[dim] - width, None, axis=dim), axis, forward
        )
        high = lax.ppermute(lax.slice_in_dim(block, 0, width, axis=dim), axis, backward)
        block = jnp.concatenate([low, block, high], axis=dim)
    return block


def gelu_parts(pre):
    cdf = 0.5 * (1.0 + lax.erf(pre * 0.7071067811865476))
    dens = jnp.exp(-0.5 * pre * pre) * 0.3989422804014327
    return (pre * cdf, cdf + pre * dens)


def row_group_sum(terms):
    lanes = 128
    flat = jnp.concatenate([t.reshape(-1, lanes) for t in terms], axis=0)
    rows = flat.shape[0]
    nx, nz = lax.axis_size("x"), lax.axis_size("z")
    quantum = 16 * nx * nz
    padded_rows = -(-rows // quantum) * quantum
    flat = jnp.pad(flat, ((0, padded_rows - rows), (0, 0)))
    flat = row_group_allreduce(flat, nx, nz)
    out = []
    at = 0
    for t in terms:
        size = t.size // lanes
        out.append(flat[at : at + size].reshape(t.shape))
        at += size
    return out


def shards(inputs, cotangent, expand_w, expand_b, depth_k, depth_b, project_w):
    rows_in, rows_cot = (
        lax.all_gather(inputs, CHAN_AXES, axis=0, tiled=True),
        lax.all_gather(cotangent, CHAN_AXES, axis=0, tiled=True),
    )
    nrows, ncols, cin = rows_in.shape
    hslice = expand_w.shape[1]
    flat_inputs = rows_in.reshape(nrows * ncols, cin)
    flat_cotan = rows_cot.reshape(nrows * ncols, cin)
    pre_one = (
        jnp.dot(flat_inputs, expand_w, preferred_element_type=jnp.float32).reshape(
            nrows, ncols, hslice
        )
        + expand_b
    )
    hidden, slope_one = gelu_parts(pre_one)
    hidden = hidden.astype(jnp.bfloat16)
    rimmed = extended(hidden, ((ROW_AXES, 0),), 2)
    padded = jnp.pad(rimmed, ((0, 0), (2, 2), (0, 0))).astype(jnp.float32)
    pre_two = jnp.zeros((nrows, ncols, hslice), jnp.float32) + depth_b
    for row_tap in range(5):
        for col_tap in range(5):
            pre_two = (
                pre_two
                + depth_k[5 * row_tap + col_tap]
                * padded[row_tap : row_tap + nrows, col_tap : col_tap + ncols]
            )
    mixed, slope_two = gelu_parts(pre_two)
    mixed = mixed.astype(jnp.bfloat16).reshape(nrows * ncols, hslice)
    grad_w2 = jnp.dot(mixed.T, flat_cotan, preferred_element_type=jnp.float32)
    grad_mixed = jnp.dot(flat_cotan, project_w.T, preferred_element_type=jnp.float32).reshape(
        nrows, ncols, hslice
    )
    grad_pre = (grad_mixed * slope_two).astype(jnp.bfloat16)
    grad_pre_f = grad_pre.astype(jnp.float32)
    grad_bd = jnp.sum(grad_pre_f, axis=(0, 1))
    grad_rimmed = extended(grad_pre, ((ROW_AXES, 0),), 2)
    grad_pad = jnp.pad(grad_rimmed, ((0, 0), (2, 2), (0, 0))).astype(jnp.float32)
    taps = []
    grad_hidden = jnp.zeros((nrows, ncols, hslice), jnp.float32)
    for row_tap in range(5):
        for col_tap in range(5):
            taps.append(
                jnp.sum(
                    padded[row_tap : row_tap + nrows, col_tap : col_tap + ncols] * grad_pre_f,
                    axis=(0, 1),
                )
            )
            grad_hidden = (
                grad_hidden
                + depth_k[5 * row_tap + col_tap]
                * grad_pad[4 - row_tap : 4 - row_tap + nrows, 4 - col_tap : 4 - col_tap + ncols]
            )
    grad_k = jnp.stack(taps, axis=0)
    grad_act = (grad_hidden * slope_one).astype(jnp.bfloat16)
    flat_act = grad_act.reshape(nrows * ncols, hslice)
    grad_b1 = jnp.sum(flat_act.astype(jnp.float32), axis=0)
    grad_w1 = jnp.dot(flat_inputs.T, flat_act, preferred_element_type=jnp.float32)
    summed = row_group_sum([grad_w1, grad_b1[None], grad_k, grad_bd[None], grad_w2])
    summed[1] = summed[1][0]
    summed[3] = summed[3][0]
    own_part = lax.psum_scatter(
        jnp.einsum("rwh,ch->rwc", grad_act, expand_w, preferred_element_type=jnp.float32),
        CHAN_AXES,
        scatter_dimension=0,
        tiled=True,
    )
    input_grad = (cotangent.astype(jnp.float32) + own_part).astype(jnp.bfloat16)
    return (input_grad, summed[0], summed[1], summed[2], summed[3], summed[4])


def solution(mesh):
    fine = Mesh(mesh.devices.reshape(2, 8, 4, 2, 2), ROW_AXES + CHAN_AXES)
    rows = ROW_AXES + CHAN_AXES
    in_specs = (
        P(rows, None, None),
        P(rows, None, None),
        P(None, CHAN_AXES),
        P(CHAN_AXES),
        P(None, CHAN_AXES),
        P(CHAN_AXES),
        P(CHAN_AXES, None),
    )
    out_specs = (
        P(rows, None, None),
        P(None, CHAN_AXES),
        P(CHAN_AXES),
        P(None, CHAN_AXES),
        P(CHAN_AXES),
        P(CHAN_AXES, None),
    )
    return jax.shard_map(shards, mesh=fine, in_specs=in_specs, out_specs=out_specs, check_vma=False)
```

```python
import jax
import jax.numpy as jnp
from jax import lax
from jax.experimental import pallas as pl
from jax.experimental.pallas import tpu as pltpu
from jax.sharding import Mesh, PartitionSpec as P

MESH_ID = pl.DeviceIdType.MESH
ALL_AXES = ("y_lo", "z", "x", "y_hi", "core")
ROW_AXES = ("y_lo", "z", "x")
CHAN_AXES = ("y_hi", "core")


def _sum_kernel(nx, nz, data, out, xs, zs, ys, sems):
    (xsend, xrecv, zsend, zrecv, ysend, yrecv, gzsend, gzrecv, gxsend, gxrecv) = sems
    coords = [lax.axis_index(a) for a in ALL_AXES]
    iy, iz, ix = coords[0], coords[1], coords[2]

    def dev(y=None, z=None, x=None):
        c = list(coords)
        if y is not None:
            c[0] = y
        if z is not None:
            c[1] = z
        if x is not None:
            c[2] = x
        return tuple(c)

    x_next = [dev(x=lax.rem(ix + 1, nx)), dev(x=lax.rem(ix + nx - 1, nx))]
    z_next = [dev(z=lax.rem(iz + 1, nz)), dev(z=lax.rem(iz + nz - 1, nz))]
    partner = dev(y=1 - iy)

    barrier = pltpu.get_barrier_semaphore()
    z_peer = [None] + [dev(z=lax.rem(iz + d, nz)) for d in range(1, nz)]
    peers = [x_next[0], x_next[1], partner] + z_peer[1:]
    if nx == 2:
        peers = peers[1:]
    for d in peers:
        pl.semaphore_signal(barrier, inc=1, device_id=d, device_id_type=MESH_ID)
    pl.semaphore_wait(barrier, len(peers))

    rows = data.shape[0]
    half = rows // 2
    bx = half // nx
    bz = bx // nz
    steps = (1, -1)

    def xblock(h, k):
        return pl.ds(pl.multiple_of(h * half + lax.rem(k + 4 * nx, nx) * bx, 8), bx)

    def zblock(k):
        return pl.ds(pl.multiple_of(lax.rem(k + 4 * nz, nz) * bz, 8), bz)

    def oblock(h, kx, kz):
        at = h * half + lax.rem(kx + 4 * nx, nx) * bx + lax.rem(kz + 4 * nz, nz) * bz
        return pl.ds(pl.multiple_of(at, 8), bz)

    def obig(h, kx):
        return pl.ds(pl.multiple_of(h * half + lax.rem(kx + 4 * nx, nx) * bx, 8), bx)

    for s in range(nx - 1):
        copies = []
        for h in range(2):
            sg = steps[h]
            src = data.at[xblock(h, ix - sg)] if s == 0 else xs.at[h, s - 1]
            c = pltpu.make_async_remote_copy(
                src_ref=src, dst_ref=xs.at[h, s], send_sem=xsend.at[h * nx + s],
                recv_sem=xrecv.at[h * nx + s], device_id=x_next[h], device_id_type=MESH_ID)
            c.start()
            copies.append(c)
        for h in range(2):
            sg = steps[h]
            copies[h].wait_recv()
            xs[h, s] = xs[h, s] + data[xblock(h, ix - sg * (s + 2))]
            copies[h].wait_send()
    last = nx - 2
    copies = []
    for h in range(2):
        for d in range(1, nz):
            c = pltpu.make_async_remote_copy(
                src_ref=xs.at[h, last, zblock(iz + d)], dst_ref=zs.at[h, d - 1],
                send_sem=zsend.at[h * nz + d], recv_sem=zrecv.at[h * nz + d],
                device_id=z_peer[d], device_id_type=MESH_ID)
            c.start()
            copies.append(c)
    for c in copies:
        c.wait_recv()
    for h in range(2):
        acc = xs[h, last, zblock(iz)]
        for d in range(1, nz):
            acc = acc + zs[h, d - 1]
        zs[h, nz - 1] = acc
    for c in copies:
        c.wait_send()
    zl = nz - 1
    c = pltpu.make_async_remote_copy(
        src_ref=zs.at[:, zl], dst_ref=ys, send_sem=ysend.at[0], recv_sem=yrecv.at[0],
        device_id=partner, device_id_type=MESH_ID)
    c.start()
    c.wait_recv()
    for h in range(2):
        out[oblock(h, ix, iz)] = zs[h, zl] + ys[h]
    c.wait_send()
    copies = []
    for h in range(2):
        loc = oblock(h, ix, iz)
        for d in range(1, nz):
            c = pltpu.make_async_remote_copy(
                src_ref=out.at[loc], dst_ref=out.at[loc], send_sem=gzsend.at[h * nz + d],
                recv_sem=gzrecv.at[h * nz + d], device_id=z_peer[d], device_id_type=MESH_ID)
            c.start()
            copies.append(c)
    for c in copies:
        c.wait_recv()
    for c in copies:
        c.wait_send()
    for s in range(nx - 1):
        copies = []
        for h in range(2):
            sg = steps[h]
            loc = obig(h, ix - sg * s)
            c = pltpu.make_async_remote_copy(
                src_ref=out.at[loc], dst_ref=out.at[loc], send_sem=gxsend.at[h * nx + s],
                recv_sem=gxrecv.at[h * nx + s], device_id=x_next[h], device_id_type=MESH_ID)
            c.start()
            copies.append(c)
        for h in range(2):
            copies[h].wait_recv()
            copies[h].wait_send()


def row_group_allreduce(flat, nx, nz):
    rows, cols = flat.shape
    half = rows // 2
    bx = half // nx
    bz = bx // nz
    sems = [pltpu.SemaphoreType.DMA((2 * nx,)), pltpu.SemaphoreType.DMA((2 * nx,)),
            pltpu.SemaphoreType.DMA((2 * nz,)), pltpu.SemaphoreType.DMA((2 * nz,)),
            pltpu.SemaphoreType.DMA((1,)), pltpu.SemaphoreType.DMA((1,)),
            pltpu.SemaphoreType.DMA((2 * nz,)), pltpu.SemaphoreType.DMA((2 * nz,)),
            pltpu.SemaphoreType.DMA((2 * nx,)), pltpu.SemaphoreType.DMA((2 * nx,))]

    def body(data, out, xs, zs, ys, *s):
        _sum_kernel(nx, nz, data, out, xs, zs, ys, s)

    return pl.pallas_call(
        body,
        out_shape=jax.ShapeDtypeStruct((rows, cols), jnp.float32),
        in_specs=[pl.BlockSpec(memory_space=pltpu.VMEM)],
        out_specs=pl.BlockSpec(memory_space=pltpu.VMEM),
        scratch_shapes=[
            pltpu.VMEM((2, nx - 1, bx, cols), jnp.float32),
            pltpu.VMEM((2, nz, bz, cols), jnp.float32),
            pltpu.VMEM((2, bz, cols), jnp.float32),
        ] + sems,
        compiler_params=pltpu.CompilerParams(collective_id=0, has_side_effects=True,
                                             vmem_limit_bytes=48 * 1024 * 1024),
    )(flat)


def extended(block, sides, width):
    for axis, dim in sides:
        count = 1
        for name in axis:
            count *= lax.axis_size(name)
        forward = [(i, i + 1) for i in range(count - 1)]
        backward = [(target, source) for source, target in forward]
        low = lax.ppermute(
            lax.slice_in_dim(block, block.shape[dim] - width, None, axis=dim), axis, forward
        )
        high = lax.ppermute(lax.slice_in_dim(block, 0, width, axis=dim), axis, backward)
        block = jnp.concatenate([low, block, high], axis=dim)
    return block


def gelu_parts(pre):
    cdf = 0.5 * (1.0 + lax.erf(pre * 0.7071067811865476))
    dens = jnp.exp(-0.5 * pre * pre) * 0.3989422804014327
    return (pre * cdf, cdf + pre * dens)


def row_group_sum(terms):
    lanes = 128
    flat = jnp.concatenate([t.reshape(-1, lanes) for t in terms], axis=0)
    rows = flat.shape[0]
    nx, nz = lax.axis_size("x"), lax.axis_size("z")
    quantum = 16 * nx * nz
    padded_rows = -(-rows // quantum) * quantum
    flat = jnp.pad(flat, ((0, padded_rows - rows), (0, 0)))
    flat = row_group_allreduce(flat, nx, nz)
    out = []
    at = 0
    for t in terms:
        size = t.size // lanes
        out.append(flat[at : at + size].reshape(t.shape))
        at += size
    return out


def shards(inputs, cotangent, expand_w, expand_b, depth_k, depth_b, project_w):
    rows_in, rows_cot = (
        lax.all_gather(inputs, CHAN_AXES, axis=0, tiled=True),
        lax.all_gather(cotangent, CHAN_AXES, axis=0, tiled=True),
    )
    nrows, ncols, cin = rows_in.shape
    hslice = expand_w.shape[1]
    flat_inputs = rows_in.reshape(nrows * ncols, cin)
    flat_cotan = rows_cot.reshape(nrows * ncols, cin)
    pre_one = (
        jnp.dot(flat_inputs, expand_w, preferred_element_type=jnp.float32).reshape(
            nrows, ncols, hslice
        )
        + expand_b
    )
    hidden, slope_one = gelu_parts(pre_one)
    hidden = hidden.astype(jnp.bfloat16)
    rimmed = extended(hidden, ((ROW_AXES, 0),), 2)
    padded = jnp.pad(rimmed, ((0, 0), (2, 2), (0, 0))).astype(jnp.float32)
    pre_two = jnp.zeros((nrows, ncols, hslice), jnp.float32) + depth_b
    for row_tap in range(5):
        for col_tap in range(5):
            pre_two = (
                pre_two
                + depth_k[5 * row_tap + col_tap]
                * padded[row_tap : row_tap + nrows, col_tap : col_tap + ncols]
            )
    mixed, slope_two = gelu_parts(pre_two)
    mixed = mixed.astype(jnp.bfloat16).reshape(nrows * ncols, hslice)
    grad_w2 = jnp.dot(mixed.T, flat_cotan, preferred_element_type=jnp.float32)
    grad_mixed = jnp.dot(flat_cotan, project_w.T, preferred_element_type=jnp.float32).reshape(
        nrows, ncols, hslice
    )
    grad_pre = (grad_mixed * slope_two).astype(jnp.bfloat16)
    grad_pre_f = grad_pre.astype(jnp.float32)
    grad_bd = jnp.sum(grad_pre_f, axis=(0, 1))
    grad_rimmed = extended(grad_pre, ((ROW_AXES, 0),), 2)
    grad_pad = jnp.pad(grad_rimmed, ((0, 0), (2, 2), (0, 0))).astype(jnp.float32)
    taps = []
    grad_hidden = jnp.zeros((nrows, ncols, hslice), jnp.float32)
    for row_tap in range(5):
        for col_tap in range(5):
            taps.append(
                jnp.sum(
                    padded[row_tap : row_tap + nrows, col_tap : col_tap + ncols] * grad_pre_f,
                    axis=(0, 1),
                )
            )
            grad_hidden = (
                grad_hidden
                + depth_k[5 * row_tap + col_tap]
                * grad_pad[4 - row_tap : 4 - row_tap + nrows, 4 - col_tap : 4 - col_tap + ncols]
            )
    grad_k = jnp.stack(taps, axis=0)
    grad_act = (grad_hidden * slope_one).astype(jnp.bfloat16)
    flat_act = grad_act.reshape(nrows * ncols, hslice)
    grad_b1 = jnp.sum(flat_act.astype(jnp.float32), axis=0)
    grad_w1 = jnp.dot(flat_inputs.T, flat_act, preferred_element_type=jnp.float32)
    summed = row_group_sum([grad_w1, grad_b1[None], grad_k, grad_bd[None], grad_w2])
    summed[1] = summed[1][0]
    summed[3] = summed[3][0]
    own_part = lax.psum_scatter(
        jnp.einsum("rwh,ch->rwc", grad_act, expand_w, preferred_element_type=jnp.float32),
        CHAN_AXES,
        scatter_dimension=0,
        tiled=True,
    )
    input_grad = (cotangent.astype(jnp.float32) + own_part).astype(jnp.bfloat16)
    return (input_grad, summed[0], summed[1], summed[2], summed[3], summed[4])


def solution(mesh):
    fine = Mesh(mesh.devices.reshape(2, 8, 4, 2, 2), ROW_AXES + CHAN_AXES)
    rows = ROW_AXES + CHAN_AXES
    in_specs = (
        P(rows, None, None),
        P(rows, None, None),
        P(None, CHAN_AXES),
        P(CHAN_AXES),
        P(None, CHAN_AXES),
        P(CHAN_AXES),
        P(CHAN_AXES, None),
    )
    out_specs = (
        P(rows, None, None),
        P(None, CHAN_AXES),
        P(CHAN_AXES),
        P(None, CHAN_AXES),
        P(CHAN_AXES),
        P(CHAN_AXES, None),
    )
    return jax.shard_map(shards, mesh=fine, in_specs=in_specs, out_specs=out_specs, check_vma=False)
```

```python
import jax
import jax.numpy as jnp
from jax import lax
from jax.experimental import pallas as pl
from jax.experimental.pallas import tpu as pltpu
from jax.sharding import Mesh, PartitionSpec as P

MESH_ID = pl.DeviceIdType.MESH
ALL_AXES = ("y_lo", "z", "x", "y_hi", "core")
ROW_AXES = ("y_lo", "z", "x")
CHAN_AXES = ("y_hi", "core")


def _sum_kernel(nx, nz, data, out, xs, zs, ys, sems):
    (xsend, xrecv, zsend, zrecv, ysend, yrecv, gzsend, gzrecv, gxsend, gxrecv) = sems
    coords = [lax.axis_index(a) for a in ALL_AXES]
    iy, iz, ix = coords[0], coords[1], coords[2]

    def dev(y=None, z=None, x=None):
        c = list(coords)
        if y is not None:
            c[0] = y
        if z is not None:
            c[1] = z
        if x is not None:
            c[2] = x
        return tuple(c)

    x_next = [dev(x=lax.rem(ix + 1, nx)), dev(x=lax.rem(ix + nx - 1, nx))]
    z_next = [dev(z=lax.rem(iz + 1, nz)), dev(z=lax.rem(iz + nz - 1, nz))]
    partner = dev(y=1 - iy)

    barrier = pltpu.get_barrier_semaphore()
    z_peer = [None] + [dev(z=lax.rem(iz + d, nz)) for d in range(1, nz)]
    peers = [x_next[0], x_next[1], partner] + z_peer[1:]
    if nx == 2:
        peers = peers[1:]
    for d in peers:
        pl.semaphore_signal(barrier, inc=1, device_id=d, device_id_type=MESH_ID)
    pl.semaphore_wait(barrier, len(peers))

    rows = data.shape[0]
    half = rows // 2
    bx = half // nx
    bz = bx // nz
    steps = (1, -1)

    def xblock(h, k):
        return pl.ds(pl.multiple_of(h * half + lax.rem(k + 4 * nx, nx) * bx, 8), bx)

    def zblock(k):
        return pl.ds(pl.multiple_of(lax.rem(k + 4 * nz, nz) * bz, 8), bz)

    def oblock(h, kx, kz):
        at = h * half + lax.rem(kx + 4 * nx, nx) * bx + lax.rem(kz + 4 * nz, nz) * bz
        return pl.ds(pl.multiple_of(at, 8), bz)

    def obig(h, kx):
        return pl.ds(pl.multiple_of(h * half + lax.rem(kx + 4 * nx, nx) * bx, 8), bx)

    for s in range(nx - 1):
        copies = []
        for h in range(2):
            sg = steps[h]
            src = data.at[xblock(h, ix - sg)] if s == 0 else xs.at[h, s - 1]
            c = pltpu.make_async_remote_copy(
                src_ref=src, dst_ref=xs.at[h, s], send_sem=xsend.at[h * nx + s],
                recv_sem=xrecv.at[h * nx + s], device_id=x_next[h], device_id_type=MESH_ID)
            c.start()
            copies.append(c)
        for h in range(2):
            sg = steps[h]
            copies[h].wait_recv()
            xs[h, s] = xs[h, s] + data[xblock(h, ix - sg * (s + 2))]
            copies[h].wait_send()
    last = nx - 2
    copies = []
    for h in range(2):
        for d in range(1, nz):
            c = pltpu.make_async_remote_copy(
                src_ref=xs.at[h, last, zblock(iz + d)], dst_ref=zs.at[h, d - 1],
                send_sem=zsend.at[h * nz + d], recv_sem=zrecv.at[h * nz + d],
                device_id=z_peer[d], device_id_type=MESH_ID)
            c.start()
            copies.append(c)
    for c in copies:
        c.wait_recv()
    for h in range(2):
        acc = xs[h, last, zblock(iz)]
        for d in range(1, nz):
            acc = acc + zs[h, d - 1]
        zs[h, nz - 1] = acc
    for c in copies:
        c.wait_send()
    zl = nz - 1
    c = pltpu.make_async_remote_copy(
        src_ref=zs.at[:, zl], dst_ref=ys, send_sem=ysend.at[0], recv_sem=yrecv.at[0],
        device_id=partner, device_id_type=MESH_ID)
    c.start()
    c.wait_recv()
    for h in range(2):
        out[oblock(h, ix, iz)] = zs[h, zl] + ys[h]
    c.wait_send()
    copies = []
    for h in range(2):
        loc = oblock(h, ix, iz)
        for d in range(1, nz):
            c = pltpu.make_async_remote_copy(
                src_ref=out.at[loc], dst_ref=out.at[loc], send_sem=gzsend.at[h * nz + d],
                recv_sem=gzrecv.at[h * nz + d], device_id=z_peer[d], device_id_type=MESH_ID)
            c.start()
            copies.append(c)
    for c in copies:
        c.wait_recv()
    for c in copies:
        c.wait_send()
    for s in range(nx - 1):
        copies = []
        for h in range(2):
            sg = steps[h]
            loc = obig(h, ix - sg * s)
            c = pltpu.make_async_remote_copy(
                src_ref=out.at[loc], dst_ref=out.at[loc], send_sem=gxsend.at[h * nx + s],
                recv_sem=gxrecv.at[h * nx + s], device_id=x_next[h], device_id_type=MESH_ID)
            c.start()
            copies.append(c)
        for h in range(2):
            copies[h].wait_recv()
            copies[h].wait_send()


def row_group_allreduce(flat, nx, nz):
    rows, cols = flat.shape
    half = rows // 2
    bx = half // nx
    bz = bx // nz
    sems = [pltpu.SemaphoreType.DMA((2 * nx,)), pltpu.SemaphoreType.DMA((2 * nx,)),
            pltpu.SemaphoreType.DMA((2 * nz,)), pltpu.SemaphoreType.DMA((2 * nz,)),
            pltpu.SemaphoreType.DMA((1,)), pltpu.SemaphoreType.DMA((1,)),
            pltpu.SemaphoreType.DMA((2 * nz,)), pltpu.SemaphoreType.DMA((2 * nz,)),
            pltpu.SemaphoreType.DMA((2 * nx,)), pltpu.SemaphoreType.DMA((2 * nx,))]

    def body(data, out, xs, zs, ys, *s):
        _sum_kernel(nx, nz, data, out, xs, zs, ys, s)

    return pl.pallas_call(
        body,
        out_shape=jax.ShapeDtypeStruct((rows, cols), jnp.float32),
        in_specs=[pl.BlockSpec(memory_space=pltpu.VMEM)],
        out_specs=pl.BlockSpec(memory_space=pltpu.VMEM),
        scratch_shapes=[
            pltpu.VMEM((2, nx - 1, bx, cols), jnp.float32),
            pltpu.VMEM((2, nz, bz, cols), jnp.float32),
            pltpu.VMEM((2, bz, cols), jnp.float32),
        ] + sems,
        compiler_params=pltpu.CompilerParams(collective_id=0, has_side_effects=True,
                                             vmem_limit_bytes=48 * 1024 * 1024),
    )(flat)


def _chan_gather_kernel(first, second, out_first, out_second, sems):
    coords = [lax.axis_index(a) for a in ALL_AXES]
    hi, core = coords[3], coords[4]

    def dev(h, c):
        return (coords[0], coords[1], coords[2], h, c)

    me = hi * 2 + core
    across = hi * 2 + (1 - core)
    over = (1 - hi) * 2 + core
    pair, far = dev(hi, 1 - core), dev(1 - hi, core)

    barrier = pltpu.get_barrier_semaphore()
    for d in (pair, far):
        pl.semaphore_signal(barrier, inc=1, device_id=d, device_id_type=MESH_ID)
    pl.semaphore_wait(barrier, 2)

    sources = (first, second)
    outs = (out_first, out_second)
    step_one = []
    for k in range(2):
        for j, target in enumerate((pair, far)):
            c = pltpu.make_async_remote_copy(
                src_ref=sources[k], dst_ref=outs[k].at[me], send_sem=sems.at[0, k, j],
                recv_sem=sems.at[1, k, j], device_id=target, device_id_type=MESH_ID)
            c.start()
            step_one.append(c)
    for k in range(2):
        outs[k][me] = sources[k][...]
    for c in step_one:
        c.wait_recv()
    relay = []
    for k in range(2):
        c = pltpu.make_async_remote_copy(
            src_ref=outs[k].at[over], dst_ref=outs[k].at[over], send_sem=sems.at[0, k, 2],
            recv_sem=sems.at[1, k, 2], device_id=pair, device_id_type=MESH_ID)
        c.start()
        relay.append(c)
    for c in relay:
        c.wait_recv()
    for c in step_one + relay:
        c.wait_send()


def chan_gather(first, second):
    shape = (4,) + first.shape
    result = pl.pallas_call(
        _chan_gather_kernel,
        out_shape=(jax.ShapeDtypeStruct(shape, first.dtype), jax.ShapeDtypeStruct(shape, second.dtype)),
        in_specs=[pl.BlockSpec(memory_space=pltpu.VMEM)] * 2,
        out_specs=(pl.BlockSpec(memory_space=pltpu.VMEM),) * 2,
        scratch_shapes=[pltpu.SemaphoreType.DMA((2, 2, 3))],
        compiler_params=pltpu.CompilerParams(collective_id=1, has_side_effects=True),
    )(first, second)
    return tuple(r.reshape((-1,) + first.shape[1:]) for r in result)


def extended(block, sides, width):
    for axis, dim in sides:
        count = 1
        for name in axis:
            count *= lax.axis_size(name)
        forward = [(i, i + 1) for i in range(count - 1)]
        backward = [(target, source) for source, target in forward]
        low = lax.ppermute(
            lax.slice_in_dim(block, block.shape[dim] - width, None, axis=dim), axis, forward
        )
        high = lax.ppermute(lax.slice_in_dim(block, 0, width, axis=dim), axis, backward)
        block = jnp.concatenate([low, block, high], axis=dim)
    return block


def gelu_parts(pre):
    cdf = 0.5 * (1.0 + lax.erf(pre * 0.7071067811865476))
    dens = jnp.exp(-0.5 * pre * pre) * 0.3989422804014327
    return (pre * cdf, cdf + pre * dens)


def row_group_sum(terms):
    lanes = 128
    flat = jnp.concatenate([t.reshape(-1, lanes) for t in terms], axis=0)
    rows = flat.shape[0]
    nx, nz = lax.axis_size("x"), lax.axis_size("z")
    quantum = 16 * nx * nz
    padded_rows = -(-rows // quantum) * quantum
    flat = jnp.pad(flat, ((0, padded_rows - rows), (0, 0)))
    flat = row_group_allreduce(flat, nx, nz)
    out = []
    at = 0
    for t in terms:
        size = t.size // lanes
        out.append(flat[at : at + size].reshape(t.shape))
        at += size
    return out


def shards(inputs, cotangent, expand_w, expand_b, depth_k, depth_b, project_w):
    rows_in, rows_cot = chan_gather(inputs, cotangent)
    nrows, ncols, cin = rows_in.shape
    hslice = expand_w.shape[1]
    flat_inputs = rows_in.reshape(nrows * ncols, cin)
    flat_cotan = rows_cot.reshape(nrows * ncols, cin)
    pre_one = (
        jnp.dot(flat_inputs, expand_w, preferred_element_type=jnp.float32).reshape(
            nrows, ncols, hslice
        )
        + expand_b
    )
    hidden, slope_one = gelu_parts(pre_one)
    hidden = hidden.astype(jnp.bfloat16)
    rimmed = extended(hidden, ((ROW_AXES, 0),), 2)
    padded = jnp.pad(rimmed, ((0, 0), (2, 2), (0, 0))).astype(jnp.float32)
    pre_two = jnp.zeros((nrows, ncols, hslice), jnp.float32) + depth_b
    for row_tap in range(5):
        for col_tap in range(5):
            pre_two = (
                pre_two
                + depth_k[5 * row_tap + col_tap]
                * padded[row_tap : row_tap + nrows, col_tap : col_tap + ncols]
            )
    mixed, slope_two = gelu_parts(pre_two)
    mixed = mixed.astype(jnp.bfloat16).reshape(nrows * ncols, hslice)
    grad_w2 = jnp.dot(mixed.T, flat_cotan, preferred_element_type=jnp.float32)
    grad_mixed = jnp.dot(flat_cotan, project_w.T, preferred_element_type=jnp.float32).reshape(
        nrows, ncols, hslice
    )
    grad_pre = (grad_mixed * slope_two).astype(jnp.bfloat16)
    grad_pre_f = grad_pre.astype(jnp.float32)
    grad_bd = jnp.sum(grad_pre_f, axis=(0, 1))
    grad_rimmed = extended(grad_pre, ((ROW_AXES, 0),), 2)
    grad_pad = jnp.pad(grad_rimmed, ((0, 0), (2, 2), (0, 0))).astype(jnp.float32)
    taps = []
    grad_hidden = jnp.zeros((nrows, ncols, hslice), jnp.float32)
    for row_tap in range(5):
        for col_tap in range(5):
            taps.append(
                jnp.sum(
                    padded[row_tap : row_tap + nrows, col_tap : col_tap + ncols] * grad_pre_f,
                    axis=(0, 1),
                )
            )
            grad_hidden = (
                grad_hidden
                + depth_k[5 * row_tap + col_tap]
                * grad_pad[4 - row_tap : 4 - row_tap + nrows, 4 - col_tap : 4 - col_tap + ncols]
            )
    grad_k = jnp.stack(taps, axis=0)
    grad_act = (grad_hidden * slope_one).astype(jnp.bfloat16)
    flat_act = grad_act.reshape(nrows * ncols, hslice)
    grad_b1 = jnp.sum(flat_act.astype(jnp.float32), axis=0)
    grad_w1 = jnp.dot(flat_inputs.T, flat_act, preferred_element_type=jnp.float32)
    summed = row_group_sum([grad_w1, grad_b1[None], grad_k, grad_bd[None], grad_w2])
    summed[1] = summed[1][0]
    summed[3] = summed[3][0]
    own_part = lax.psum_scatter(
        jnp.einsum("rwh,ch->rwc", grad_act, expand_w, preferred_element_type=jnp.float32),
        CHAN_AXES,
        scatter_dimension=0,
        tiled=True,
    )
    input_grad = (cotangent.astype(jnp.float32) + own_part).astype(jnp.bfloat16)
    return (input_grad, summed[0], summed[1], summed[2], summed[3], summed[4])


def solution(mesh):
    fine = Mesh(mesh.devices.reshape(2, 8, 4, 2, 2), ROW_AXES + CHAN_AXES)
    rows = ROW_AXES + CHAN_AXES
    in_specs = (
        P(rows, None, None),
        P(rows, None, None),
        P(None, CHAN_AXES),
        P(CHAN_AXES),
        P(None, CHAN_AXES),
        P(CHAN_AXES),
        P(CHAN_AXES, None),
    )
    out_specs = (
        P(rows, None, None),
        P(None, CHAN_AXES),
        P(CHAN_AXES),
        P(None, CHAN_AXES),
        P(CHAN_AXES),
        P(CHAN_AXES, None),
    )
    return jax.shard_map(shards, mesh=fine, in_specs=in_specs, out_specs=out_specs, check_vma=False)
```

```python
import functools

import jax
import jax.numpy as jnp
from jax import lax
from jax.experimental import pallas as pl
from jax.experimental.pallas import tpu as pltpu
from jax.sharding import Mesh, PartitionSpec as P

MESH_ID = pl.DeviceIdType.MESH
ALL_AXES = ("y_lo", "z", "x", "y_hi", "core")
ROW_AXES = ("y_lo", "z", "x")
CHAN_AXES = ("y_hi", "core")


def _sum_kernel(nx, nz, data, out, xs, zs, ys, sems):
    (xsend, xrecv, zsend, zrecv, ysend, yrecv, gzsend, gzrecv, gxsend, gxrecv) = sems
    coords = [lax.axis_index(a) for a in ALL_AXES]
    iy, iz, ix = coords[0], coords[1], coords[2]

    def dev(y=None, z=None, x=None):
        c = list(coords)
        if y is not None:
            c[0] = y
        if z is not None:
            c[1] = z
        if x is not None:
            c[2] = x
        return tuple(c)

    x_next = [dev(x=lax.rem(ix + 1, nx)), dev(x=lax.rem(ix + nx - 1, nx))]
    z_next = [dev(z=lax.rem(iz + 1, nz)), dev(z=lax.rem(iz + nz - 1, nz))]
    partner = dev(y=1 - iy)

    barrier = pltpu.get_barrier_semaphore()
    z_peer = [None] + [dev(z=lax.rem(iz + d, nz)) for d in range(1, nz)]
    peers = [x_next[0], x_next[1], partner] + z_peer[1:]
    if nx == 2:
        peers = peers[1:]
    for d in peers:
        pl.semaphore_signal(barrier, inc=1, device_id=d, device_id_type=MESH_ID)
    pl.semaphore_wait(barrier, len(peers))

    rows = data.shape[0]
    half = rows // 2
    bx = half // nx
    bz = bx // nz
    steps = (1, -1)

    def xblock(h, k):
        return pl.ds(pl.multiple_of(h * half + lax.rem(k + 4 * nx, nx) * bx, 8), bx)

    def zblock(k):
        return pl.ds(pl.multiple_of(lax.rem(k + 4 * nz, nz) * bz, 8), bz)

    def oblock(h, kx, kz):
        at = h * half + lax.rem(kx + 4 * nx, nx) * bx + lax.rem(kz + 4 * nz, nz) * bz
        return pl.ds(pl.multiple_of(at, 8), bz)

    def obig(h, kx):
        return pl.ds(pl.multiple_of(h * half + lax.rem(kx + 4 * nx, nx) * bx, 8), bx)

    for s in range(nx - 1):
        copies = []
        for h in range(2):
            sg = steps[h]
            src = data.at[xblock(h, ix - sg)] if s == 0 else xs.at[h, s - 1]
            c = pltpu.make_async_remote_copy(
                src_ref=src, dst_ref=xs.at[h, s], send_sem=xsend.at[h * nx + s],
                recv_sem=xrecv.at[h * nx + s], device_id=x_next[h], device_id_type=MESH_ID)
            c.start()
            copies.append(c)
        for h in range(2):
            sg = steps[h]
            copies[h].wait_recv()
            xs[h, s] = xs[h, s] + data[xblock(h, ix - sg * (s + 2))]
            copies[h].wait_send()
    last = nx - 2
    copies = []
    for h in range(2):
        for d in range(1, nz):
            c = pltpu.make_async_remote_copy(
                src_ref=xs.at[h, last, zblock(iz + d)], dst_ref=zs.at[h, d - 1],
                send_sem=zsend.at[h * nz + d], recv_sem=zrecv.at[h * nz + d],
                device_id=z_peer[d], device_id_type=MESH_ID)
            c.start()
            copies.append(c)
    for c in copies:
        c.wait_recv()
    for h in range(2):
        acc = xs[h, last, zblock(iz)]
        for d in range(1, nz):
            acc = acc + zs[h, d - 1]
        zs[h, nz - 1] = acc
    for c in copies:
        c.wait_send()
    zl = nz - 1
    c = pltpu.make_async_remote_copy(
        src_ref=zs.at[:, zl], dst_ref=ys, send_sem=ysend.at[0], recv_sem=yrecv.at[0],
        device_id=partner, device_id_type=MESH_ID)
    c.start()
    c.wait_recv()
    for h in range(2):
        out[oblock(h, ix, iz)] = zs[h, zl] + ys[h]
    c.wait_send()
    copies = []
    for h in range(2):
        loc = oblock(h, ix, iz)
        for d in range(1, nz):
            c = pltpu.make_async_remote_copy(
                src_ref=out.at[loc], dst_ref=out.at[loc], send_sem=gzsend.at[h * nz + d],
                recv_sem=gzrecv.at[h * nz + d], device_id=z_peer[d], device_id_type=MESH_ID)
            c.start()
            copies.append(c)
    for c in copies:
        c.wait_recv()
    for c in copies:
        c.wait_send()
    for s in range(nx - 1):
        copies = []
        for h in range(2):
            sg = steps[h]
            loc = obig(h, ix - sg * s)
            c = pltpu.make_async_remote_copy(
                src_ref=out.at[loc], dst_ref=out.at[loc], send_sem=gxsend.at[h * nx + s],
                recv_sem=gxrecv.at[h * nx + s], device_id=x_next[h], device_id_type=MESH_ID)
            c.start()
            copies.append(c)
        for h in range(2):
            copies[h].wait_recv()
            copies[h].wait_send()


def row_group_allreduce(flat, nx, nz):
    rows, cols = flat.shape
    half = rows // 2
    bx = half // nx
    bz = bx // nz
    sems = [pltpu.SemaphoreType.DMA((2 * nx,)), pltpu.SemaphoreType.DMA((2 * nx,)),
            pltpu.SemaphoreType.DMA((2 * nz,)), pltpu.SemaphoreType.DMA((2 * nz,)),
            pltpu.SemaphoreType.DMA((1,)), pltpu.SemaphoreType.DMA((1,)),
            pltpu.SemaphoreType.DMA((2 * nz,)), pltpu.SemaphoreType.DMA((2 * nz,)),
            pltpu.SemaphoreType.DMA((2 * nx,)), pltpu.SemaphoreType.DMA((2 * nx,))]

    def body(data, out, xs, zs, ys, *s):
        _sum_kernel(nx, nz, data, out, xs, zs, ys, s)

    return pl.pallas_call(
        body,
        out_shape=jax.ShapeDtypeStruct((rows, cols), jnp.float32),
        in_specs=[pl.BlockSpec(memory_space=pltpu.VMEM)],
        out_specs=pl.BlockSpec(memory_space=pltpu.VMEM),
        scratch_shapes=[
            pltpu.VMEM((2, nx - 1, bx, cols), jnp.float32),
            pltpu.VMEM((2, nz, bz, cols), jnp.float32),
            pltpu.VMEM((2, bz, cols), jnp.float32),
        ] + sems,
        compiler_params=pltpu.CompilerParams(collective_id=0, has_side_effects=True,
                                             vmem_limit_bytes=48 * 1024 * 1024),
    )(flat)


def _chan_gather_kernel(first, second, out_first, out_second, sems):
    coords = [lax.axis_index(a) for a in ALL_AXES]
    hi, core = coords[3], coords[4]

    def dev(h, c):
        return (coords[0], coords[1], coords[2], h, c)

    me = hi * 2 + core
    across = hi * 2 + (1 - core)
    over = (1 - hi) * 2 + core
    pair, far = dev(hi, 1 - core), dev(1 - hi, core)

    barrier = pltpu.get_barrier_semaphore()
    for d in (pair, far):
        pl.semaphore_signal(barrier, inc=1, device_id=d, device_id_type=MESH_ID)
    pl.semaphore_wait(barrier, 2)

    sources = (first, second)
    outs = (out_first, out_second)
    step_one = []
    for k in range(2):
        for j, target in enumerate((pair, far)):
            c = pltpu.make_async_remote_copy(
                src_ref=sources[k], dst_ref=outs[k].at[me], send_sem=sems.at[0, k, j],
                recv_sem=sems.at[1, k, j], device_id=target, device_id_type=MESH_ID)
            c.start()
            step_one.append(c)
    for k in range(2):
        outs[k][me] = sources[k][...]
    for c in step_one:
        c.wait_recv()
    relay = []
    for k in range(2):
        c = pltpu.make_async_remote_copy(
            src_ref=outs[k].at[over], dst_ref=outs[k].at[over], send_sem=sems.at[0, k, 2],
            recv_sem=sems.at[1, k, 2], device_id=pair, device_id_type=MESH_ID)
        c.start()
        relay.append(c)
    for c in relay:
        c.wait_recv()
    for c in step_one + relay:
        c.wait_send()


def chan_gather(first, second):
    shape = (4,) + first.shape
    result = pl.pallas_call(
        _chan_gather_kernel,
        out_shape=(jax.ShapeDtypeStruct(shape, first.dtype), jax.ShapeDtypeStruct(shape, second.dtype)),
        in_specs=[pl.BlockSpec(memory_space=pltpu.VMEM)] * 2,
        out_specs=(pl.BlockSpec(memory_space=pltpu.VMEM),) * 2,
        scratch_shapes=[pltpu.SemaphoreType.DMA((2, 2, 3))],
        compiler_params=pltpu.CompilerParams(collective_id=1, has_side_effects=True),
    )(first, second)
    return tuple(r.reshape((-1,) + first.shape[1:]) for r in result)


def _halo_kernel(width, block, low, high, sems):
    coords = [lax.axis_index(a) for a in ALL_AXES]
    ny, nz, nx = (lax.axis_size(a) for a in ROW_AXES)
    count = ny * nz * nx
    me = (coords[0] * nz + coords[1]) * nx + coords[2]

    def dev(index):
        index = lax.rem(index + count, count)
        return (index // (nz * nx), lax.rem(index // nx, nz), lax.rem(index, nx), coords[3], coords[4])

    up, down = dev(me + 1), dev(me - 1)
    barrier = pltpu.get_barrier_semaphore()
    for d in (up, down):
        pl.semaphore_signal(barrier, inc=1, device_id=d, device_id_type=MESH_ID)
    pl.semaphore_wait(barrier, 2)
    rows = block.shape[0]
    copies = [
        pltpu.make_async_remote_copy(
            src_ref=block.at[pl.ds(rows - width, width)], dst_ref=low, send_sem=sems.at[0, 0],
            recv_sem=sems.at[1, 0], device_id=up, device_id_type=MESH_ID),
        pltpu.make_async_remote_copy(
            src_ref=block.at[pl.ds(0, width)], dst_ref=high, send_sem=sems.at[0, 1],
            recv_sem=sems.at[1, 1], device_id=down, device_id_type=MESH_ID),
    ]
    for c in copies:
        c.start()
    for c in copies:
        c.wait_recv()
    for c in copies:
        c.wait_send()


def with_halo(block, width):
    edge = jax.ShapeDtypeStruct((width,) + block.shape[1:], block.dtype)
    low, high = pl.pallas_call(
        functools.partial(_halo_kernel, width),
        out_shape=(edge, edge),
        in_specs=[pl.BlockSpec(memory_space=pl.ANY)],
        out_specs=(pl.BlockSpec(memory_space=pltpu.VMEM),) * 2,
        scratch_shapes=[pltpu.SemaphoreType.DMA((2, 2))],
        compiler_params=pltpu.CompilerParams(collective_id=2, has_side_effects=True),
    )(block)
    ny, nz, nx = (lax.axis_size(a) for a in ROW_AXES)
    me = (lax.axis_index("y_lo") * nz + lax.axis_index("z")) * nx + lax.axis_index("x")
    low = jnp.where(me == 0, jnp.zeros_like(low), low)
    high = jnp.where(me == ny * nz * nx - 1, jnp.zeros_like(high), high)
    return jnp.concatenate([low, block, high], axis=0)


def gelu_parts(pre):
    cdf = 0.5 * (1.0 + lax.erf(pre * 0.7071067811865476))
    dens = jnp.exp(-0.5 * pre * pre) * 0.3989422804014327
    return (pre * cdf, cdf + pre * dens)


def row_group_sum(terms):
    lanes = 128
    flat = jnp.concatenate([t.reshape(-1, lanes) for t in terms], axis=0)
    rows = flat.shape[0]
    nx, nz = lax.axis_size("x"), lax.axis_size("z")
    quantum = 16 * nx * nz
    padded_rows = -(-rows // quantum) * quantum
    flat = jnp.pad(flat, ((0, padded_rows - rows), (0, 0)))
    flat = row_group_allreduce(flat, nx, nz)
    out = []
    at = 0
    for t in terms:
        size = t.size // lanes
        out.append(flat[at : at + size].reshape(t.shape))
        at += size
    return out


def shards(inputs, cotangent, expand_w, expand_b, depth_k, depth_b, project_w):
    rows_in, rows_cot = chan_gather(inputs, cotangent)
    nrows, ncols, cin = rows_in.shape
    hslice = expand_w.shape[1]
    flat_inputs = rows_in.reshape(nrows * ncols, cin)
    flat_cotan = rows_cot.reshape(nrows * ncols, cin)
    pre_one = (
        jnp.dot(flat_inputs, expand_w, preferred_element_type=jnp.float32).reshape(
            nrows, ncols, hslice
        )
        + expand_b
    )
    hidden, slope_one = gelu_parts(pre_one)
    hidden = hidden.astype(jnp.bfloat16)
    rimmed = with_halo(hidden, 2)
    padded = jnp.pad(rimmed, ((0, 0), (2, 2), (0, 0))).astype(jnp.float32)
    pre_two = jnp.zeros((nrows, ncols, hslice), jnp.float32) + depth_b
    for row_tap in range(5):
        for col_tap in range(5):
            pre_two = (
                pre_two
                + depth_k[5 * row_tap + col_tap]
                * padded[row_tap : row_tap + nrows, col_tap : col_tap + ncols]
            )
    mixed, slope_two = gelu_parts(pre_two)
    mixed = mixed.astype(jnp.bfloat16).reshape(nrows * ncols, hslice)
    grad_w2 = jnp.dot(mixed.T, flat_cotan, preferred_element_type=jnp.float32)
    grad_mixed = jnp.dot(flat_cotan, project_w.T, preferred_element_type=jnp.float32).reshape(
        nrows, ncols, hslice
    )
    grad_pre = (grad_mixed * slope_two).astype(jnp.bfloat16)
    grad_pre_f = grad_pre.astype(jnp.float32)
    grad_bd = jnp.sum(grad_pre_f, axis=(0, 1))
    grad_rimmed = with_halo(grad_pre, 2)
    grad_pad = jnp.pad(grad_rimmed, ((0, 0), (2, 2), (0, 0))).astype(jnp.float32)
    taps = []
    grad_hidden = jnp.zeros((nrows, ncols, hslice), jnp.float32)
    for row_tap in range(5):
        for col_tap in range(5):
            taps.append(
                jnp.sum(
                    padded[row_tap : row_tap + nrows, col_tap : col_tap + ncols] * grad_pre_f,
                    axis=(0, 1),
                )
            )
            grad_hidden = (
                grad_hidden
                + depth_k[5 * row_tap + col_tap]
                * grad_pad[4 - row_tap : 4 - row_tap + nrows, 4 - col_tap : 4 - col_tap + ncols]
            )
    grad_k = jnp.stack(taps, axis=0)
    grad_act = (grad_hidden * slope_one).astype(jnp.bfloat16)
    flat_act = grad_act.reshape(nrows * ncols, hslice)
    grad_b1 = jnp.sum(flat_act.astype(jnp.float32), axis=0)
    grad_w1 = jnp.dot(flat_inputs.T, flat_act, preferred_element_type=jnp.float32)
    summed = row_group_sum([grad_w1, grad_b1[None], grad_k, grad_bd[None], grad_w2])
    summed[1] = summed[1][0]
    summed[3] = summed[3][0]
    own_part = lax.psum_scatter(
        jnp.einsum("rwh,ch->rwc", grad_act, expand_w, preferred_element_type=jnp.float32),
        CHAN_AXES,
        scatter_dimension=0,
        tiled=True,
    )
    input_grad = (cotangent.astype(jnp.float32) + own_part).astype(jnp.bfloat16)
    return (input_grad, summed[0], summed[1], summed[2], summed[3], summed[4])


def solution(mesh):
    fine = Mesh(mesh.devices.reshape(2, 8, 4, 2, 2), ROW_AXES + CHAN_AXES)
    rows = ROW_AXES + CHAN_AXES
    in_specs = (
        P(rows, None, None),
        P(rows, None, None),
        P(None, CHAN_AXES),
        P(CHAN_AXES),
        P(None, CHAN_AXES),
        P(CHAN_AXES),
        P(CHAN_AXES, None),
    )
    out_specs = (
        P(rows, None, None),
        P(None, CHAN_AXES),
        P(CHAN_AXES),
        P(None, CHAN_AXES),
        P(CHAN_AXES),
        P(CHAN_AXES, None),
    )
    return jax.shard_map(shards, mesh=fine, in_specs=in_specs, out_specs=out_specs, check_vma=False)
```

```python
import jax
import jax.numpy as jnp
from jax import lax
from jax.experimental import pallas as pl
from jax.experimental.pallas import tpu as pltpu
from jax.sharding import Mesh, PartitionSpec as P

MESH_ID = pl.DeviceIdType.MESH
ALL_AXES = ("y_lo", "z", "x", "y_hi", "core")
ROW_AXES = ("y_lo", "z", "x")
CHAN_AXES = ("y_hi", "core")


def _sum_kernel(nx, nz, layout, terms, part, cot, term_outs, grad_out, data, out, xs, zs, ys, from_pair, from_far,
                relay, sems):
    (xsend, xrecv, zsend, zrecv, ysend, yrecv, gzsend, gzrecv, gxsend, gxrecv, csems) = sems
    coords = [lax.axis_index(a) for a in ALL_AXES]
    iy, iz, ix = coords[0], coords[1], coords[2]
    hi, core = coords[3], coords[4]
    me = hi * 2 + core
    pair_at = hi * 2 + (1 - core)
    far_at = (1 - hi) * 2 + core
    diag_at = (1 - hi) * 2 + (1 - core)
    pair = (iy, iz, ix, hi, 1 - core)
    far = (iy, iz, ix, 1 - hi, core)

    def dev(y=None, z=None, x=None):
        c = list(coords)
        if y is not None:
            c[0] = y
        if z is not None:
            c[1] = z
        if x is not None:
            c[2] = x
        return tuple(c)

    x_next = [dev(x=lax.rem(ix + 1, nx)), dev(x=lax.rem(ix + nx - 1, nx))]
    z_next = [dev(z=lax.rem(iz + 1, nz)), dev(z=lax.rem(iz + nz - 1, nz))]
    partner = dev(y=1 - iy)

    barrier = pltpu.get_barrier_semaphore()
    z_peer = [None] + [dev(z=lax.rem(iz + d, nz)) for d in range(1, nz)]
    peers = [x_next[0], x_next[1], partner, pair, far] + z_peer[1:]
    if nx == 2:
        peers = peers[1:]
    for d in peers:
        pl.semaphore_signal(barrier, inc=1, device_id=d, device_id_type=MESH_ID)
    pl.semaphore_wait(barrier, len(peers))

    filled = 0
    for ref, (at, size) in zip(terms, layout):
        data[at : at + size] = ref[...]
        filled = at + size
    data[filled:] = jnp.zeros((data.shape[0] - filled, data.shape[1]), data.dtype)

    chan_one = []
    for j, src in enumerate((part.at[pair_at], part.at[diag_at])):
        c = pltpu.make_async_remote_copy(
            src_ref=src, dst_ref=from_pair.at[j], send_sem=csems.at[0, j],
            recv_sem=csems.at[1, j], device_id=pair, device_id_type=MESH_ID)
        c.start()
        chan_one.append(c)

    rows = data.shape[0]
    half = rows // 2
    bx = half // nx
    bz = bx // nz
    steps = (1, -1)

    def xblock(h, k):
        return pl.ds(pl.multiple_of(h * half + lax.rem(k + 4 * nx, nx) * bx, 8), bx)

    def zblock(k):
        return pl.ds(pl.multiple_of(lax.rem(k + 4 * nz, nz) * bz, 8), bz)

    def oblock(h, kx, kz):
        at = h * half + lax.rem(kx + 4 * nx, nx) * bx + lax.rem(kz + 4 * nz, nz) * bz
        return pl.ds(pl.multiple_of(at, 8), bz)

    def obig(h, kx):
        return pl.ds(pl.multiple_of(h * half + lax.rem(kx + 4 * nx, nx) * bx, 8), bx)

    for s in range(nx - 1):
        copies = []
        for h in range(2):
            sg = steps[h]
            src = data.at[xblock(h, ix - sg)] if s == 0 else xs.at[h, s - 1]
            c = pltpu.make_async_remote_copy(
                src_ref=src, dst_ref=xs.at[h, s], send_sem=xsend.at[h * nx + s],
                recv_sem=xrecv.at[h * nx + s], device_id=x_next[h], device_id_type=MESH_ID)
            c.start()
            copies.append(c)
        for h in range(2):
            sg = steps[h]
            copies[h].wait_recv()
            xs[h, s] = xs[h, s] + data[xblock(h, ix - sg * (s + 2))]
            copies[h].wait_send()
    last = nx - 2
    for c in chan_one:
        c.wait_recv()
    relay[...] = part[far_at] + from_pair[1]
    chan_two = pltpu.make_async_remote_copy(
        src_ref=relay, dst_ref=from_far, send_sem=csems.at[0, 2],
        recv_sem=csems.at[1, 2], device_id=far, device_id_type=MESH_ID)
    chan_two.start()
    copies = []
    for h in range(2):
        for d in range(1, nz):
            c = pltpu.make_async_remote_copy(
                src_ref=xs.at[h, last, zblock(iz + d)], dst_ref=zs.at[h, d - 1],
                send_sem=zsend.at[h * nz + d], recv_sem=zrecv.at[h * nz + d],
                device_id=z_peer[d], device_id_type=MESH_ID)
            c.start()
            copies.append(c)
    for c in copies:
        c.wait_recv()
    for h in range(2):
        acc = xs[h, last, zblock(iz)]
        for d in range(1, nz):
            acc = acc + zs[h, d - 1]
        zs[h, nz - 1] = acc
    for c in copies:
        c.wait_send()
    zl = nz - 1
    c = pltpu.make_async_remote_copy(
        src_ref=zs.at[:, zl], dst_ref=ys, send_sem=ysend.at[0], recv_sem=yrecv.at[0],
        device_id=partner, device_id_type=MESH_ID)
    c.start()
    c.wait_recv()
    for h in range(2):
        out[oblock(h, ix, iz)] = zs[h, zl] + ys[h]
    c.wait_send()
    copies = []
    for h in range(2):
        loc = oblock(h, ix, iz)
        for d in range(1, nz):
            c = pltpu.make_async_remote_copy(
                src_ref=out.at[loc], dst_ref=out.at[loc], send_sem=gzsend.at[h * nz + d],
                recv_sem=gzrecv.at[h * nz + d], device_id=z_peer[d], device_id_type=MESH_ID)
            c.start()
            copies.append(c)
    for c in copies:
        c.wait_recv()
    for c in copies:
        c.wait_send()
    for s in range(nx - 1):
        copies = []
        for h in range(2):
            sg = steps[h]
            loc = obig(h, ix - sg * s)
            c = pltpu.make_async_remote_copy(
                src_ref=out.at[loc], dst_ref=out.at[loc], send_sem=gxsend.at[h * nx + s],
                recv_sem=gxrecv.at[h * nx + s], device_id=x_next[h], device_id_type=MESH_ID)
            c.start()
            copies.append(c)
        for h in range(2):
            copies[h].wait_recv()
            copies[h].wait_send()

    for ref, (at, size) in zip(term_outs, layout):
        ref[...] = out[at : at + size]
    chan_two.wait_recv()
    total = part[me] + from_pair[0] + from_far[...]
    grad_out[...] = (cot[...].astype(jnp.float32) + total).astype(grad_out.dtype)
    for c in chan_one:
        c.wait_send()
    chan_two.wait_send()

def row_group_allreduce(terms, nx, nz, part, cot):
    cols = terms[0].shape[-1]
    layout = []
    at = 0
    for t in terms:
        layout.append((at, t.shape[0]))
        at += t.shape[0]
    quantum = 2 * nx * nz * 8
    rows = -(-at // quantum) * quantum
    half = rows // 2
    bx = half // nx
    bz = bx // nz
    sems = [pltpu.SemaphoreType.DMA((2 * nx,)), pltpu.SemaphoreType.DMA((2 * nx,)),
            pltpu.SemaphoreType.DMA((2 * nz,)), pltpu.SemaphoreType.DMA((2 * nz,)),
            pltpu.SemaphoreType.DMA((1,)), pltpu.SemaphoreType.DMA((1,)),
            pltpu.SemaphoreType.DMA((2 * nz,)), pltpu.SemaphoreType.DMA((2 * nz,)),
            pltpu.SemaphoreType.DMA((2 * nx,)), pltpu.SemaphoreType.DMA((2 * nx,)),
            pltpu.SemaphoreType.DMA((2, 3))]
    block = part.shape[1:]
    count = len(terms)

    def body(*refs):
        ins, outs, scratch = refs[: count + 2], refs[count + 2 : 2 * count + 3], refs[2 * count + 3 :]
        _sum_kernel(nx, nz, layout, ins[:count], ins[count], ins[count + 1], outs[:count], outs[count],
                    *scratch[:8], scratch[8:])

    return pl.pallas_call(
        body,
        out_shape=tuple(jax.ShapeDtypeStruct(t.shape, jnp.float32) for t in terms)
        + (jax.ShapeDtypeStruct(cot.shape, cot.dtype),),
        in_specs=[pl.BlockSpec(memory_space=pltpu.VMEM)] * (count + 2),
        out_specs=(pl.BlockSpec(memory_space=pltpu.VMEM),) * (count + 1),
        scratch_shapes=[
            pltpu.VMEM((rows, cols), jnp.float32),
            pltpu.VMEM((rows, cols), jnp.float32),
            pltpu.VMEM((2, nx - 1, bx, cols), jnp.float32),
            pltpu.VMEM((2, nz, bz, cols), jnp.float32),
            pltpu.VMEM((2, bz, cols), jnp.float32),
            pltpu.VMEM((2,) + block, jnp.float32),
            pltpu.VMEM(block, jnp.float32),
            pltpu.VMEM(block, jnp.float32),
        ] + sems,
        compiler_params=pltpu.CompilerParams(collective_id=0, has_side_effects=True,
                                             vmem_limit_bytes=48 * 1024 * 1024),
    )(*terms, part, cot)


def _chan_gather_kernel(first, second, out_first, out_second, sems):
    coords = [lax.axis_index(a) for a in ALL_AXES]
    hi, core = coords[3], coords[4]

    def dev(h, c):
        return (coords[0], coords[1], coords[2], h, c)

    me = hi * 2 + core
    across = hi * 2 + (1 - core)
    over = (1 - hi) * 2 + core
    pair, far = dev(hi, 1 - core), dev(1 - hi, core)

    barrier = pltpu.get_barrier_semaphore()
    for d in (pair, far):
        pl.semaphore_signal(barrier, inc=1, device_id=d, device_id_type=MESH_ID)
    pl.semaphore_wait(barrier, 2)

    sources = (first, second)
    outs = (out_first, out_second)
    step_one = []
    for k in range(2):
        for j, target in enumerate((pair, far)):
            c = pltpu.make_async_remote_copy(
                src_ref=sources[k], dst_ref=outs[k].at[me], send_sem=sems.at[0, k, j],
                recv_sem=sems.at[1, k, j], device_id=target, device_id_type=MESH_ID)
            c.start()
            step_one.append(c)
    for k in range(2):
        outs[k][me] = sources[k][...]
    for c in step_one:
        c.wait_recv()
    relay = []
    for k in range(2):
        c = pltpu.make_async_remote_copy(
            src_ref=outs[k].at[over], dst_ref=outs[k].at[over], send_sem=sems.at[0, k, 2],
            recv_sem=sems.at[1, k, 2], device_id=pair, device_id_type=MESH_ID)
        c.start()
        relay.append(c)
    for c in relay:
        c.wait_recv()
    for c in step_one + relay:
        c.wait_send()


def chan_gather(first, second):
    shape = (4,) + first.shape
    result = pl.pallas_call(
        _chan_gather_kernel,
        out_shape=(jax.ShapeDtypeStruct(shape, first.dtype), jax.ShapeDtypeStruct(shape, second.dtype)),
        in_specs=[pl.BlockSpec(memory_space=pltpu.VMEM)] * 2,
        out_specs=(pl.BlockSpec(memory_space=pltpu.VMEM),) * 2,
        scratch_shapes=[pltpu.SemaphoreType.DMA((2, 2, 3))],
        compiler_params=pltpu.CompilerParams(collective_id=1, has_side_effects=True),
    )(first, second)
    return tuple(r.reshape((-1,) + first.shape[1:]) for r in result)


def extended(block, sides, width):
    for axis, dim in sides:
        count = 1
        for name in axis:
            count *= lax.axis_size(name)
        forward = [(i, i + 1) for i in range(count - 1)]
        backward = [(target, source) for source, target in forward]
        low = lax.ppermute(
            lax.slice_in_dim(block, block.shape[dim] - width, None, axis=dim), axis, forward
        )
        high = lax.ppermute(lax.slice_in_dim(block, 0, width, axis=dim), axis, backward)
        block = jnp.concatenate([low, block, high], axis=dim)
    return block


def gelu_parts(pre):
    cdf = 0.5 * (1.0 + lax.erf(pre * 0.7071067811865476))
    dens = jnp.exp(-0.5 * pre * pre) * 0.3989422804014327
    return (pre * cdf, cdf + pre * dens)


def shards(inputs, cotangent, expand_w, expand_b, depth_k, depth_b, project_w):
    rows_in, rows_cot = chan_gather(inputs, cotangent)
    nrows, ncols, cin = rows_in.shape
    hslice = expand_w.shape[1]
    flat_inputs = rows_in.reshape(nrows * ncols, cin)
    flat_cotan = rows_cot.reshape(nrows * ncols, cin)
    pre_one = (
        jnp.dot(flat_inputs, expand_w, preferred_element_type=jnp.float32).reshape(
            nrows, ncols, hslice
        )
        + expand_b
    )
    hidden, slope_one = gelu_parts(pre_one)
    hidden = hidden.astype(jnp.bfloat16)
    rimmed = extended(hidden, ((ROW_AXES, 0),), 2)
    padded = jnp.pad(rimmed, ((0, 0), (2, 2), (0, 0))).astype(jnp.float32)
    pre_two = jnp.zeros((nrows, ncols, hslice), jnp.float32) + depth_b
    for row_tap in range(5):
        for col_tap in range(5):
            pre_two = (
                pre_two
                + depth_k[5 * row_tap + col_tap]
                * padded[row_tap : row_tap + nrows, col_tap : col_tap + ncols]
            )
    mixed, slope_two = gelu_parts(pre_two)
    mixed = mixed.astype(jnp.bfloat16).reshape(nrows * ncols, hslice)
    grad_w2 = jnp.dot(mixed.T, flat_cotan, preferred_element_type=jnp.float32)
    grad_mixed = jnp.dot(flat_cotan, project_w.T, preferred_element_type=jnp.float32).reshape(
        nrows, ncols, hslice
    )
    grad_pre = (grad_mixed * slope_two).astype(jnp.bfloat16)
    grad_pre_f = grad_pre.astype(jnp.float32)
    grad_bd = jnp.sum(grad_pre_f, axis=(0, 1))
    grad_rimmed = extended(grad_pre, ((ROW_AXES, 0),), 2)
    grad_pad = jnp.pad(grad_rimmed, ((0, 0), (2, 2), (0, 0))).astype(jnp.float32)
    taps = []
    grad_hidden = jnp.zeros((nrows, ncols, hslice), jnp.float32)
    for row_tap in range(5):
        for col_tap in range(5):
            taps.append(
                jnp.sum(
                    padded[row_tap : row_tap + nrows, col_tap : col_tap + ncols] * grad_pre_f,
                    axis=(0, 1),
                )
            )
            grad_hidden = (
                grad_hidden
                + depth_k[5 * row_tap + col_tap]
                * grad_pad[4 - row_tap : 4 - row_tap + nrows, 4 - col_tap : 4 - col_tap + ncols]
            )
    grad_k = jnp.stack(taps, axis=0)
    grad_act = (grad_hidden * slope_one).astype(jnp.bfloat16)
    flat_act = grad_act.reshape(nrows * ncols, hslice)
    grad_b1 = jnp.sum(flat_act.astype(jnp.float32), axis=0)
    grad_w1 = jnp.dot(flat_inputs.T, flat_act, preferred_element_type=jnp.float32)
    part = jnp.einsum("rwh,ch->rwc", grad_act, expand_w, preferred_element_type=jnp.float32)
    part = part.reshape((4, -1) + part.shape[1:])
    nx, nz = lax.axis_size("x"), lax.axis_size("z")
    w1, w2, k, b1, bd, input_grad = row_group_allreduce(
        [grad_w1, grad_w2, grad_k, grad_b1[None], grad_bd[None]], nx, nz, part, cotangent
    )
    return (input_grad, w1, b1[0], k, bd[0], w2)


def solution(mesh):
    fine = Mesh(mesh.devices.reshape(2, 8, 4, 2, 2), ROW_AXES + CHAN_AXES)
    rows = ROW_AXES + CHAN_AXES
    in_specs = (
        P(rows, None, None),
        P(rows, None, None),
        P(None, CHAN_AXES),
        P(CHAN_AXES),
        P(None, CHAN_AXES),
        P(CHAN_AXES),
        P(CHAN_AXES, None),
    )
    out_specs = (
        P(rows, None, None),
        P(None, CHAN_AXES),
        P(CHAN_AXES),
        P(None, CHAN_AXES),
        P(CHAN_AXES),
        P(CHAN_AXES, None),
    )
    return jax.shard_map(shards, mesh=fine, in_specs=in_specs, out_specs=out_specs, check_vma=False)
```

```python
import jax
import jax.numpy as jnp
from jax import lax
from jax.experimental import pallas as pl
from jax.experimental.pallas import tpu as pltpu
from jax.sharding import Mesh, PartitionSpec as P

MESH_ID = pl.DeviceIdType.MESH
ALL_AXES = ("y_lo", "z", "x", "y_hi", "core")
ROW_AXES = ("y_lo", "z", "x")
CHAN_AXES = ("y_hi", "core")


def _sum_kernel(nx, nz, data, part, cot, out, grad_out, xs, zs, ys, fin, from_pair, from_far, relay, sems):
    (xsend, xrecv, zsend, zrecv, ysend, yrecv, gzsend, gzrecv, gxsend, gxrecv, csems, local) = sems
    coords = [lax.axis_index(a) for a in ALL_AXES]
    iy, iz, ix = coords[0], coords[1], coords[2]
    hi, core = coords[3], coords[4]
    me = hi * 2 + core
    pair_at = hi * 2 + (1 - core)
    far_at = (1 - hi) * 2 + core
    diag_at = (1 - hi) * 2 + (1 - core)
    pair = (iy, iz, ix, hi, 1 - core)
    far = (iy, iz, ix, 1 - hi, core)

    def dev(y=None, z=None, x=None):
        c = list(coords)
        if y is not None:
            c[0] = y
        if z is not None:
            c[1] = z
        if x is not None:
            c[2] = x
        return tuple(c)

    x_next = [dev(x=lax.rem(ix + 1, nx)), dev(x=lax.rem(ix + nx - 1, nx))]
    z_next = [dev(z=lax.rem(iz + 1, nz)), dev(z=lax.rem(iz + nz - 1, nz))]
    partner = dev(y=1 - iy)

    barrier = pltpu.get_barrier_semaphore()
    z_peer = [None] + [dev(z=lax.rem(iz + d, nz)) for d in range(1, nz)]
    peers = [x_next[0], x_next[1], partner, pair, far] + z_peer[1:]
    if nx == 2:
        peers = peers[1:]
    for d in peers:
        pl.semaphore_signal(barrier, inc=1, device_id=d, device_id_type=MESH_ID)
    pl.semaphore_wait(barrier, len(peers))

    chan_one = []
    for j, src in enumerate((part.at[pair_at], part.at[diag_at])):
        c = pltpu.make_async_remote_copy(
            src_ref=src, dst_ref=from_pair.at[j], send_sem=csems.at[0, j],
            recv_sem=csems.at[1, j], device_id=pair, device_id_type=MESH_ID)
        c.start()
        chan_one.append(c)

    rows, cols = data.shape
    half = cols // 2
    bx = rows // nx
    bz = bx // (nz // 2)
    lanes = half // 2
    steps = (1, -1)

    def xblock(h, k):
        return (pl.ds(pl.multiple_of(lax.rem(k + 4 * nx, nx) * bx, 8), bx), pl.ds(h * half, half))

    def zblock(k):
        k = lax.rem(k + 4 * nz, nz)
        return (pl.ds(pl.multiple_of((k // 2) * bz, 8), bz), pl.ds(pl.multiple_of(lax.rem(k, 2) * lanes, 128), lanes))

    def oblock(h, kx, kz):
        r, c = zblock(kz)
        start = pl.multiple_of(lax.rem(kx + 4 * nx, nx) * bx + r.start, 8)
        return (pl.ds(start, bz), pl.ds(pl.multiple_of(h * half + c.start, 128), lanes))

    def obig(h, kx):
        return xblock(h, kx)

    for s in range(nx - 1):
        copies = []
        for h in range(2):
            sg = steps[h]
            src = data.at[xblock(h, ix - sg)] if s == 0 else xs.at[h, s - 1]
            c = pltpu.make_async_remote_copy(
                src_ref=src, dst_ref=xs.at[h, s], send_sem=xsend.at[h * nx + s],
                recv_sem=xrecv.at[h * nx + s], device_id=x_next[h], device_id_type=MESH_ID)
            c.start()
            copies.append(c)
        for h in range(2):
            sg = steps[h]
            copies[h].wait_recv()
            r, c = xblock(h, ix - sg * (s + 2))
            xs[h, s] = xs[h, s] + data[r, c]
            copies[h].wait_send()
    last = nx - 2
    for c in chan_one:
        c.wait_recv()
    relay[...] = part[far_at] + from_pair[1]
    chan_two = pltpu.make_async_remote_copy(
        src_ref=relay, dst_ref=from_far, send_sem=csems.at[0, 2],
        recv_sem=csems.at[1, 2], device_id=far, device_id_type=MESH_ID)
    chan_two.start()
    copies = []
    for h in range(2):
        for d in range(1, nz):
            c = pltpu.make_async_remote_copy(
                src_ref=xs.at[(h, last) + zblock(iz + d)], dst_ref=zs.at[h, d - 1],
                send_sem=zsend.at[h * nz + d], recv_sem=zrecv.at[h * nz + d],
                device_id=z_peer[d], device_id_type=MESH_ID)
            c.start()
            copies.append(c)
    own = [pltpu.make_async_copy(xs.at[(h, last) + zblock(iz)], zs.at[h, nz - 1], local.at[h]) for h in range(2)]
    for c in own:
        c.start()
    for c in own:
        c.wait()
    for c in copies:
        c.wait_recv()
    for h in range(2):
        acc = zs[h, nz - 1]
        for d in range(1, nz):
            acc = acc + zs[h, d - 1]
        zs[h, nz] = acc
    for c in copies:
        c.wait_send()
    zl = nz
    c = pltpu.make_async_remote_copy(
        src_ref=zs.at[:, zl], dst_ref=ys, send_sem=ysend.at[0], recv_sem=yrecv.at[0],
        device_id=partner, device_id_type=MESH_ID)
    c.start()
    c.wait_recv()
    for h in range(2):
        fin[h] = zs[h, zl] + ys[h]
    placed = [pltpu.make_async_copy(fin.at[h], out.at[oblock(h, ix, iz)], local.at[2 + h]) for h in range(2)]
    for p in placed:
        p.start()
    for p in placed:
        p.wait()
    c.wait_send()
    copies = []
    for h in range(2):
        loc = oblock(h, ix, iz)
        for d in range(1, nz):
            c = pltpu.make_async_remote_copy(
                src_ref=out.at[loc], dst_ref=out.at[loc], send_sem=gzsend.at[h * nz + d],
                recv_sem=gzrecv.at[h * nz + d], device_id=z_peer[d], device_id_type=MESH_ID)
            c.start()
            copies.append(c)
    for c in copies:
        c.wait_recv()
    for c in copies:
        c.wait_send()
    for s in range(nx - 1):
        copies = []
        for h in range(2):
            sg = steps[h]
            loc = obig(h, ix - sg * s)
            c = pltpu.make_async_remote_copy(
                src_ref=out.at[loc], dst_ref=out.at[loc], send_sem=gxsend.at[h * nx + s],
                recv_sem=gxrecv.at[h * nx + s], device_id=x_next[h], device_id_type=MESH_ID)
            c.start()
            copies.append(c)
        for h in range(2):
            copies[h].wait_recv()
            copies[h].wait_send()

    chan_two.wait_recv()
    total = part[me] + from_pair[0] + from_far[...]
    grad_out[...] = (cot[...].astype(jnp.float32) + total).astype(grad_out.dtype)
    for c in chan_one:
        c.wait_send()
    chan_two.wait_send()

def row_group_allreduce(pieces, nx, nz, part, cot):
    cols = pieces[0].shape[-1]
    layout = []
    at = 0
    for piece in pieces:
        layout.append((at, piece.shape[0]))
        at += piece.shape[0]
    quantum = 8 * nx * (nz // 2)
    rows = -(-at // quantum) * quantum
    used = at
    count = len(pieces)
    half = cols // 2
    bx = rows // nx
    bz = bx // (nz // 2)
    sems = [pltpu.SemaphoreType.DMA((2 * nx,)), pltpu.SemaphoreType.DMA((2 * nx,)),
            pltpu.SemaphoreType.DMA((2 * nz,)), pltpu.SemaphoreType.DMA((2 * nz,)),
            pltpu.SemaphoreType.DMA((1,)), pltpu.SemaphoreType.DMA((1,)),
            pltpu.SemaphoreType.DMA((2 * nz,)), pltpu.SemaphoreType.DMA((2 * nz,)),
            pltpu.SemaphoreType.DMA((2 * nx,)), pltpu.SemaphoreType.DMA((2 * nx,)),
            pltpu.SemaphoreType.DMA((2, 3)), pltpu.SemaphoreType.DMA((4,)),
            pltpu.SemaphoreType.DMA((2 * count,))]
    block = part.shape[1:]

    def body(*refs):
        ins, outs = refs[:count], refs[count + 2 : 2 * count + 2]
        part, cot, grad_out = refs[count], refs[count + 1], refs[2 * count + 2]
        data, out, xs, zs, ys, fin, from_pair, from_far, relay = refs[2 * count + 3 : 2 * count + 12]
        s = refs[2 * count + 12 :]
        moves = s[-1]
        packs = [pltpu.make_async_copy(ref, data.at[pl.ds(at, size)], moves.at[i])
                 for i, (ref, (at, size)) in enumerate(zip(ins, layout))]
        for c in packs:
            c.start()
        data[used:] = jnp.zeros((rows - used, cols), jnp.float32)
        for c in packs:
            c.wait()
        _sum_kernel(nx, nz, data, part, cot, out, grad_out, xs, zs, ys, fin, from_pair, from_far, relay, s[:-1])
        unpacks = [pltpu.make_async_copy(out.at[pl.ds(at, size)], ref, moves.at[count + i])
                   for i, (ref, (at, size)) in enumerate(zip(outs, layout))]
        for c in unpacks:
            c.start()
        for c in unpacks:
            c.wait()

    return pl.pallas_call(
        body,
        out_shape=tuple(jax.ShapeDtypeStruct(p.shape, jnp.float32) for p in pieces)
        + (jax.ShapeDtypeStruct(cot.shape, cot.dtype),),
        in_specs=[pl.BlockSpec(memory_space=pltpu.VMEM)] * (count + 2),
        out_specs=(pl.BlockSpec(memory_space=pltpu.VMEM),) * (count + 1),
        scratch_shapes=[
            pltpu.VMEM((rows, cols), jnp.float32),
            pltpu.VMEM((rows, cols), jnp.float32),
            pltpu.VMEM((2, nx - 1, bx, half), jnp.float32),
            pltpu.VMEM((2, nz + 1, bz, half // 2), jnp.float32),
            pltpu.VMEM((2, bz, half // 2), jnp.float32),
            pltpu.VMEM((2, bz, half // 2), jnp.float32),
            pltpu.VMEM((2,) + block, jnp.float32),
            pltpu.VMEM(block, jnp.float32),
            pltpu.VMEM(block, jnp.float32),
        ] + sems,
        compiler_params=pltpu.CompilerParams(collective_id=0, has_side_effects=True,
                                             vmem_limit_bytes=48 * 1024 * 1024),
    )(*pieces, part, cot)


def _chan_gather_kernel(first, second, out_first, out_second, sems):
    coords = [lax.axis_index(a) for a in ALL_AXES]
    hi, core = coords[3], coords[4]

    def dev(h, c):
        return (coords[0], coords[1], coords[2], h, c)

    me = hi * 2 + core
    across = hi * 2 + (1 - core)
    over = (1 - hi) * 2 + core
    pair, far = dev(hi, 1 - core), dev(1 - hi, core)

    barrier = pltpu.get_barrier_semaphore()
    for d in (pair, far):
        pl.semaphore_signal(barrier, inc=1, device_id=d, device_id_type=MESH_ID)
    pl.semaphore_wait(barrier, 2)

    sources = (first, second)
    outs = (out_first, out_second)
    step_one = []
    for k in range(2):
        for j, target in enumerate((pair, far)):
            c = pltpu.make_async_remote_copy(
                src_ref=sources[k], dst_ref=outs[k].at[me], send_sem=sems.at[0, k, j],
                recv_sem=sems.at[1, k, j], device_id=target, device_id_type=MESH_ID)
            c.start()
            step_one.append(c)
    for k in range(2):
        outs[k][me] = sources[k][...]
    for c in step_one:
        c.wait_recv()
    relay = []
    for k in range(2):
        c = pltpu.make_async_remote_copy(
            src_ref=outs[k].at[over], dst_ref=outs[k].at[over], send_sem=sems.at[0, k, 2],
            recv_sem=sems.at[1, k, 2], device_id=pair, device_id_type=MESH_ID)
        c.start()
        relay.append(c)
    for c in relay:
        c.wait_recv()
    for c in step_one + relay:
        c.wait_send()


def chan_gather(first, second):
    shape = (4,) + first.shape
    result = pl.pallas_call(
        _chan_gather_kernel,
        out_shape=(jax.ShapeDtypeStruct(shape, first.dtype), jax.ShapeDtypeStruct(shape, second.dtype)),
        in_specs=[pl.BlockSpec(memory_space=pltpu.VMEM)] * 2,
        out_specs=(pl.BlockSpec(memory_space=pltpu.VMEM),) * 2,
        scratch_shapes=[pltpu.SemaphoreType.DMA((2, 2, 3))],
        compiler_params=pltpu.CompilerParams(collective_id=1, has_side_effects=True),
    )(first, second)
    return tuple(r.reshape((-1,) + first.shape[1:]) for r in result)


def extended(block, sides, width):
    for axis, dim in sides:
        count = 1
        for name in axis:
            count *= lax.axis_size(name)
        forward = [(i, i + 1) for i in range(count - 1)]
        backward = [(target, source) for source, target in forward]
        low = lax.ppermute(
            lax.slice_in_dim(block, block.shape[dim] - width, None, axis=dim), axis, forward
        )
        high = lax.ppermute(lax.slice_in_dim(block, 0, width, axis=dim), axis, backward)
        block = jnp.concatenate([low, block, high], axis=dim)
    return block


def gelu_parts(pre):
    cdf = 0.5 * (1.0 + lax.erf(pre * 0.7071067811865476))
    dens = jnp.exp(-0.5 * pre * pre) * 0.3989422804014327
    return (pre * cdf, cdf + pre * dens)


def shards(inputs, cotangent, expand_w, expand_b, depth_k, depth_b, project_w):
    rows_in, rows_cot = chan_gather(inputs, cotangent)
    nrows, ncols, cin = rows_in.shape
    hslice = expand_w.shape[1]
    flat_inputs = rows_in.reshape(nrows * ncols, cin)
    flat_cotan = rows_cot.reshape(nrows * ncols, cin)
    pre_one = (
        jnp.dot(flat_inputs, expand_w, preferred_element_type=jnp.float32).reshape(
            nrows, ncols, hslice
        )
        + expand_b
    )
    hidden, slope_one = gelu_parts(pre_one)
    hidden = hidden.astype(jnp.bfloat16)
    rimmed = extended(hidden, ((ROW_AXES, 0),), 2)
    padded = jnp.pad(rimmed, ((0, 0), (2, 2), (0, 0))).astype(jnp.float32)
    pre_two = jnp.zeros((nrows, ncols, hslice), jnp.float32) + depth_b
    for row_tap in range(5):
        for col_tap in range(5):
            pre_two = (
                pre_two
                + depth_k[5 * row_tap + col_tap]
                * padded[row_tap : row_tap + nrows, col_tap : col_tap + ncols]
            )
    mixed, slope_two = gelu_parts(pre_two)
    mixed = mixed.astype(jnp.bfloat16).reshape(nrows * ncols, hslice)
    grad_w2 = jnp.dot(mixed.T, flat_cotan, preferred_element_type=jnp.float32)
    grad_mixed = jnp.dot(flat_cotan, project_w.T, preferred_element_type=jnp.float32).reshape(
        nrows, ncols, hslice
    )
    grad_pre = (grad_mixed * slope_two).astype(jnp.bfloat16)
    grad_pre_f = grad_pre.astype(jnp.float32)
    grad_bd = jnp.sum(grad_pre_f, axis=(0, 1))
    grad_rimmed = extended(grad_pre, ((ROW_AXES, 0),), 2)
    grad_pad = jnp.pad(grad_rimmed, ((0, 0), (2, 2), (0, 0))).astype(jnp.float32)
    taps = []
    grad_hidden = jnp.zeros((nrows, ncols, hslice), jnp.float32)
    for row_tap in range(5):
        for col_tap in range(5):
            taps.append(
                jnp.sum(
                    padded[row_tap : row_tap + nrows, col_tap : col_tap + ncols] * grad_pre_f,
                    axis=(0, 1),
                )
            )
            grad_hidden = (
                grad_hidden
                + depth_k[5 * row_tap + col_tap]
                * grad_pad[4 - row_tap : 4 - row_tap + nrows, 4 - col_tap : 4 - col_tap + ncols]
            )
    grad_k = jnp.stack(taps, axis=0)
    grad_act = (grad_hidden * slope_one).astype(jnp.bfloat16)
    flat_act = grad_act.reshape(nrows * ncols, hslice)
    grad_b1 = jnp.sum(flat_act.astype(jnp.float32), axis=0)
    grad_w1 = jnp.dot(flat_inputs.T, flat_act, preferred_element_type=jnp.float32)
    part = jnp.einsum("rwh,ch->rwc", grad_act, expand_w, preferred_element_type=jnp.float32)
    part = part.reshape((4, -1) + part.shape[1:])
    small = jnp.concatenate([grad_k, grad_b1[None], grad_bd[None]], axis=0)
    taps_count = grad_k.shape[0]
    small = jnp.pad(small, ((0, -small.shape[0] % 8), (0, 0)))
    nx, nz = lax.axis_size("x"), lax.axis_size("z")
    w1, w2, small, input_grad = row_group_allreduce([grad_w1, grad_w2, small], nx, nz, part, cotangent)
    summed = [w1, small[taps_count], small[:taps_count], small[taps_count + 1], w2]
    return (input_grad, summed[0], summed[1], summed[2], summed[3], summed[4])


def solution(mesh):
    fine = Mesh(mesh.devices.reshape(2, 8, 4, 2, 2), ROW_AXES + CHAN_AXES)
    rows = ROW_AXES + CHAN_AXES
    in_specs = (
        P(rows, None, None),
        P(rows, None, None),
        P(None, CHAN_AXES),
        P(CHAN_AXES),
        P(None, CHAN_AXES),
        P(CHAN_AXES),
        P(CHAN_AXES, None),
    )
    out_specs = (
        P(rows, None, None),
        P(None, CHAN_AXES),
        P(CHAN_AXES),
        P(None, CHAN_AXES),
        P(CHAN_AXES),
        P(CHAN_AXES, None),
    )
    return jax.shard_map(shards, mesh=fine, in_specs=in_specs, out_specs=out_specs, check_vma=False)
```

```python
import jax
import jax.numpy as jnp
from jax import lax
from jax.experimental import pallas as pl
from jax.experimental.pallas import tpu as pltpu
from jax.sharding import Mesh, PartitionSpec as P

MESH_ID = pl.DeviceIdType.MESH
ALL_AXES = ("y_lo", "z", "x", "y_hi", "core")
ROW_AXES = ("y_lo", "z", "x")
CHAN_AXES = ("y_hi", "core")


def _sum_kernel(nx, nz, data, part, cot, out, grad_out, xs, zs, ys, fin, from_pair, from_far, relay, sems):
    (xsend, xrecv, zsend, zrecv, ysend, yrecv, gzsend, gzrecv, gxsend, gxrecv, csems, local) = sems
    coords = [lax.axis_index(a) for a in ALL_AXES]
    iy, iz, ix = coords[0], coords[1], coords[2]
    hi, core = coords[3], coords[4]
    me = hi * 2 + core
    pair_at = hi * 2 + (1 - core)
    far_at = (1 - hi) * 2 + core
    diag_at = (1 - hi) * 2 + (1 - core)
    pair = (iy, iz, ix, hi, 1 - core)
    far = (iy, iz, ix, 1 - hi, core)

    def dev(y=None, z=None, x=None):
        c = list(coords)
        if y is not None:
            c[0] = y
        if z is not None:
            c[1] = z
        if x is not None:
            c[2] = x
        return tuple(c)

    x_next = [dev(x=lax.rem(ix + 1, nx)), dev(x=lax.rem(ix + nx - 1, nx))]
    z_next = [dev(z=lax.rem(iz + 1, nz)), dev(z=lax.rem(iz + nz - 1, nz))]
    partner = dev(y=1 - iy)

    barrier = pltpu.get_barrier_semaphore()
    z_peer = [None] + [dev(z=lax.rem(iz + d, nz)) for d in range(1, nz)]
    peers = [x_next[0], x_next[1], partner, pair, far] + z_peer[1:]
    if nx == 2:
        peers = peers[1:]
    for d in peers:
        pl.semaphore_signal(barrier, inc=1, device_id=d, device_id_type=MESH_ID)
    pl.semaphore_wait(barrier, len(peers))

    chan_one = []
    for j, src in enumerate((part.at[pair_at], part.at[diag_at])):
        c = pltpu.make_async_remote_copy(
            src_ref=src, dst_ref=from_pair.at[j], send_sem=csems.at[0, j],
            recv_sem=csems.at[1, j], device_id=pair, device_id_type=MESH_ID)
        c.start()
        chan_one.append(c)

    rows, cols = data.shape
    half = cols // 2
    bx = rows // nx
    bz = bx // (nz // 2)
    lanes = half // 2
    steps = (1, -1)

    def xblock(h, k):
        return (pl.ds(pl.multiple_of(lax.rem(k + 4 * nx, nx) * bx, 8), bx), pl.ds(h * half, half))

    def zblock(k):
        k = lax.rem(k + 4 * nz, nz)
        return (pl.ds(pl.multiple_of((k // 2) * bz, 8), bz), pl.ds(pl.multiple_of(lax.rem(k, 2) * lanes, 128), lanes))

    def oblock(h, kx, kz):
        r, c = zblock(kz)
        start = pl.multiple_of(lax.rem(kx + 4 * nx, nx) * bx + r.start, 8)
        return (pl.ds(start, bz), pl.ds(pl.multiple_of(h * half + c.start, 128), lanes))

    def obig(h, kx):
        return xblock(h, kx)

    for s in range(nx - 1):
        copies = []
        for h in range(2):
            sg = steps[h]
            src = data.at[xblock(h, ix - sg)] if s == 0 else xs.at[h, s - 1]
            c = pltpu.make_async_remote_copy(
                src_ref=src, dst_ref=xs.at[h, s], send_sem=xsend.at[h * nx + s],
                recv_sem=xrecv.at[h * nx + s], device_id=x_next[h], device_id_type=MESH_ID)
            c.start()
            copies.append(c)
        for h in range(2):
            sg = steps[h]
            copies[h].wait_recv()
            r, c = xblock(h, ix - sg * (s + 2))
            xs[h, s] = xs[h, s] + data[r, c]
            copies[h].wait_send()
    last = nx - 2
    for c in chan_one:
        c.wait_recv()
    relay[...] = part[far_at] + from_pair[1]
    chan_two = pltpu.make_async_remote_copy(
        src_ref=relay, dst_ref=from_far, send_sem=csems.at[0, 2],
        recv_sem=csems.at[1, 2], device_id=far, device_id_type=MESH_ID)
    chan_two.start()
    copies = []
    for h in range(2):
        for d in range(1, nz):
            c = pltpu.make_async_remote_copy(
                src_ref=xs.at[(h, last) + zblock(iz + d)], dst_ref=zs.at[h, d - 1],
                send_sem=zsend.at[h * nz + d], recv_sem=zrecv.at[h * nz + d],
                device_id=z_peer[d], device_id_type=MESH_ID)
            c.start()
            copies.append(c)
    own = [pltpu.make_async_copy(xs.at[(h, last) + zblock(iz)], zs.at[h, nz - 1], local.at[h]) for h in range(2)]
    for c in own:
        c.start()
    for c in own:
        c.wait()
    for c in copies:
        c.wait_recv()
    for h in range(2):
        acc = zs[h, nz - 1]
        for d in range(1, nz):
            acc = acc + zs[h, d - 1]
        zs[h, nz] = acc
    for c in copies:
        c.wait_send()
    zl = nz
    c = pltpu.make_async_remote_copy(
        src_ref=zs.at[:, zl], dst_ref=ys, send_sem=ysend.at[0], recv_sem=yrecv.at[0],
        device_id=partner, device_id_type=MESH_ID)
    c.start()
    c.wait_recv()
    for h in range(2):
        fin[h] = zs[h, zl] + ys[h]
    placed = [pltpu.make_async_copy(fin.at[h], out.at[oblock(h, ix, iz)], local.at[2 + h]) for h in range(2)]
    for p in placed:
        p.start()
    for p in placed:
        p.wait()
    c.wait_send()
    copies = []
    for h in range(2):
        loc = oblock(h, ix, iz)
        for d in range(1, nz):
            c = pltpu.make_async_remote_copy(
                src_ref=out.at[loc], dst_ref=out.at[loc], send_sem=gzsend.at[h * nz + d],
                recv_sem=gzrecv.at[h * nz + d], device_id=z_peer[d], device_id_type=MESH_ID)
            c.start()
            copies.append(c)
    for c in copies:
        c.wait_recv()
    for c in copies:
        c.wait_send()
    for s in range(nx - 1):
        copies = []
        for h in range(2):
            sg = steps[h]
            loc = obig(h, ix - sg * s)
            c = pltpu.make_async_remote_copy(
                src_ref=out.at[loc], dst_ref=out.at[loc], send_sem=gxsend.at[h * nx + s],
                recv_sem=gxrecv.at[h * nx + s], device_id=x_next[h], device_id_type=MESH_ID)
            c.start()
            copies.append(c)
        for h in range(2):
            copies[h].wait_recv()
            copies[h].wait_send()

    chan_two.wait_recv()
    total = part[me] + from_pair[0] + from_far[...]
    grad_out[...] = (cot[...].astype(jnp.float32) + total).astype(grad_out.dtype)
    for c in chan_one:
        c.wait_send()
    chan_two.wait_send()

def row_group_allreduce(pieces, nx, nz, part, cot):
    cols = pieces[0].shape[-1]
    layout = []
    at = 0
    for piece in pieces:
        layout.append((at, piece.shape[0]))
        at += piece.shape[0]
    quantum = 8 * nx * (nz // 2)
    rows = -(-at // quantum) * quantum
    used = at
    count = len(pieces)
    half = cols // 2
    bx = rows // nx
    bz = bx // (nz // 2)
    sems = [pltpu.SemaphoreType.DMA((2 * nx,)), pltpu.SemaphoreType.DMA((2 * nx,)),
            pltpu.SemaphoreType.DMA((2 * nz,)), pltpu.SemaphoreType.DMA((2 * nz,)),
            pltpu.SemaphoreType.DMA((1,)), pltpu.SemaphoreType.DMA((1,)),
            pltpu.SemaphoreType.DMA((2 * nz,)), pltpu.SemaphoreType.DMA((2 * nz,)),
            pltpu.SemaphoreType.DMA((2 * nx,)), pltpu.SemaphoreType.DMA((2 * nx,)),
            pltpu.SemaphoreType.DMA((2, 3)), pltpu.SemaphoreType.DMA((4,)),
            pltpu.SemaphoreType.DMA((2 * count,))]
    block = part.shape[1:]

    def body(*refs):
        ins, outs = refs[:count], refs[count + 2 : 2 * count + 2]
        part, cot, grad_out = refs[count], refs[count + 1], refs[2 * count + 2]
        data, out, xs, zs, ys, fin, from_pair, from_far, relay = refs[2 * count + 3 : 2 * count + 12]
        s = refs[2 * count + 12 :]
        moves = s[-1]
        packs = [pltpu.make_async_copy(ref, data.at[pl.ds(at, size)], moves.at[i])
                 for i, (ref, (at, size)) in enumerate(zip(ins, layout))]
        for c in packs:
            c.start()
        data[used:] = jnp.zeros((rows - used, cols), jnp.float32)
        for c in packs:
            c.wait()
        _sum_kernel(nx, nz, data, part, cot, out, grad_out, xs, zs, ys, fin, from_pair, from_far, relay, s[:-1])
        unpacks = [pltpu.make_async_copy(out.at[pl.ds(at, size)], ref, moves.at[count + i])
                   for i, (ref, (at, size)) in enumerate(zip(outs, layout))]
        for c in unpacks:
            c.start()
        for c in unpacks:
            c.wait()

    return pl.pallas_call(
        body,
        out_shape=tuple(jax.ShapeDtypeStruct(p.shape, jnp.float32) for p in pieces)
        + (jax.ShapeDtypeStruct(cot.shape, cot.dtype),),
        in_specs=[pl.BlockSpec(memory_space=pltpu.VMEM)] * (count + 2),
        out_specs=(pl.BlockSpec(memory_space=pltpu.VMEM),) * (count + 1),
        scratch_shapes=[
            pltpu.VMEM((rows, cols), jnp.float32),
            pltpu.VMEM((rows, cols), jnp.float32),
            pltpu.VMEM((2, nx - 1, bx, half), jnp.float32),
            pltpu.VMEM((2, nz + 1, bz, half // 2), jnp.float32),
            pltpu.VMEM((2, bz, half // 2), jnp.float32),
            pltpu.VMEM((2, bz, half // 2), jnp.float32),
            pltpu.VMEM((2,) + block, jnp.float32),
            pltpu.VMEM(block, jnp.float32),
            pltpu.VMEM(block, jnp.float32),
        ] + sems,
        compiler_params=pltpu.CompilerParams(collective_id=0, has_side_effects=True,
                                             vmem_limit_bytes=48 * 1024 * 1024),
    )(*pieces, part, cot)


def _chan_gather_kernel(first, second, out_first, out_second, sems):
    coords = [lax.axis_index(a) for a in ALL_AXES]
    hi, core = coords[3], coords[4]

    def dev(h, c):
        return (coords[0], coords[1], coords[2], h, c)

    me = hi * 2 + core
    targets = (dev(hi, 1 - core), dev(1 - hi, core), dev(1 - hi, 1 - core))

    barrier = pltpu.get_barrier_semaphore()
    for d in targets:
        pl.semaphore_signal(barrier, inc=1, device_id=d, device_id_type=MESH_ID)
    pl.semaphore_wait(barrier, len(targets))

    sources = (first, second)
    outs = (out_first, out_second)
    copies = []
    for k in range(2):
        for j, target in enumerate(targets):
            c = pltpu.make_async_remote_copy(
                src_ref=sources[k], dst_ref=outs[k].at[me], send_sem=sems.at[0, k, j],
                recv_sem=sems.at[1, k, j], device_id=target, device_id_type=MESH_ID)
            c.start()
            copies.append(c)
    for k in range(2):
        outs[k][me] = sources[k][...]
    for c in copies:
        c.wait_recv()
    for c in copies:
        c.wait_send()


def chan_gather(first, second):
    shape = (4,) + first.shape
    result = pl.pallas_call(
        _chan_gather_kernel,
        out_shape=(jax.ShapeDtypeStruct(shape, first.dtype), jax.ShapeDtypeStruct(shape, second.dtype)),
        in_specs=[pl.BlockSpec(memory_space=pltpu.VMEM)] * 2,
        out_specs=(pl.BlockSpec(memory_space=pltpu.VMEM),) * 2,
        scratch_shapes=[pltpu.SemaphoreType.DMA((2, 2, 3))],
        compiler_params=pltpu.CompilerParams(collective_id=1, has_side_effects=True),
    )(first, second)
    return tuple(r.reshape((-1,) + first.shape[1:]) for r in result)


def extended(block, sides, width):
    for axis, dim in sides:
        count = 1
        for name in axis:
            count *= lax.axis_size(name)
        forward = [(i, i + 1) for i in range(count - 1)]
        backward = [(target, source) for source, target in forward]
        low = lax.ppermute(
            lax.slice_in_dim(block, block.shape[dim] - width, None, axis=dim), axis, forward
        )
        high = lax.ppermute(lax.slice_in_dim(block, 0, width, axis=dim), axis, backward)
        block = jnp.concatenate([low, block, high], axis=dim)
    return block


def gelu_parts(pre):
    cdf = 0.5 * (1.0 + lax.erf(pre * 0.7071067811865476))
    dens = jnp.exp(-0.5 * pre * pre) * 0.3989422804014327
    return (pre * cdf, cdf + pre * dens)


def shards(inputs, cotangent, expand_w, expand_b, depth_k, depth_b, project_w):
    rows_in, rows_cot = chan_gather(inputs, cotangent)
    nrows, ncols, cin = rows_in.shape
    hslice = expand_w.shape[1]
    flat_inputs = rows_in.reshape(nrows * ncols, cin)
    flat_cotan = rows_cot.reshape(nrows * ncols, cin)
    pre_one = (
        jnp.dot(flat_inputs, expand_w, preferred_element_type=jnp.float32).reshape(
            nrows, ncols, hslice
        )
        + expand_b
    )
    hidden, slope_one = gelu_parts(pre_one)
    hidden = hidden.astype(jnp.bfloat16)
    rimmed = extended(hidden, ((ROW_AXES, 0),), 2)
    padded = jnp.pad(rimmed, ((0, 0), (2, 2), (0, 0))).astype(jnp.float32)
    pre_two = jnp.zeros((nrows, ncols, hslice), jnp.float32) + depth_b
    for row_tap in range(5):
        for col_tap in range(5):
            pre_two = (
                pre_two
                + depth_k[5 * row_tap + col_tap]
                * padded[row_tap : row_tap + nrows, col_tap : col_tap + ncols]
            )
    mixed, slope_two = gelu_parts(pre_two)
    mixed = mixed.astype(jnp.bfloat16).reshape(nrows * ncols, hslice)
    grad_w2 = jnp.dot(mixed.T, flat_cotan, preferred_element_type=jnp.float32)
    grad_mixed = jnp.dot(flat_cotan, project_w.T, preferred_element_type=jnp.float32).reshape(
        nrows, ncols, hslice
    )
    grad_pre = (grad_mixed * slope_two).astype(jnp.bfloat16)
    grad_pre_f = grad_pre.astype(jnp.float32)
    grad_bd = jnp.sum(grad_pre_f, axis=(0, 1))
    grad_rimmed = extended(grad_pre, ((ROW_AXES, 0),), 2)
    grad_pad = jnp.pad(grad_rimmed, ((0, 0), (2, 2), (0, 0))).astype(jnp.float32)
    taps = []
    grad_hidden = jnp.zeros((nrows, ncols, hslice), jnp.float32)
    for row_tap in range(5):
        for col_tap in range(5):
            taps.append(
                jnp.sum(
                    padded[row_tap : row_tap + nrows, col_tap : col_tap + ncols] * grad_pre_f,
                    axis=(0, 1),
                )
            )
            grad_hidden = (
                grad_hidden
                + depth_k[5 * row_tap + col_tap]
                * grad_pad[4 - row_tap : 4 - row_tap + nrows, 4 - col_tap : 4 - col_tap + ncols]
            )
    grad_k = jnp.stack(taps, axis=0)
    grad_act = (grad_hidden * slope_one).astype(jnp.bfloat16)
    flat_act = grad_act.reshape(nrows * ncols, hslice)
    grad_b1 = jnp.sum(flat_act.astype(jnp.float32), axis=0)
    grad_w1 = jnp.dot(flat_inputs.T, flat_act, preferred_element_type=jnp.float32)
    part = jnp.einsum("rwh,ch->rwc", grad_act, expand_w, preferred_element_type=jnp.float32)
    part = part.reshape((4, -1) + part.shape[1:])
    small = jnp.concatenate([grad_k, grad_b1[None], grad_bd[None]], axis=0)
    taps_count = grad_k.shape[0]
    small = jnp.pad(small, ((0, -small.shape[0] % 8), (0, 0)))
    nx, nz = lax.axis_size("x"), lax.axis_size("z")
    w1, w2, small, input_grad = row_group_allreduce([grad_w1, grad_w2, small], nx, nz, part, cotangent)
    summed = [w1, small[taps_count], small[:taps_count], small[taps_count + 1], w2]
    return (input_grad, summed[0], summed[1], summed[2], summed[3], summed[4])


def solution(mesh):
    fine = Mesh(mesh.devices.reshape(2, 8, 4, 2, 2), ROW_AXES + CHAN_AXES)
    rows = ROW_AXES + CHAN_AXES
    in_specs = (
        P(rows, None, None),
        P(rows, None, None),
        P(None, CHAN_AXES),
        P(CHAN_AXES),
        P(None, CHAN_AXES),
        P(CHAN_AXES),
        P(CHAN_AXES, None),
    )
    out_specs = (
        P(rows, None, None),
        P(None, CHAN_AXES),
        P(CHAN_AXES),
        P(None, CHAN_AXES),
        P(CHAN_AXES),
        P(CHAN_AXES, None),
    )
    return jax.shard_map(shards, mesh=fine, in_specs=in_specs, out_specs=out_specs, check_vma=False)
```

```python
import jax
import jax.numpy as jnp
from jax import lax
from jax.experimental import pallas as pl
from jax.experimental.pallas import tpu as pltpu
from jax.sharding import Mesh, PartitionSpec as P

MESH_ID = pl.DeviceIdType.MESH
ALL_AXES = ("y_lo", "z", "x", "y_hi", "core")
ROW_AXES = ("y_lo", "z", "x")
CHAN_AXES = ("y_hi", "core")


def _sum_kernel(nx, nz, data, part, cot, out, grad_out, xs, zs, ys, fin, from_pair, from_far, relay, sems):
    (xsend, xrecv, zsend, zrecv, ysend, yrecv, gzsend, gzrecv, gxsend, gxrecv, csems, local) = sems
    coords = [lax.axis_index(a) for a in ALL_AXES]
    iy, iz, ix = coords[0], coords[1], coords[2]
    hi, core = coords[3], coords[4]
    me = hi * 2 + core
    pair_at = hi * 2 + (1 - core)
    far_at = (1 - hi) * 2 + core
    diag_at = (1 - hi) * 2 + (1 - core)
    pair = (iy, iz, ix, hi, 1 - core)
    far = (iy, iz, ix, 1 - hi, core)

    def dev(y=None, z=None, x=None):
        c = list(coords)
        if y is not None:
            c[0] = y
        if z is not None:
            c[1] = z
        if x is not None:
            c[2] = x
        return tuple(c)

    x_next = [dev(x=lax.rem(ix + 1, nx)), dev(x=lax.rem(ix + nx - 1, nx))]
    z_next = [dev(z=lax.rem(iz + 1, nz)), dev(z=lax.rem(iz + nz - 1, nz))]
    partner = dev(y=1 - iy)

    barrier = pltpu.get_barrier_semaphore()
    z_peer = [None] + [dev(z=lax.rem(iz + d, nz)) for d in range(1, nz)]
    peers = [x_next[0], x_next[1], partner, pair, far] + z_peer[1:]
    if nx == 2:
        peers = peers[1:]
    for d in peers:
        pl.semaphore_signal(barrier, inc=1, device_id=d, device_id_type=MESH_ID)
    pl.semaphore_wait(barrier, len(peers))

    chan_one = []
    for j, src in enumerate((part.at[pair_at], part.at[diag_at])):
        c = pltpu.make_async_remote_copy(
            src_ref=src, dst_ref=from_pair.at[j], send_sem=csems.at[0, j],
            recv_sem=csems.at[1, j], device_id=pair, device_id_type=MESH_ID)
        c.start()
        chan_one.append(c)

    rows, cols = data.shape
    half = cols // 2
    bx = rows // nx
    bz = bx // (nz // 2)
    lanes = half // 2
    steps = (1, -1)

    def xblock(h, k):
        return (pl.ds(pl.multiple_of(lax.rem(k + 4 * nx, nx) * bx, 8), bx), pl.ds(h * half, half))

    def zblock(k):
        k = lax.rem(k + 4 * nz, nz)
        return (pl.ds(pl.multiple_of((k // 2) * bz, 8), bz), pl.ds(pl.multiple_of(lax.rem(k, 2) * lanes, 128), lanes))

    def oblock(h, kx, kz):
        r, c = zblock(kz)
        start = pl.multiple_of(lax.rem(kx + 4 * nx, nx) * bx + r.start, 8)
        return (pl.ds(start, bz), pl.ds(pl.multiple_of(h * half + c.start, 128), lanes))

    def obig(h, kx):
        return xblock(h, kx)

    for s in range(nx - 1):
        copies = []
        for h in range(2):
            sg = steps[h]
            src = data.at[xblock(h, ix - sg)] if s == 0 else xs.at[h, s - 1]
            c = pltpu.make_async_remote_copy(
                src_ref=src, dst_ref=xs.at[h, s], send_sem=xsend.at[h * nx + s],
                recv_sem=xrecv.at[h * nx + s], device_id=x_next[h], device_id_type=MESH_ID)
            c.start()
            copies.append(c)
        for h in range(2):
            sg = steps[h]
            copies[h].wait_recv()
            r, c = xblock(h, ix - sg * (s + 2))
            xs[h, s] = xs[h, s] + data[r, c]
            copies[h].wait_send()
    last = nx - 2
    for c in chan_one:
        c.wait_recv()
    relay[...] = part[far_at] + from_pair[1]
    chan_two = pltpu.make_async_remote_copy(
        src_ref=relay, dst_ref=from_far, send_sem=csems.at[0, 2],
        recv_sem=csems.at[1, 2], device_id=far, device_id_type=MESH_ID)
    chan_two.start()
    copies = []
    for h in range(2):
        for d in range(1, nz):
            c = pltpu.make_async_remote_copy(
                src_ref=xs.at[(h, last) + zblock(iz + d)], dst_ref=zs.at[h, d - 1],
                send_sem=zsend.at[h * nz + d], recv_sem=zrecv.at[h * nz + d],
                device_id=z_peer[d], device_id_type=MESH_ID)
            c.start()
            copies.append(c)
    own = [pltpu.make_async_copy(xs.at[(h, last) + zblock(iz)], zs.at[h, nz - 1], local.at[h]) for h in range(2)]
    for c in own:
        c.start()
    for c in own:
        c.wait()
    for c in copies:
        c.wait_recv()
    for h in range(2):
        acc = zs[h, nz - 1]
        for d in range(1, nz):
            acc = acc + zs[h, d - 1]
        zs[h, nz] = acc
    for c in copies:
        c.wait_send()
    zl = nz
    c = pltpu.make_async_remote_copy(
        src_ref=zs.at[:, zl], dst_ref=ys, send_sem=ysend.at[0], recv_sem=yrecv.at[0],
        device_id=partner, device_id_type=MESH_ID)
    c.start()
    c.wait_recv()
    for h in range(2):
        fin[h] = zs[h, zl] + ys[h]
    placed = [pltpu.make_async_copy(fin.at[h], out.at[oblock(h, ix, iz)], local.at[2 + h]) for h in range(2)]
    for p in placed:
        p.start()
    for p in placed:
        p.wait()
    c.wait_send()
    copies = []
    for h in range(2):
        loc = oblock(h, ix, iz)
        for d in range(1, nz):
            c = pltpu.make_async_remote_copy(
                src_ref=out.at[loc], dst_ref=out.at[loc], send_sem=gzsend.at[h * nz + d],
                recv_sem=gzrecv.at[h * nz + d], device_id=z_peer[d], device_id_type=MESH_ID)
            c.start()
            copies.append(c)
    for c in copies:
        c.wait_recv()
    for c in copies:
        c.wait_send()
    for s in range(nx - 1):
        copies = []
        for h in range(2):
            sg = steps[h]
            loc = obig(h, ix - sg * s)
            c = pltpu.make_async_remote_copy(
                src_ref=out.at[loc], dst_ref=out.at[loc], send_sem=gxsend.at[h * nx + s],
                recv_sem=gxrecv.at[h * nx + s], device_id=x_next[h], device_id_type=MESH_ID)
            c.start()
            copies.append(c)
        for h in range(2):
            copies[h].wait_recv()
            copies[h].wait_send()

    chan_two.wait_recv()
    total = part[me] + from_pair[0] + from_far[...]
    grad_out[...] = (cot[...].astype(jnp.float32) + total).astype(grad_out.dtype)
    for c in chan_one:
        c.wait_send()
    chan_two.wait_send()

def row_group_allreduce(pieces, nx, nz, part, cot):
    cols = pieces[0].shape[-1]
    layout = []
    at = 0
    for piece in pieces:
        layout.append((at, piece.shape[0]))
        at += piece.shape[0]
    quantum = 8 * nx * (nz // 2)
    rows = -(-at // quantum) * quantum
    used = at
    count = len(pieces)
    half = cols // 2
    bx = rows // nx
    bz = bx // (nz // 2)
    sems = [pltpu.SemaphoreType.DMA((2 * nx,)), pltpu.SemaphoreType.DMA((2 * nx,)),
            pltpu.SemaphoreType.DMA((2 * nz,)), pltpu.SemaphoreType.DMA((2 * nz,)),
            pltpu.SemaphoreType.DMA((1,)), pltpu.SemaphoreType.DMA((1,)),
            pltpu.SemaphoreType.DMA((2 * nz,)), pltpu.SemaphoreType.DMA((2 * nz,)),
            pltpu.SemaphoreType.DMA((2 * nx,)), pltpu.SemaphoreType.DMA((2 * nx,)),
            pltpu.SemaphoreType.DMA((2, 3)), pltpu.SemaphoreType.DMA((4,)),
            pltpu.SemaphoreType.DMA((2 * count,))]
    block = part.shape[1:]

    def body(*refs):
        ins, outs = refs[:count], refs[count + 2 : 2 * count + 2]
        part, cot, grad_out = refs[count], refs[count + 1], refs[2 * count + 2]
        data, out, xs, zs, ys, fin, from_pair, from_far, relay = refs[2 * count + 3 : 2 * count + 12]
        s = refs[2 * count + 12 :]
        moves = s[-1]
        packs = [pltpu.make_async_copy(ref, data.at[pl.ds(at, size)], moves.at[i])
                 for i, (ref, (at, size)) in enumerate(zip(ins, layout))]
        for c in packs:
            c.start()
        data[used:] = jnp.zeros((rows - used, cols), jnp.float32)
        for c in packs:
            c.wait()
        _sum_kernel(nx, nz, data, part, cot, out, grad_out, xs, zs, ys, fin, from_pair, from_far, relay, s[:-1])
        unpacks = [pltpu.make_async_copy(out.at[pl.ds(at, size)], ref, moves.at[count + i])
                   for i, (ref, (at, size)) in enumerate(zip(outs, layout))]
        for c in unpacks:
            c.start()
        for c in unpacks:
            c.wait()

    return pl.pallas_call(
        body,
        out_shape=tuple(jax.ShapeDtypeStruct(p.shape, jnp.float32) for p in pieces)
        + (jax.ShapeDtypeStruct(cot.shape, cot.dtype),),
        in_specs=[pl.BlockSpec(memory_space=pltpu.VMEM)] * (count + 2),
        out_specs=(pl.BlockSpec(memory_space=pltpu.VMEM),) * (count + 1),
        scratch_shapes=[
            pltpu.VMEM((rows, cols), jnp.float32),
            pltpu.VMEM((rows, cols), jnp.float32),
            pltpu.VMEM((2, nx - 1, bx, half), jnp.float32),
            pltpu.VMEM((2, nz + 1, bz, half // 2), jnp.float32),
            pltpu.VMEM((2, bz, half // 2), jnp.float32),
            pltpu.VMEM((2, bz, half // 2), jnp.float32),
            pltpu.VMEM((2,) + block, jnp.float32),
            pltpu.VMEM(block, jnp.float32),
            pltpu.VMEM(block, jnp.float32),
        ] + sems,
        compiler_params=pltpu.CompilerParams(collective_id=0, has_side_effects=True,
                                             vmem_limit_bytes=48 * 1024 * 1024),
    )(*pieces, part, cot)


def _chan_gather_kernel(first, second, out_first, out_second, sems):
    coords = [lax.axis_index(a) for a in ALL_AXES]
    hi, core = coords[3], coords[4]

    def dev(h, c):
        return (coords[0], coords[1], coords[2], h, c)

    me = hi * 2 + core
    across = hi * 2 + (1 - core)
    over = (1 - hi) * 2 + core
    pair, far = dev(hi, 1 - core), dev(1 - hi, core)

    barrier = pltpu.get_barrier_semaphore()
    for d in (pair, far):
        pl.semaphore_signal(barrier, inc=1, device_id=d, device_id_type=MESH_ID)
    pl.semaphore_wait(barrier, 2)

    sources = (first, second)
    outs = (out_first, out_second)
    step_one = []
    for k in range(2):
        for j, target in enumerate((pair, far)):
            c = pltpu.make_async_remote_copy(
                src_ref=sources[k], dst_ref=outs[k].at[me], send_sem=sems.at[0, k, j],
                recv_sem=sems.at[1, k, j], device_id=target, device_id_type=MESH_ID)
            c.start()
            step_one.append(c)
    for k in range(2):
        outs[k][me] = sources[k][...]
    for c in step_one:
        c.wait_recv()
    relay = []
    for k in range(2):
        c = pltpu.make_async_remote_copy(
            src_ref=outs[k].at[over], dst_ref=outs[k].at[over], send_sem=sems.at[0, k, 2],
            recv_sem=sems.at[1, k, 2], device_id=pair, device_id_type=MESH_ID)
        c.start()
        relay.append(c)
    for c in relay:
        c.wait_recv()
    for c in step_one + relay:
        c.wait_send()


def chan_gather(first, second):
    shape = (4,) + first.shape
    result = pl.pallas_call(
        _chan_gather_kernel,
        out_shape=(jax.ShapeDtypeStruct(shape, first.dtype), jax.ShapeDtypeStruct(shape, second.dtype)),
        in_specs=[pl.BlockSpec(memory_space=pltpu.VMEM)] * 2,
        out_specs=(pl.BlockSpec(memory_space=pltpu.VMEM),) * 2,
        scratch_shapes=[pltpu.SemaphoreType.DMA((2, 2, 3))],
        compiler_params=pltpu.CompilerParams(collective_id=1, has_side_effects=True),
    )(first, second)
    return tuple(r.reshape((-1,) + first.shape[1:]) for r in result)


def extended(block, sides, width):
    for axis, dim in sides:
        count = 1
        for name in axis:
            count *= lax.axis_size(name)
        forward = [(i, i + 1) for i in range(count - 1)]
        backward = [(target, source) for source, target in forward]
        low = lax.ppermute(
            lax.slice_in_dim(block, block.shape[dim] - width, None, axis=dim), axis, forward
        )
        high = lax.ppermute(lax.slice_in_dim(block, 0, width, axis=dim), axis, backward)
        block = jnp.concatenate([low, block, high], axis=dim)
    return block


def gelu_parts(pre):
    cdf = 0.5 * (1.0 + lax.erf(pre * 0.7071067811865476))
    dens = jnp.exp(-0.5 * pre * pre) * 0.3989422804014327
    return (pre * cdf, cdf + pre * dens)


def shards(inputs, cotangent, expand_w, expand_b, depth_k, depth_b, project_w):
    rows_in, rows_cot = chan_gather(inputs, cotangent)
    nrows, ncols, cin = rows_in.shape
    hslice = expand_w.shape[1]
    flat_inputs = rows_in.reshape(nrows * ncols, cin)
    flat_cotan = rows_cot.reshape(nrows * ncols, cin)
    pre_one = (
        jnp.dot(flat_inputs, expand_w, preferred_element_type=jnp.float32).reshape(
            nrows, ncols, hslice
        )
        + expand_b
    )
    hidden, slope_one = gelu_parts(pre_one)
    hidden = hidden.astype(jnp.bfloat16)
    count = 1
    for name in ROW_AXES:
        count *= lax.axis_size(name)
    forward = [(i, i + 1) for i in range(count - 1)]
    backward = [(t, f) for f, t in forward]
    low = lax.ppermute(jnp.concatenate([hidden[nrows - 4 :], rows_cot[nrows - 2 :]], axis=0), ROW_AXES, forward)
    high = lax.ppermute(jnp.concatenate([hidden[:4], rows_cot[:2]], axis=0), ROW_AXES, backward)
    hidden_ext = jnp.concatenate([low[:4], hidden, high[:4]], axis=0)
    cot_ext = jnp.concatenate([low[4:], rows_cot, high[4:]], axis=0)
    wide = nrows + 4
    padded_ext = jnp.pad(hidden_ext, ((0, 0), (2, 2), (0, 0))).astype(jnp.float32)
    padded = padded_ext[2 : 2 + wide]
    pre_two = jnp.zeros((wide, ncols, hslice), jnp.float32) + depth_b
    for row_tap in range(5):
        for col_tap in range(5):
            pre_two = (
                pre_two
                + depth_k[5 * row_tap + col_tap]
                * padded_ext[row_tap : row_tap + wide, col_tap : col_tap + ncols]
            )
    mixed, slope_two = gelu_parts(pre_two)
    mixed = mixed[2 : 2 + nrows].astype(jnp.bfloat16).reshape(nrows * ncols, hslice)
    grad_w2 = jnp.dot(mixed.T, flat_cotan, preferred_element_type=jnp.float32)
    grad_mixed = jnp.dot(
        cot_ext.reshape(wide * ncols, cin), project_w.T, preferred_element_type=jnp.float32
    ).reshape(wide, ncols, hslice)
    grad_rimmed = (grad_mixed * slope_two).astype(jnp.bfloat16)
    grad_pre_f = grad_rimmed[2 : 2 + nrows].astype(jnp.float32)
    grad_bd = jnp.sum(grad_pre_f, axis=(0, 1))
    grad_pad = jnp.pad(grad_rimmed, ((0, 0), (2, 2), (0, 0))).astype(jnp.float32)
    taps = []
    grad_hidden = jnp.zeros((nrows, ncols, hslice), jnp.float32)
    for row_tap in range(5):
        for col_tap in range(5):
            taps.append(
                jnp.sum(
                    padded[row_tap : row_tap + nrows, col_tap : col_tap + ncols] * grad_pre_f,
                    axis=(0, 1),
                )
            )
            grad_hidden = (
                grad_hidden
                + depth_k[5 * row_tap + col_tap]
                * grad_pad[4 - row_tap : 4 - row_tap + nrows, 4 - col_tap : 4 - col_tap + ncols]
            )
    grad_k = jnp.stack(taps, axis=0)
    grad_act = (grad_hidden * slope_one).astype(jnp.bfloat16)
    flat_act = grad_act.reshape(nrows * ncols, hslice)
    grad_b1 = jnp.sum(flat_act.astype(jnp.float32), axis=0)
    grad_w1 = jnp.dot(flat_inputs.T, flat_act, preferred_element_type=jnp.float32)
    part = jnp.einsum("rwh,ch->rwc", grad_act, expand_w, preferred_element_type=jnp.float32)
    part = part.reshape((4, -1) + part.shape[1:])
    small = jnp.concatenate([grad_k, grad_b1[None], grad_bd[None]], axis=0)
    taps_count = grad_k.shape[0]
    small = jnp.pad(small, ((0, -small.shape[0] % 8), (0, 0)))
    nx, nz = lax.axis_size("x"), lax.axis_size("z")
    w1, w2, small, input_grad = row_group_allreduce([grad_w1, grad_w2, small], nx, nz, part, cotangent)
    summed = [w1, small[taps_count], small[:taps_count], small[taps_count + 1], w2]
    return (input_grad, summed[0], summed[1], summed[2], summed[3], summed[4])


def solution(mesh):
    fine = Mesh(mesh.devices.reshape(2, 8, 4, 2, 2), ROW_AXES + CHAN_AXES)
    rows = ROW_AXES + CHAN_AXES
    in_specs = (
        P(rows, None, None),
        P(rows, None, None),
        P(None, CHAN_AXES),
        P(CHAN_AXES),
        P(None, CHAN_AXES),
        P(CHAN_AXES),
        P(CHAN_AXES, None),
    )
    out_specs = (
        P(rows, None, None),
        P(None, CHAN_AXES),
        P(CHAN_AXES),
        P(None, CHAN_AXES),
        P(CHAN_AXES),
        P(CHAN_AXES, None),
    )
    return jax.shard_map(shards, mesh=fine, in_specs=in_specs, out_specs=out_specs, check_vma=False)
```

```python
import jax
import jax.numpy as jnp
from jax import lax
from jax.experimental import pallas as pl
from jax.experimental.pallas import tpu as pltpu
from jax.sharding import Mesh, PartitionSpec as P

MESH_ID = pl.DeviceIdType.MESH
ALL_AXES = ("y_lo", "z", "x", "y_hi", "core")
ROW_AXES = ("y_lo", "z", "x")
CHAN_AXES = ("y_hi", "core")


def _sum_kernel(nx, nz, data, part, cot, out, grad_out, xs, zs, ys, fin, from_pair, from_far, relay, sems):
    (xsend, xrecv, zsend, zrecv, ysend, yrecv, gzsend, gzrecv, gxsend, gxrecv, csems, local) = sems
    coords = [lax.axis_index(a) for a in ALL_AXES]
    iy, iz, ix = coords[0], coords[1], coords[2]
    hi, core = coords[3], coords[4]
    me = hi * 2 + core
    pair_at = hi * 2 + (1 - core)
    far_at = (1 - hi) * 2 + core
    diag_at = (1 - hi) * 2 + (1 - core)
    pair = (iy, iz, ix, hi, 1 - core)
    far = (iy, iz, ix, 1 - hi, core)

    def dev(y=None, z=None, x=None):
        c = list(coords)
        if y is not None:
            c[0] = y
        if z is not None:
            c[1] = z
        if x is not None:
            c[2] = x
        return tuple(c)

    x_next = [dev(x=lax.rem(ix + 1, nx)), dev(x=lax.rem(ix + nx - 1, nx))]
    z_next = [dev(z=lax.rem(iz + 1, nz)), dev(z=lax.rem(iz + nz - 1, nz))]
    partner = dev(y=1 - iy)

    barrier = pltpu.get_barrier_semaphore()
    z_peer = [None] + [dev(z=lax.rem(iz + d, nz)) for d in range(1, nz)]
    peers = [x_next[0], x_next[1], partner, pair, far] + z_peer[1:]
    if nx == 2:
        peers = peers[1:]
    for d in peers:
        pl.semaphore_signal(barrier, inc=1, device_id=d, device_id_type=MESH_ID)
    pl.semaphore_wait(barrier, len(peers))

    chan_one = []
    for j, src in enumerate((part.at[pair_at], part.at[diag_at])):
        c = pltpu.make_async_remote_copy(
            src_ref=src, dst_ref=from_pair.at[j], send_sem=csems.at[0, j],
            recv_sem=csems.at[1, j], device_id=pair, device_id_type=MESH_ID)
        c.start()
        chan_one.append(c)

    rows, cols = data.shape
    half = cols // 2
    bx = rows // nx
    bz = bx // (nz // 2)
    lanes = half // 2
    steps = (1, -1)

    def xblock(h, k):
        return (pl.ds(pl.multiple_of(lax.rem(k + 4 * nx, nx) * bx, 8), bx), pl.ds(h * half, half))

    def zblock(k):
        k = lax.rem(k + 4 * nz, nz)
        return (pl.ds(pl.multiple_of((k // 2) * bz, 8), bz), pl.ds(pl.multiple_of(lax.rem(k, 2) * lanes, 128), lanes))

    def oblock(h, kx, kz):
        r, c = zblock(kz)
        start = pl.multiple_of(lax.rem(kx + 4 * nx, nx) * bx + r.start, 8)
        return (pl.ds(start, bz), pl.ds(pl.multiple_of(h * half + c.start, 128), lanes))

    def obig(h, kx):
        return xblock(h, kx)

    for s in range(nx - 1):
        copies = []
        for h in range(2):
            sg = steps[h]
            src = data.at[xblock(h, ix - sg)] if s == 0 else xs.at[h, s - 1]
            c = pltpu.make_async_remote_copy(
                src_ref=src, dst_ref=xs.at[h, s], send_sem=xsend.at[h * nx + s],
                recv_sem=xrecv.at[h * nx + s], device_id=x_next[h], device_id_type=MESH_ID)
            c.start()
            copies.append(c)
        for h in range(2):
            sg = steps[h]
            copies[h].wait_recv()
            r, c = xblock(h, ix - sg * (s + 2))
            xs[h, s] = xs[h, s] + data[r, c]
            copies[h].wait_send()
    last = nx - 2
    for c in chan_one:
        c.wait_recv()
    relay[...] = part[far_at] + from_pair[1]
    chan_two = pltpu.make_async_remote_copy(
        src_ref=relay, dst_ref=from_far, send_sem=csems.at[0, 2],
        recv_sem=csems.at[1, 2], device_id=far, device_id_type=MESH_ID)
    chan_two.start()
    copies = []
    for h in range(2):
        for d in range(1, nz):
            c = pltpu.make_async_remote_copy(
                src_ref=xs.at[(h, last) + zblock(iz + d)], dst_ref=zs.at[h, d - 1],
                send_sem=zsend.at[h * nz + d], recv_sem=zrecv.at[h * nz + d],
                device_id=z_peer[d], device_id_type=MESH_ID)
            c.start()
            copies.append(c)
    own = [pltpu.make_async_copy(xs.at[(h, last) + zblock(iz)], zs.at[h, nz - 1], local.at[h]) for h in range(2)]
    for c in own:
        c.start()
    for c in own:
        c.wait()
    for c in copies:
        c.wait_recv()
    for h in range(2):
        acc = zs[h, nz - 1]
        for d in range(1, nz):
            acc = acc + zs[h, d - 1]
        zs[h, nz] = acc
    for c in copies:
        c.wait_send()
    zl = nz
    c = pltpu.make_async_remote_copy(
        src_ref=zs.at[:, zl], dst_ref=ys, send_sem=ysend.at[0], recv_sem=yrecv.at[0],
        device_id=partner, device_id_type=MESH_ID)
    c.start()
    c.wait_recv()
    for h in range(2):
        fin[h] = zs[h, zl] + ys[h]
    placed = [pltpu.make_async_copy(fin.at[h], out.at[oblock(h, ix, iz)], local.at[2 + h]) for h in range(2)]
    for p in placed:
        p.start()
    for p in placed:
        p.wait()
    c.wait_send()
    copies = []
    for h in range(2):
        loc = oblock(h, ix, iz)
        for d in range(1, nz):
            c = pltpu.make_async_remote_copy(
                src_ref=out.at[loc], dst_ref=out.at[loc], send_sem=gzsend.at[h * nz + d],
                recv_sem=gzrecv.at[h * nz + d], device_id=z_peer[d], device_id_type=MESH_ID)
            c.start()
            copies.append(c)
    for c in copies:
        c.wait_recv()
    for c in copies:
        c.wait_send()
    for s in range(nx - 1):
        copies = []
        for h in range(2):
            sg = steps[h]
            loc = obig(h, ix - sg * s)
            c = pltpu.make_async_remote_copy(
                src_ref=out.at[loc], dst_ref=out.at[loc], send_sem=gxsend.at[h * nx + s],
                recv_sem=gxrecv.at[h * nx + s], device_id=x_next[h], device_id_type=MESH_ID)
            c.start()
            copies.append(c)
        for h in range(2):
            copies[h].wait_recv()
            copies[h].wait_send()

    chan_two.wait_recv()
    total = part[me] + from_pair[0] + from_far[...]
    grad_out[...] = (cot[...].astype(jnp.float32) + total).astype(grad_out.dtype)
    for c in chan_one:
        c.wait_send()
    chan_two.wait_send()

def row_group_allreduce(pieces, nx, nz, part, cot):
    cols = pieces[0].shape[-1]
    layout = []
    at = 0
    for piece in pieces:
        layout.append((at, piece.shape[0]))
        at += piece.shape[0]
    quantum = 8 * nx * (nz // 2)
    rows = -(-at // quantum) * quantum
    used = at
    count = len(pieces)
    half = cols // 2
    bx = rows // nx
    bz = bx // (nz // 2)
    sems = [pltpu.SemaphoreType.DMA((2 * nx,)), pltpu.SemaphoreType.DMA((2 * nx,)),
            pltpu.SemaphoreType.DMA((2 * nz,)), pltpu.SemaphoreType.DMA((2 * nz,)),
            pltpu.SemaphoreType.DMA((1,)), pltpu.SemaphoreType.DMA((1,)),
            pltpu.SemaphoreType.DMA((2 * nz,)), pltpu.SemaphoreType.DMA((2 * nz,)),
            pltpu.SemaphoreType.DMA((2 * nx,)), pltpu.SemaphoreType.DMA((2 * nx,)),
            pltpu.SemaphoreType.DMA((2, 3)), pltpu.SemaphoreType.DMA((4,)),
            pltpu.SemaphoreType.DMA((2 * count + 1,))]
    block = part.shape[1:]

    def body(*refs):
        ins, outs = refs[:count], refs[count + 2 : 2 * count + 2]
        part, cot, grad_out = refs[count], refs[count + 1], refs[2 * count + 2]
        data, out, xs, zs, ys, fin, from_pair, from_far, relay, staged = refs[2 * count + 3 : 2 * count + 13]
        s = refs[2 * count + 13 :]
        moves = s[-1]
        packs = [pltpu.make_async_copy(ref, data.at[pl.ds(at, size)], moves.at[i])
                 for i, (ref, (at, size)) in enumerate(zip(ins, layout))]
        for c in packs:
            c.start()
        data[used:] = jnp.zeros((rows - used, cols), jnp.float32)
        for c in packs:
            c.wait()
        _sum_kernel(nx, nz, data, part, cot, out, staged, xs, zs, ys, fin, from_pair, from_far, relay, s[:-1])
        unpacks = [pltpu.make_async_copy(out.at[pl.ds(at, size)], ref, moves.at[count + i])
                   for i, (ref, (at, size)) in enumerate(zip(outs, layout))]
        unpacks.append(pltpu.make_async_copy(staged, grad_out, moves.at[2 * count]))
        for c in unpacks:
            c.start()
        for c in unpacks:
            c.wait()

    return pl.pallas_call(
        body,
        out_shape=tuple(jax.ShapeDtypeStruct(p.shape, jnp.float32) for p in pieces)
        + (jax.ShapeDtypeStruct(cot.shape, cot.dtype),),
        in_specs=[pl.BlockSpec(memory_space=pltpu.VMEM)] * (count + 2),
        out_specs=tuple(pl.BlockSpec(memory_space=pl.ANY if p.shape[0] >= 256 else pltpu.VMEM) for p in pieces)
        + (pl.BlockSpec(memory_space=pl.ANY),),
        scratch_shapes=[
            pltpu.VMEM((rows, cols), jnp.float32),
            pltpu.VMEM((rows, cols), jnp.float32),
            pltpu.VMEM((2, nx - 1, bx, half), jnp.float32),
            pltpu.VMEM((2, nz + 1, bz, half // 2), jnp.float32),
            pltpu.VMEM((2, bz, half // 2), jnp.float32),
            pltpu.VMEM((2, bz, half // 2), jnp.float32),
            pltpu.VMEM((2,) + block, jnp.float32),
            pltpu.VMEM(block, jnp.float32),
            pltpu.VMEM(block, jnp.float32),
            pltpu.VMEM(cot.shape, cot.dtype),
        ] + sems,
        compiler_params=pltpu.CompilerParams(collective_id=0, has_side_effects=True,
                                             vmem_limit_bytes=48 * 1024 * 1024),
    )(*pieces, part, cot)


def _chan_gather_kernel(first, second, out_first, out_second, sems):
    coords = [lax.axis_index(a) for a in ALL_AXES]
    hi, core = coords[3], coords[4]

    def dev(h, c):
        return (coords[0], coords[1], coords[2], h, c)

    me = hi * 2 + core
    across = hi * 2 + (1 - core)
    over = (1 - hi) * 2 + core
    pair, far = dev(hi, 1 - core), dev(1 - hi, core)

    barrier = pltpu.get_barrier_semaphore()
    for d in (pair, far):
        pl.semaphore_signal(barrier, inc=1, device_id=d, device_id_type=MESH_ID)
    pl.semaphore_wait(barrier, 2)

    sources = (first, second)
    outs = (out_first, out_second)
    step_one = []
    for k in range(2):
        for j, target in enumerate((pair, far)):
            c = pltpu.make_async_remote_copy(
                src_ref=sources[k], dst_ref=outs[k].at[me], send_sem=sems.at[0, k, j],
                recv_sem=sems.at[1, k, j], device_id=target, device_id_type=MESH_ID)
            c.start()
            step_one.append(c)
    for k in range(2):
        outs[k][me] = sources[k][...]
    for c in step_one:
        c.wait_recv()
    relay = []
    for k in range(2):
        c = pltpu.make_async_remote_copy(
            src_ref=outs[k].at[over], dst_ref=outs[k].at[over], send_sem=sems.at[0, k, 2],
            recv_sem=sems.at[1, k, 2], device_id=pair, device_id_type=MESH_ID)
        c.start()
        relay.append(c)
    for c in relay:
        c.wait_recv()
    for c in step_one + relay:
        c.wait_send()


def chan_gather(first, second):
    shape = (4,) + first.shape
    result = pl.pallas_call(
        _chan_gather_kernel,
        out_shape=(jax.ShapeDtypeStruct(shape, first.dtype), jax.ShapeDtypeStruct(shape, second.dtype)),
        in_specs=[pl.BlockSpec(memory_space=pltpu.VMEM)] * 2,
        out_specs=(pl.BlockSpec(memory_space=pltpu.VMEM),) * 2,
        scratch_shapes=[pltpu.SemaphoreType.DMA((2, 2, 3))],
        compiler_params=pltpu.CompilerParams(collective_id=1, has_side_effects=True),
    )(first, second)
    return tuple(r.reshape((-1,) + first.shape[1:]) for r in result)


def extended(block, sides, width):
    for axis, dim in sides:
        count = 1
        for name in axis:
            count *= lax.axis_size(name)
        forward = [(i, i + 1) for i in range(count - 1)]
        backward = [(target, source) for source, target in forward]
        low = lax.ppermute(
            lax.slice_in_dim(block, block.shape[dim] - width, None, axis=dim), axis, forward
        )
        high = lax.ppermute(lax.slice_in_dim(block, 0, width, axis=dim), axis, backward)
        block = jnp.concatenate([low, block, high], axis=dim)
    return block


def gelu_parts(pre):
    cdf = 0.5 * (1.0 + lax.erf(pre * 0.7071067811865476))
    dens = jnp.exp(-0.5 * pre * pre) * 0.3989422804014327
    return (pre * cdf, cdf + pre * dens)


def shards(inputs, cotangent, expand_w, expand_b, depth_k, depth_b, project_w):
    rows_in, rows_cot = chan_gather(inputs, cotangent)
    nrows, ncols, cin = rows_in.shape
    hslice = expand_w.shape[1]
    flat_inputs = rows_in.reshape(nrows * ncols, cin)
    flat_cotan = rows_cot.reshape(nrows * ncols, cin)
    pre_one = (
        jnp.dot(flat_inputs, expand_w, preferred_element_type=jnp.float32).reshape(
            nrows, ncols, hslice
        )
        + expand_b
    )
    hidden, slope_one = gelu_parts(pre_one)
    hidden = hidden.astype(jnp.bfloat16)
    rimmed = extended(hidden, ((ROW_AXES, 0),), 2)
    padded = jnp.pad(rimmed, ((0, 0), (2, 2), (0, 0))).astype(jnp.float32)
    pre_two = jnp.zeros((nrows, ncols, hslice), jnp.float32) + depth_b
    for row_tap in range(5):
        for col_tap in range(5):
            pre_two = (
                pre_two
                + depth_k[5 * row_tap + col_tap]
                * padded[row_tap : row_tap + nrows, col_tap : col_tap + ncols]
            )
    mixed, slope_two = gelu_parts(pre_two)
    mixed = mixed.astype(jnp.bfloat16).reshape(nrows * ncols, hslice)
    grad_w2 = jnp.dot(mixed.T, flat_cotan, preferred_element_type=jnp.float32)
    grad_mixed = jnp.dot(flat_cotan, project_w.T, preferred_element_type=jnp.float32).reshape(
        nrows, ncols, hslice
    )
    grad_pre = (grad_mixed * slope_two).astype(jnp.bfloat16)
    grad_pre_f = grad_pre.astype(jnp.float32)
    grad_bd = jnp.sum(grad_pre_f, axis=(0, 1))
    grad_rimmed = extended(grad_pre, ((ROW_AXES, 0),), 2)
    grad_pad = jnp.pad(grad_rimmed, ((0, 0), (2, 2), (0, 0))).astype(jnp.float32)
    taps = []
    grad_hidden = jnp.zeros((nrows, ncols, hslice), jnp.float32)
    for row_tap in range(5):
        for col_tap in range(5):
            taps.append(
                jnp.sum(
                    padded[row_tap : row_tap + nrows, col_tap : col_tap + ncols] * grad_pre_f,
                    axis=(0, 1),
                )
            )
            grad_hidden = (
                grad_hidden
                + depth_k[5 * row_tap + col_tap]
                * grad_pad[4 - row_tap : 4 - row_tap + nrows, 4 - col_tap : 4 - col_tap + ncols]
            )
    grad_k = jnp.stack(taps, axis=0)
    grad_act = (grad_hidden * slope_one).astype(jnp.bfloat16)
    flat_act = grad_act.reshape(nrows * ncols, hslice)
    grad_b1 = jnp.sum(flat_act.astype(jnp.float32), axis=0)
    grad_w1 = jnp.dot(flat_inputs.T, flat_act, preferred_element_type=jnp.float32)
    part = jnp.einsum("rwh,ch->rwc", grad_act, expand_w, preferred_element_type=jnp.float32)
    part = part.reshape((4, -1) + part.shape[1:])
    small = jnp.concatenate([grad_k, grad_b1[None], grad_bd[None]], axis=0)
    taps_count = grad_k.shape[0]
    small = jnp.pad(small, ((0, -small.shape[0] % 8), (0, 0)))
    nx, nz = lax.axis_size("x"), lax.axis_size("z")
    w1, w2, small, input_grad = row_group_allreduce([grad_w1, grad_w2, small], nx, nz, part, cotangent)
    summed = [w1, small[taps_count], small[:taps_count], small[taps_count + 1], w2]
    return (input_grad, summed[0], summed[1], summed[2], summed[3], summed[4])


def solution(mesh):
    fine = Mesh(mesh.devices.reshape(2, 8, 4, 2, 2), ROW_AXES + CHAN_AXES)
    rows = ROW_AXES + CHAN_AXES
    in_specs = (
        P(rows, None, None),
        P(rows, None, None),
        P(None, CHAN_AXES),
        P(CHAN_AXES),
        P(None, CHAN_AXES),
        P(CHAN_AXES),
        P(CHAN_AXES, None),
    )
    out_specs = (
        P(rows, None, None),
        P(None, CHAN_AXES),
        P(CHAN_AXES),
        P(None, CHAN_AXES),
        P(CHAN_AXES),
        P(CHAN_AXES, None),
    )
    return jax.shard_map(shards, mesh=fine, in_specs=in_specs, out_specs=out_specs, check_vma=False)
```

```python
import jax
import jax.numpy as jnp
from jax import lax
from jax.experimental import pallas as pl
from jax.experimental.pallas import tpu as pltpu
from jax.sharding import Mesh, PartitionSpec as P

MESH_ID = pl.DeviceIdType.MESH
ALL_AXES = ("y_lo", "z", "x", "y_hi", "core")
ROW_AXES = ("y_lo", "z", "x")
CHAN_AXES = ("y_hi", "core")


def _sum_kernel(nx, nz, data, part, cot, out, grad_out, xs, zs, ys, fin, from_pair, from_far, relay, sems):
    (xsend, xrecv, zsend, zrecv, ysend, yrecv, gzsend, gzrecv, gxsend, gxrecv, csems, local) = sems
    coords = [lax.axis_index(a) for a in ALL_AXES]
    iy, iz, ix = coords[0], coords[1], coords[2]
    hi, core = coords[3], coords[4]
    me = hi * 2 + core
    pair_at = hi * 2 + (1 - core)
    far_at = (1 - hi) * 2 + core
    diag_at = (1 - hi) * 2 + (1 - core)
    pair = (iy, iz, ix, hi, 1 - core)
    far = (iy, iz, ix, 1 - hi, core)

    def dev(y=None, z=None, x=None):
        c = list(coords)
        if y is not None:
            c[0] = y
        if z is not None:
            c[1] = z
        if x is not None:
            c[2] = x
        return tuple(c)

    x_next = [dev(x=lax.rem(ix + 1, nx)), dev(x=lax.rem(ix + nx - 1, nx))]
    z_next = [dev(z=lax.rem(iz + 1, nz)), dev(z=lax.rem(iz + nz - 1, nz))]
    partner = dev(y=1 - iy)

    barrier = pltpu.get_barrier_semaphore()
    z_peer = [None] + [dev(z=lax.rem(iz + d, nz)) for d in range(1, nz)]
    peers = [x_next[0], x_next[1], partner, pair, far] + z_peer[1:]
    if nx == 2:
        peers = peers[1:]
    for d in peers:
        pl.semaphore_signal(barrier, inc=1, device_id=d, device_id_type=MESH_ID)
    pl.semaphore_wait(barrier, len(peers))

    chan_one = []
    for j, src in enumerate((part.at[pair_at], part.at[diag_at])):
        c = pltpu.make_async_remote_copy(
            src_ref=src, dst_ref=from_pair.at[j], send_sem=csems.at[0, j],
            recv_sem=csems.at[1, j], device_id=pair, device_id_type=MESH_ID)
        c.start()
        chan_one.append(c)

    rows, cols = data.shape
    half = cols // 2
    bx = rows // nx
    bz = bx // (nz // 2)
    lanes = half // 2
    steps = (1, -1)

    def xblock(h, k):
        return (pl.ds(pl.multiple_of(lax.rem(k + 4 * nx, nx) * bx, 8), bx), pl.ds(h * half, half))

    def zblock(k):
        k = lax.rem(k + 4 * nz, nz)
        return (pl.ds(pl.multiple_of((k // 2) * bz, 8), bz), pl.ds(pl.multiple_of(lax.rem(k, 2) * lanes, 128), lanes))

    def oblock(h, kx, kz):
        r, c = zblock(kz)
        start = pl.multiple_of(lax.rem(kx + 4 * nx, nx) * bx + r.start, 8)
        return (pl.ds(start, bz), pl.ds(pl.multiple_of(h * half + c.start, 128), lanes))

    def obig(h, kx):
        return xblock(h, kx)

    pending = []
    for s in range(nx - 1):
        copies = []
        for h in range(2):
            sg = steps[h]
            src = data.at[xblock(h, ix - sg)] if s == 0 else xs.at[h, s - 1]
            c = pltpu.make_async_remote_copy(
                src_ref=src, dst_ref=xs.at[h, s], send_sem=xsend.at[h * nx + s],
                recv_sem=xrecv.at[h * nx + s], device_id=x_next[h], device_id_type=MESH_ID)
            c.start()
            copies.append(c)
        for h in range(2):
            sg = steps[h]
            copies[h].wait_recv()
            r, c = xblock(h, ix - sg * (s + 2))
            xs[h, s] = xs[h, s] + data[r, c]
        pending.extend(copies)
    last = nx - 2
    for c in chan_one:
        c.wait_recv()
    relay[...] = part[far_at] + from_pair[1]
    chan_two = pltpu.make_async_remote_copy(
        src_ref=relay, dst_ref=from_far, send_sem=csems.at[0, 2],
        recv_sem=csems.at[1, 2], device_id=far, device_id_type=MESH_ID)
    chan_two.start()
    copies = []
    for h in range(2):
        for d in range(1, nz):
            c = pltpu.make_async_remote_copy(
                src_ref=xs.at[(h, last) + zblock(iz + d)], dst_ref=zs.at[h, d - 1],
                send_sem=zsend.at[h * nz + d], recv_sem=zrecv.at[h * nz + d],
                device_id=z_peer[d], device_id_type=MESH_ID)
            c.start()
            copies.append(c)
    own = [pltpu.make_async_copy(xs.at[(h, last) + zblock(iz)], zs.at[h, nz - 1], local.at[h]) for h in range(2)]
    for c in own:
        c.start()
    for c in own:
        c.wait()
    for c in copies:
        c.wait_recv()
    for h in range(2):
        acc = zs[h, nz - 1]
        for d in range(1, nz):
            acc = acc + zs[h, d - 1]
        zs[h, nz] = acc
    pending.extend(copies)
    zl = nz
    c = pltpu.make_async_remote_copy(
        src_ref=zs.at[:, zl], dst_ref=ys, send_sem=ysend.at[0], recv_sem=yrecv.at[0],
        device_id=partner, device_id_type=MESH_ID)
    c.start()
    c.wait_recv()
    for h in range(2):
        fin[h] = zs[h, zl] + ys[h]
    placed = [pltpu.make_async_copy(fin.at[h], out.at[oblock(h, ix, iz)], local.at[2 + h]) for h in range(2)]
    for p in placed:
        p.start()
    for p in placed:
        p.wait()
    pending.append(c)
    copies = []
    for h in range(2):
        loc = oblock(h, ix, iz)
        for d in range(1, nz):
            c = pltpu.make_async_remote_copy(
                src_ref=out.at[loc], dst_ref=out.at[loc], send_sem=gzsend.at[h * nz + d],
                recv_sem=gzrecv.at[h * nz + d], device_id=z_peer[d], device_id_type=MESH_ID)
            c.start()
            copies.append(c)
    for c in copies:
        c.wait_recv()
    pending.extend(copies)
    for s in range(nx - 1):
        copies = []
        for h in range(2):
            sg = steps[h]
            loc = obig(h, ix - sg * s)
            c = pltpu.make_async_remote_copy(
                src_ref=out.at[loc], dst_ref=out.at[loc], send_sem=gxsend.at[h * nx + s],
                recv_sem=gxrecv.at[h * nx + s], device_id=x_next[h], device_id_type=MESH_ID)
            c.start()
            copies.append(c)
        for h in range(2):
            copies[h].wait_recv()
        pending.extend(copies)

    chan_two.wait_recv()
    total = part[me] + from_pair[0] + from_far[...]
    grad_out[...] = (cot[...].astype(jnp.float32) + total).astype(grad_out.dtype)
    for c in chan_one + [chan_two] + pending:
        c.wait_send()

def row_group_allreduce(pieces, nx, nz, part, cot):
    cols = pieces[0].shape[-1]
    layout = []
    at = 0
    for piece in pieces:
        layout.append((at, piece.shape[0]))
        at += piece.shape[0]
    quantum = 8 * nx * (nz // 2)
    rows = -(-at // quantum) * quantum
    used = at
    count = len(pieces)
    half = cols // 2
    bx = rows // nx
    bz = bx // (nz // 2)
    sems = [pltpu.SemaphoreType.DMA((2 * nx,)), pltpu.SemaphoreType.DMA((2 * nx,)),
            pltpu.SemaphoreType.DMA((2 * nz,)), pltpu.SemaphoreType.DMA((2 * nz,)),
            pltpu.SemaphoreType.DMA((1,)), pltpu.SemaphoreType.DMA((1,)),
            pltpu.SemaphoreType.DMA((2 * nz,)), pltpu.SemaphoreType.DMA((2 * nz,)),
            pltpu.SemaphoreType.DMA((2 * nx,)), pltpu.SemaphoreType.DMA((2 * nx,)),
            pltpu.SemaphoreType.DMA((2, 3)), pltpu.SemaphoreType.DMA((4,)),
            pltpu.SemaphoreType.DMA((2 * count,))]
    block = part.shape[1:]

    def body(*refs):
        ins, outs = refs[:count], refs[count + 2 : 2 * count + 2]
        part, cot, grad_out = refs[count], refs[count + 1], refs[2 * count + 2]
        data, out, xs, zs, ys, fin, from_pair, from_far, relay = refs[2 * count + 3 : 2 * count + 12]
        s = refs[2 * count + 12 :]
        moves = s[-1]
        packs = [pltpu.make_async_copy(ref, data.at[pl.ds(at, size)], moves.at[i])
                 for i, (ref, (at, size)) in enumerate(zip(ins, layout))]
        for c in packs:
            c.start()
        data[used:] = jnp.zeros((rows - used, cols), jnp.float32)
        for c in packs:
            c.wait()
        _sum_kernel(nx, nz, data, part, cot, out, grad_out, xs, zs, ys, fin, from_pair, from_far, relay, s[:-1])
        unpacks = [pltpu.make_async_copy(out.at[pl.ds(at, size)], ref, moves.at[count + i])
                   for i, (ref, (at, size)) in enumerate(zip(outs, layout))]
        for c in unpacks:
            c.start()
        for c in unpacks:
            c.wait()

    return pl.pallas_call(
        body,
        out_shape=tuple(jax.ShapeDtypeStruct(p.shape, jnp.float32) for p in pieces)
        + (jax.ShapeDtypeStruct(cot.shape, cot.dtype),),
        in_specs=[pl.BlockSpec(memory_space=pltpu.VMEM)] * (count + 2),
        out_specs=(pl.BlockSpec(memory_space=pltpu.VMEM),) * (count + 1),
        scratch_shapes=[
            pltpu.VMEM((rows, cols), jnp.float32),
            pltpu.VMEM((rows, cols), jnp.float32),
            pltpu.VMEM((2, nx - 1, bx, half), jnp.float32),
            pltpu.VMEM((2, nz + 1, bz, half // 2), jnp.float32),
            pltpu.VMEM((2, bz, half // 2), jnp.float32),
            pltpu.VMEM((2, bz, half // 2), jnp.float32),
            pltpu.VMEM((2,) + block, jnp.float32),
            pltpu.VMEM(block, jnp.float32),
            pltpu.VMEM(block, jnp.float32),
        ] + sems,
        compiler_params=pltpu.CompilerParams(collective_id=0, has_side_effects=True,
                                             vmem_limit_bytes=48 * 1024 * 1024),
    )(*pieces, part, cot)


def _chan_gather_kernel(first, second, out_first, out_second, sems):
    coords = [lax.axis_index(a) for a in ALL_AXES]
    hi, core = coords[3], coords[4]

    def dev(h, c):
        return (coords[0], coords[1], coords[2], h, c)

    me = hi * 2 + core
    across = hi * 2 + (1 - core)
    over = (1 - hi) * 2 + core
    pair, far = dev(hi, 1 - core), dev(1 - hi, core)

    barrier = pltpu.get_barrier_semaphore()
    for d in (pair, far):
        pl.semaphore_signal(barrier, inc=1, device_id=d, device_id_type=MESH_ID)
    pl.semaphore_wait(barrier, 2)

    sources = (first, second)
    outs = (out_first, out_second)
    step_one = []
    for k in range(2):
        for j, target in enumerate((pair, far)):
            c = pltpu.make_async_remote_copy(
                src_ref=sources[k], dst_ref=outs[k].at[me], send_sem=sems.at[0, k, j],
                recv_sem=sems.at[1, k, j], device_id=target, device_id_type=MESH_ID)
            c.start()
            step_one.append(c)
    for k in range(2):
        outs[k][me] = sources[k][...]
    for c in step_one:
        c.wait_recv()
    relay = []
    for k in range(2):
        c = pltpu.make_async_remote_copy(
            src_ref=outs[k].at[over], dst_ref=outs[k].at[over], send_sem=sems.at[0, k, 2],
            recv_sem=sems.at[1, k, 2], device_id=pair, device_id_type=MESH_ID)
        c.start()
        relay.append(c)
    for c in relay:
        c.wait_recv()
    for c in step_one + relay:
        c.wait_send()


def chan_gather(first, second):
    shape = (4,) + first.shape
    result = pl.pallas_call(
        _chan_gather_kernel,
        out_shape=(jax.ShapeDtypeStruct(shape, first.dtype), jax.ShapeDtypeStruct(shape, second.dtype)),
        in_specs=[pl.BlockSpec(memory_space=pltpu.VMEM)] * 2,
        out_specs=(pl.BlockSpec(memory_space=pltpu.VMEM),) * 2,
        scratch_shapes=[pltpu.SemaphoreType.DMA((2, 2, 3))],
        compiler_params=pltpu.CompilerParams(collective_id=1, has_side_effects=True),
    )(first, second)
    return tuple(r.reshape((-1,) + first.shape[1:]) for r in result)


def extended(block, sides, width):
    for axis, dim in sides:
        count = 1
        for name in axis:
            count *= lax.axis_size(name)
        forward = [(i, i + 1) for i in range(count - 1)]
        backward = [(target, source) for source, target in forward]
        low = lax.ppermute(
            lax.slice_in_dim(block, block.shape[dim] - width, None, axis=dim), axis, forward
        )
        high = lax.ppermute(lax.slice_in_dim(block, 0, width, axis=dim), axis, backward)
        block = jnp.concatenate([low, block, high], axis=dim)
    return block


def gelu_parts(pre):
    cdf = 0.5 * (1.0 + lax.erf(pre * 0.7071067811865476))
    dens = jnp.exp(-0.5 * pre * pre) * 0.3989422804014327
    return (pre * cdf, cdf + pre * dens)


def shards(inputs, cotangent, expand_w, expand_b, depth_k, depth_b, project_w):
    rows_in, rows_cot = chan_gather(inputs, cotangent)
    nrows, ncols, cin = rows_in.shape
    hslice = expand_w.shape[1]
    flat_inputs = rows_in.reshape(nrows * ncols, cin)
    flat_cotan = rows_cot.reshape(nrows * ncols, cin)
    pre_one = (
        jnp.dot(flat_inputs, expand_w, preferred_element_type=jnp.float32).reshape(
            nrows, ncols, hslice
        )
        + expand_b
    )
    hidden, slope_one = gelu_parts(pre_one)
    hidden = hidden.astype(jnp.bfloat16)
    rimmed = extended(hidden, ((ROW_AXES, 0),), 2)
    padded = jnp.pad(rimmed, ((0, 0), (2, 2), (0, 0))).astype(jnp.float32)
    pre_two = jnp.zeros((nrows, ncols, hslice), jnp.float32) + depth_b
    for row_tap in range(5):
        for col_tap in range(5):
            pre_two = (
                pre_two
                + depth_k[5 * row_tap + col_tap]
                * padded[row_tap : row_tap + nrows, col_tap : col_tap + ncols]
            )
    mixed, slope_two = gelu_parts(pre_two)
    mixed = mixed.astype(jnp.bfloat16).reshape(nrows * ncols, hslice)
    grad_w2 = jnp.dot(mixed.T, flat_cotan, preferred_element_type=jnp.float32)
    grad_mixed = jnp.dot(flat_cotan, project_w.T, preferred_element_type=jnp.float32).reshape(
        nrows, ncols, hslice
    )
    grad_pre = (grad_mixed * slope_two).astype(jnp.bfloat16)
    grad_pre_f = grad_pre.astype(jnp.float32)
    grad_bd = jnp.sum(grad_pre_f, axis=(0, 1))
    grad_rimmed = extended(grad_pre, ((ROW_AXES, 0),), 2)
    grad_pad = jnp.pad(grad_rimmed, ((0, 0), (2, 2), (0, 0))).astype(jnp.float32)
    taps = []
    grad_hidden = jnp.zeros((nrows, ncols, hslice), jnp.float32)
    for row_tap in range(5):
        for col_tap in range(5):
            taps.append(
                jnp.sum(
                    padded[row_tap : row_tap + nrows, col_tap : col_tap + ncols] * grad_pre_f,
                    axis=(0, 1),
                )
            )
            grad_hidden = (
                grad_hidden
                + depth_k[5 * row_tap + col_tap]
                * grad_pad[4 - row_tap : 4 - row_tap + nrows, 4 - col_tap : 4 - col_tap + ncols]
            )
    grad_k = jnp.stack(taps, axis=0)
    grad_act = (grad_hidden * slope_one).astype(jnp.bfloat16)
    flat_act = grad_act.reshape(nrows * ncols, hslice)
    grad_b1 = jnp.sum(flat_act.astype(jnp.float32), axis=0)
    grad_w1 = jnp.dot(flat_inputs.T, flat_act, preferred_element_type=jnp.float32)
    part = jnp.einsum("rwh,ch->rwc", grad_act, expand_w, preferred_element_type=jnp.float32)
    part = part.reshape((4, -1) + part.shape[1:])
    small = jnp.concatenate([grad_k, grad_b1[None], grad_bd[None]], axis=0)
    taps_count = grad_k.shape[0]
    small = jnp.pad(small, ((0, -small.shape[0] % 8), (0, 0)))
    nx, nz = lax.axis_size("x"), lax.axis_size("z")
    w1, w2, small, input_grad = row_group_allreduce([grad_w1, grad_w2, small], nx, nz, part, cotangent)
    summed = [w1, small[taps_count], small[:taps_count], small[taps_count + 1], w2]
    return (input_grad, summed[0], summed[1], summed[2], summed[3], summed[4])


def solution(mesh):
    fine = Mesh(mesh.devices.reshape(2, 8, 4, 2, 2), ROW_AXES + CHAN_AXES)
    rows = ROW_AXES + CHAN_AXES
    in_specs = (
        P(rows, None, None),
        P(rows, None, None),
        P(None, CHAN_AXES),
        P(CHAN_AXES),
        P(None, CHAN_AXES),
        P(CHAN_AXES),
        P(CHAN_AXES, None),
    )
    out_specs = (
        P(rows, None, None),
        P(None, CHAN_AXES),
        P(CHAN_AXES),
        P(None, CHAN_AXES),
        P(CHAN_AXES),
        P(CHAN_AXES, None),
    )
    return jax.shard_map(shards, mesh=fine, in_specs=in_specs, out_specs=out_specs, check_vma=False)
```

```python
import jax
import jax.numpy as jnp
from jax import lax
from jax.experimental import pallas as pl
from jax.experimental.pallas import tpu as pltpu
from jax.sharding import Mesh, PartitionSpec as P

MESH_ID = pl.DeviceIdType.MESH
ALL_AXES = ("y_lo", "z", "x", "y_hi", "core")
ROW_AXES = ("y_lo", "z", "x")
CHAN_AXES = ("y_hi", "core")


def _sum_kernel(nx, nz, data, part, cot, out, grad_out, xs, zs, ys, fin, from_pair, from_far, relay, sems):
    (xsend, xrecv, zsend, zrecv, ysend, yrecv, gzsend, gzrecv, gxsend, gxrecv, csems, local) = sems
    coords = [lax.axis_index(a) for a in ALL_AXES]
    iy, iz, ix = coords[0], coords[1], coords[2]
    hi, core = coords[3], coords[4]
    me = hi * 2 + core
    pair_at = hi * 2 + (1 - core)
    far_at = (1 - hi) * 2 + core
    diag_at = (1 - hi) * 2 + (1 - core)
    pair = (iy, iz, ix, hi, 1 - core)
    far = (iy, iz, ix, 1 - hi, core)

    def dev(y=None, z=None, x=None):
        c = list(coords)
        if y is not None:
            c[0] = y
        if z is not None:
            c[1] = z
        if x is not None:
            c[2] = x
        return tuple(c)

    x_next = [dev(x=lax.rem(ix + 1, nx)), dev(x=lax.rem(ix + nx - 1, nx))]
    z_next = [dev(z=lax.rem(iz + 1, nz)), dev(z=lax.rem(iz + nz - 1, nz))]
    partner = dev(y=1 - iy)

    barrier = pltpu.get_barrier_semaphore()
    z_peer = [None] + [dev(z=lax.rem(iz + d, nz)) for d in range(1, nz)]
    peers = [x_next[0], x_next[1], partner, pair, far] + z_peer[1:]
    if nx == 2:
        peers = peers[1:]
    for d in peers:
        pl.semaphore_signal(barrier, inc=1, device_id=d, device_id_type=MESH_ID)
    pl.semaphore_wait(barrier, len(peers))

    chan_one = []
    for j, src in enumerate((part.at[pair_at], part.at[diag_at])):
        c = pltpu.make_async_remote_copy(
            src_ref=src, dst_ref=from_pair.at[j], send_sem=csems.at[0, j],
            recv_sem=csems.at[1, j], device_id=pair, device_id_type=MESH_ID)
        c.start()
        chan_one.append(c)

    rows, cols = data.shape
    half = cols // 2
    bx = rows // nx
    bz = bx // (nz // 2)
    lanes = half // 2
    steps = (1, -1)

    def xblock(h, k):
        return (pl.ds(pl.multiple_of(lax.rem(k + 4 * nx, nx) * bx, 8), bx), pl.ds(h * half, half))

    def zblock(k):
        k = lax.rem(k + 4 * nz, nz)
        return (pl.ds(pl.multiple_of((k // 2) * bz, 8), bz), pl.ds(pl.multiple_of(lax.rem(k, 2) * lanes, 128), lanes))

    def oblock(h, kx, kz):
        r, c = zblock(kz)
        start = pl.multiple_of(lax.rem(kx + 4 * nx, nx) * bx + r.start, 8)
        return (pl.ds(start, bz), pl.ds(pl.multiple_of(h * half + c.start, 128), lanes))

    def obig(h, kx):
        return xblock(h, kx)

    for s in range(nx - 1):
        copies = []
        for h in range(2):
            sg = steps[h]
            src = data.at[xblock(h, ix - sg)] if s == 0 else xs.at[h, s - 1]
            c = pltpu.make_async_remote_copy(
                src_ref=src, dst_ref=xs.at[h, s], send_sem=xsend.at[h * nx + s],
                recv_sem=xrecv.at[h * nx + s], device_id=x_next[h], device_id_type=MESH_ID)
            c.start()
            copies.append(c)
        for h in range(2):
            sg = steps[h]
            copies[h].wait_recv()
            r, c = xblock(h, ix - sg * (s + 2))
            xs[h, s] = xs[h, s] + data[r, c]
            copies[h].wait_send()
    last = nx - 2
    for c in chan_one:
        c.wait_recv()
    relay[...] = part[far_at] + from_pair[1]
    chan_two = pltpu.make_async_remote_copy(
        src_ref=relay, dst_ref=from_far, send_sem=csems.at[0, 2],
        recv_sem=csems.at[1, 2], device_id=far, device_id_type=MESH_ID)
    chan_two.start()
    copies = []
    for h in range(2):
        for d in range(1, nz):
            c = pltpu.make_async_remote_copy(
                src_ref=xs.at[(h, last) + zblock(iz + d)], dst_ref=zs.at[h, d - 1],
                send_sem=zsend.at[h * nz + d], recv_sem=zrecv.at[h * nz + d],
                device_id=z_peer[d], device_id_type=MESH_ID)
            c.start()
            copies.append(c)
    own = [pltpu.make_async_copy(xs.at[(h, last) + zblock(iz)], zs.at[h, nz - 1], local.at[h]) for h in range(2)]
    for c in own:
        c.start()
    for c in own:
        c.wait()
    for c in copies:
        c.wait_recv()
    for h in range(2):
        acc = zs[h, nz - 1]
        for d in range(1, nz):
            acc = acc + zs[h, d - 1]
        zs[h, nz] = acc
    for c in copies:
        c.wait_send()
    zl = nz
    c = pltpu.make_async_remote_copy(
        src_ref=zs.at[:, zl], dst_ref=ys, send_sem=ysend.at[0], recv_sem=yrecv.at[0],
        device_id=partner, device_id_type=MESH_ID)
    c.start()
    c.wait_recv()
    for h in range(2):
        fin[h] = zs[h, zl] + ys[h]
    placed = [pltpu.make_async_copy(fin.at[h], out.at[oblock(h, ix, iz)], local.at[2 + h]) for h in range(2)]
    for p in placed:
        p.start()
    for p in placed:
        p.wait()
    c.wait_send()
    copies = []
    for h in range(2):
        loc = oblock(h, ix, iz)
        for d in range(1, nz):
            c = pltpu.make_async_remote_copy(
                src_ref=out.at[loc], dst_ref=out.at[loc], send_sem=gzsend.at[h * nz + d],
                recv_sem=gzrecv.at[h * nz + d], device_id=z_peer[d], device_id_type=MESH_ID)
            c.start()
            copies.append(c)
    for c in copies:
        c.wait_recv()
    for c in copies:
        c.wait_send()
    for s in range(nx - 1):
        copies = []
        for h in range(2):
            sg = steps[h]
            loc = obig(h, ix - sg * s)
            c = pltpu.make_async_remote_copy(
                src_ref=out.at[loc], dst_ref=out.at[loc], send_sem=gxsend.at[h * nx + s],
                recv_sem=gxrecv.at[h * nx + s], device_id=x_next[h], device_id_type=MESH_ID)
            c.start()
            copies.append(c)
        for h in range(2):
            copies[h].wait_recv()
            copies[h].wait_send()

    chan_two.wait_recv()
    total = part[me] + from_pair[0] + from_far[...]
    grad_out[...] = (cot[...].astype(jnp.float32) + total).astype(grad_out.dtype)
    for c in chan_one:
        c.wait_send()
    chan_two.wait_send()

def row_group_allreduce(pieces, nx, nz, part, cot):
    cols = pieces[0].shape[-1]
    layout = []
    at = 0
    for piece in pieces:
        layout.append((at, piece.shape[0]))
        at += piece.shape[0]
    quantum = 8 * nx * (nz // 2)
    rows = -(-at // quantum) * quantum
    used = at
    count = len(pieces)
    half = cols // 2
    bx = rows // nx
    bz = bx // (nz // 2)
    sems = [pltpu.SemaphoreType.DMA((2 * nx,)), pltpu.SemaphoreType.DMA((2 * nx,)),
            pltpu.SemaphoreType.DMA((2 * nz,)), pltpu.SemaphoreType.DMA((2 * nz,)),
            pltpu.SemaphoreType.DMA((1,)), pltpu.SemaphoreType.DMA((1,)),
            pltpu.SemaphoreType.DMA((2 * nz,)), pltpu.SemaphoreType.DMA((2 * nz,)),
            pltpu.SemaphoreType.DMA((2 * nx,)), pltpu.SemaphoreType.DMA((2 * nx,)),
            pltpu.SemaphoreType.DMA((2, 3)), pltpu.SemaphoreType.DMA((4,)),
            pltpu.SemaphoreType.DMA((2 * count,))]
    block = part.shape[1:]

    def body(*refs):
        ins, outs = refs[:count], refs[count + 2 : 2 * count + 2]
        part, cot, grad_out = refs[count], refs[count + 1], refs[2 * count + 2]
        data, out, xs, zs, ys, fin, from_pair, from_far, relay = refs[2 * count + 3 : 2 * count + 12]
        s = refs[2 * count + 12 :]
        moves = s[-1]
        packs = [pltpu.make_async_copy(ref, data.at[pl.ds(at, size)], moves.at[i])
                 for i, (ref, (at, size)) in enumerate(zip(ins, layout))]
        for c in packs:
            c.start()
        data[used:] = jnp.zeros((rows - used, cols), jnp.float32)
        for c in packs:
            c.wait()
        _sum_kernel(nx, nz, data, part, cot, out, grad_out, xs, zs, ys, fin, from_pair, from_far, relay, s[:-1])
        unpacks = [pltpu.make_async_copy(out.at[pl.ds(at, size)], ref, moves.at[count + i])
                   for i, (ref, (at, size)) in enumerate(zip(outs, layout))]
        for c in unpacks:
            c.start()
        for c in unpacks:
            c.wait()

    return pl.pallas_call(
        body,
        out_shape=tuple(jax.ShapeDtypeStruct(p.shape, jnp.float32) for p in pieces)
        + (jax.ShapeDtypeStruct(cot.shape, cot.dtype),),
        in_specs=[pl.BlockSpec(memory_space=pltpu.VMEM)] * (count + 2),
        out_specs=(pl.BlockSpec(memory_space=pltpu.VMEM),) * (count + 1),
        scratch_shapes=[
            pltpu.VMEM((rows, cols), jnp.float32),
            pltpu.VMEM((rows, cols), jnp.float32),
            pltpu.VMEM((2, nx - 1, bx, half), jnp.float32),
            pltpu.VMEM((2, nz + 1, bz, half // 2), jnp.float32),
            pltpu.VMEM((2, bz, half // 2), jnp.float32),
            pltpu.VMEM((2, bz, half // 2), jnp.float32),
            pltpu.VMEM((2,) + block, jnp.float32),
            pltpu.VMEM(block, jnp.float32),
            pltpu.VMEM(block, jnp.float32),
        ] + sems,
        compiler_params=pltpu.CompilerParams(collective_id=0, has_side_effects=True,
                                             vmem_limit_bytes=48 * 1024 * 1024),
    )(*pieces, part, cot)


def _chan_gather_kernel(first, second, out_first, out_second, sems):
    coords = [lax.axis_index(a) for a in ALL_AXES]
    hi, core = coords[3], coords[4]

    def dev(h, c):
        return (coords[0], coords[1], coords[2], h, c)

    me = hi * 2 + core
    across = hi * 2 + (1 - core)
    over = (1 - hi) * 2 + core
    pair, far = dev(hi, 1 - core), dev(1 - hi, core)

    barrier = pltpu.get_barrier_semaphore()
    for d in (pair, far):
        pl.semaphore_signal(barrier, inc=1, device_id=d, device_id_type=MESH_ID)
    pl.semaphore_wait(barrier, 2)

    sources = (first, second)
    outs = (out_first, out_second)
    step_one = []
    for k in range(2):
        for j, target in enumerate((pair, far)):
            c = pltpu.make_async_remote_copy(
                src_ref=sources[k], dst_ref=outs[k].at[me], send_sem=sems.at[0, k, j],
                recv_sem=sems.at[1, k, j], device_id=target, device_id_type=MESH_ID)
            c.start()
            step_one.append(c)
    for k in range(2):
        outs[k][me] = sources[k][...]
    relay = []
    for k in range(2):
        step_one[2 * k + 1].wait_recv()
        c = pltpu.make_async_remote_copy(
            src_ref=outs[k].at[over], dst_ref=outs[k].at[over], send_sem=sems.at[0, k, 2],
            recv_sem=sems.at[1, k, 2], device_id=pair, device_id_type=MESH_ID)
        c.start()
        relay.append(c)
    for k in range(2):
        step_one[2 * k].wait_recv()
    for c in relay:
        c.wait_recv()
    for c in step_one + relay:
        c.wait_send()


def chan_gather(first, second):
    shape = (4,) + first.shape
    result = pl.pallas_call(
        _chan_gather_kernel,
        out_shape=(jax.ShapeDtypeStruct(shape, first.dtype), jax.ShapeDtypeStruct(shape, second.dtype)),
        in_specs=[pl.BlockSpec(memory_space=pltpu.VMEM)] * 2,
        out_specs=(pl.BlockSpec(memory_space=pltpu.VMEM),) * 2,
        scratch_shapes=[pltpu.SemaphoreType.DMA((2, 2, 3))],
        compiler_params=pltpu.CompilerParams(collective_id=1, has_side_effects=True),
    )(first, second)
    return tuple(r.reshape((-1,) + first.shape[1:]) for r in result)


def extended(block, sides, width):
    for axis, dim in sides:
        count = 1
        for name in axis:
            count *= lax.axis_size(name)
        forward = [(i, i + 1) for i in range(count - 1)]
        backward = [(target, source) for source, target in forward]
        low = lax.ppermute(
            lax.slice_in_dim(block, block.shape[dim] - width, None, axis=dim), axis, forward
        )
        high = lax.ppermute(lax.slice_in_dim(block, 0, width, axis=dim), axis, backward)
        block = jnp.concatenate([low, block, high], axis=dim)
    return block


def gelu_parts(pre):
    cdf = 0.5 * (1.0 + lax.erf(pre * 0.7071067811865476))
    dens = jnp.exp(-0.5 * pre * pre) * 0.3989422804014327
    return (pre * cdf, cdf + pre * dens)


def shards(inputs, cotangent, expand_w, expand_b, depth_k, depth_b, project_w):
    rows_in, rows_cot = chan_gather(inputs, cotangent)
    nrows, ncols, cin = rows_in.shape
    hslice = expand_w.shape[1]
    flat_inputs = rows_in.reshape(nrows * ncols, cin)
    flat_cotan = rows_cot.reshape(nrows * ncols, cin)
    pre_one = (
        jnp.dot(flat_inputs, expand_w, preferred_element_type=jnp.float32).reshape(
            nrows, ncols, hslice
        )
        + expand_b
    )
    hidden, slope_one = gelu_parts(pre_one)
    hidden = hidden.astype(jnp.bfloat16)
    rimmed = extended(hidden, ((ROW_AXES, 0),), 2)
    padded = jnp.pad(rimmed, ((0, 0), (2, 2), (0, 0))).astype(jnp.float32)
    pre_two = jnp.zeros((nrows, ncols, hslice), jnp.float32) + depth_b
    for row_tap in range(5):
        for col_tap in range(5):
            pre_two = (
                pre_two
                + depth_k[5 * row_tap + col_tap]
                * padded[row_tap : row_tap + nrows, col_tap : col_tap + ncols]
            )
    mixed, slope_two = gelu_parts(pre_two)
    mixed = mixed.astype(jnp.bfloat16).reshape(nrows * ncols, hslice)
    grad_w2 = jnp.dot(mixed.T, flat_cotan, preferred_element_type=jnp.float32)
    grad_mixed = jnp.dot(flat_cotan, project_w.T, preferred_element_type=jnp.float32).reshape(
        nrows, ncols, hslice
    )
    grad_pre = (grad_mixed * slope_two).astype(jnp.bfloat16)
    grad_pre_f = grad_pre.astype(jnp.float32)
    grad_bd = jnp.sum(grad_pre_f, axis=(0, 1))
    grad_rimmed = extended(grad_pre, ((ROW_AXES, 0),), 2)
    grad_pad = jnp.pad(grad_rimmed, ((0, 0), (2, 2), (0, 0))).astype(jnp.float32)
    taps = []
    grad_hidden = jnp.zeros((nrows, ncols, hslice), jnp.float32)
    for row_tap in range(5):
        for col_tap in range(5):
            taps.append(
                jnp.sum(
                    padded[row_tap : row_tap + nrows, col_tap : col_tap + ncols] * grad_pre_f,
                    axis=(0, 1),
                )
            )
            grad_hidden = (
                grad_hidden
                + depth_k[5 * row_tap + col_tap]
                * grad_pad[4 - row_tap : 4 - row_tap + nrows, 4 - col_tap : 4 - col_tap + ncols]
            )
    grad_k = jnp.stack(taps, axis=0)
    grad_act = (grad_hidden * slope_one).astype(jnp.bfloat16)
    flat_act = grad_act.reshape(nrows * ncols, hslice)
    grad_b1 = jnp.sum(flat_act.astype(jnp.float32), axis=0)
    grad_w1 = jnp.dot(flat_inputs.T, flat_act, preferred_element_type=jnp.float32)
    part = jnp.einsum("rwh,ch->rwc", grad_act, expand_w, preferred_element_type=jnp.float32)
    part = part.reshape((4, -1) + part.shape[1:])
    small = jnp.concatenate([grad_k, grad_b1[None], grad_bd[None]], axis=0)
    taps_count = grad_k.shape[0]
    small = jnp.pad(small, ((0, -small.shape[0] % 8), (0, 0)))
    nx, nz = lax.axis_size("x"), lax.axis_size("z")
    w1, w2, small, input_grad = row_group_allreduce([grad_w1, grad_w2, small], nx, nz, part, cotangent)
    summed = [w1, small[taps_count], small[:taps_count], small[taps_count + 1], w2]
    return (input_grad, summed[0], summed[1], summed[2], summed[3], summed[4])


def solution(mesh):
    fine = Mesh(mesh.devices.reshape(2, 8, 4, 2, 2), ROW_AXES + CHAN_AXES)
    rows = ROW_AXES + CHAN_AXES
    in_specs = (
        P(rows, None, None),
        P(rows, None, None),
        P(None, CHAN_AXES),
        P(CHAN_AXES),
        P(None, CHAN_AXES),
        P(CHAN_AXES),
        P(CHAN_AXES, None),
    )
    out_specs = (
        P(rows, None, None),
        P(None, CHAN_AXES),
        P(CHAN_AXES),
        P(None, CHAN_AXES),
        P(CHAN_AXES),
        P(CHAN_AXES, None),
    )
    return jax.shard_map(shards, mesh=fine, in_specs=in_specs, out_specs=out_specs, check_vma=False)
```

```python
import jax
import jax.numpy as jnp
from jax import lax
from jax.experimental import pallas as pl
from jax.experimental.pallas import tpu as pltpu
from jax.sharding import Mesh, PartitionSpec as P

MESH_ID = pl.DeviceIdType.MESH
ALL_AXES = ("y_lo", "z", "x", "y_hi", "core")
ROW_AXES = ("y_lo", "z", "x")
CHAN_AXES = ("y_hi", "core")


def _sum_kernel(nx, nz, data, part, cot, out, grad_out, xs, zs, ys, fin, from_pair, from_far, relay, sems):
    (xsend, xrecv, zsend, zrecv, ysend, yrecv, gzsend, gzrecv, gxsend, gxrecv, csems, local) = sems
    coords = [lax.axis_index(a) for a in ALL_AXES]
    iy, iz, ix = coords[0], coords[1], coords[2]
    hi, core = coords[3], coords[4]
    me = hi * 2 + core
    pair_at = hi * 2 + (1 - core)
    far_at = (1 - hi) * 2 + core
    diag_at = (1 - hi) * 2 + (1 - core)
    pair = (iy, iz, ix, hi, 1 - core)
    far = (iy, iz, ix, 1 - hi, core)

    def dev(y=None, z=None, x=None):
        c = list(coords)
        if y is not None:
            c[0] = y
        if z is not None:
            c[1] = z
        if x is not None:
            c[2] = x
        return tuple(c)

    x_next = [dev(x=lax.rem(ix + 1, nx)), dev(x=lax.rem(ix + nx - 1, nx))]
    z_next = [dev(z=lax.rem(iz + 1, nz)), dev(z=lax.rem(iz + nz - 1, nz))]
    partner = dev(y=1 - iy)

    barrier = pltpu.get_barrier_semaphore()
    z_peer = [None] + [dev(z=lax.rem(iz + d, nz)) for d in range(1, nz)]
    peers = [x_next[0], x_next[1], partner, pair, far] + z_peer[1:]
    if nx == 2:
        peers = peers[1:]
    for d in peers:
        pl.semaphore_signal(barrier, inc=1, device_id=d, device_id_type=MESH_ID)
    pl.semaphore_wait(barrier, len(peers))

    chan_one = []
    for j, src in enumerate((part.at[pair_at], part.at[diag_at])):
        c = pltpu.make_async_remote_copy(
            src_ref=src, dst_ref=from_pair.at[j], send_sem=csems.at[0, j],
            recv_sem=csems.at[1, j], device_id=pair, device_id_type=MESH_ID)
        c.start()
        chan_one.append(c)

    rows, cols = data.shape
    half = cols // 2
    bx = rows // nx
    bz = bx // (nz // 2)
    lanes = half // 2
    steps = (1, -1)

    def xblock(h, k):
        return (pl.ds(pl.multiple_of(lax.rem(k + 4 * nx, nx) * bx, 8), bx), pl.ds(h * half, half))

    def zblock(k):
        k = lax.rem(k + 4 * nz, nz)
        return (pl.ds(pl.multiple_of((k // 2) * bz, 8), bz), pl.ds(pl.multiple_of(lax.rem(k, 2) * lanes, 128), lanes))

    def oblock(h, kx, kz):
        r, c = zblock(kz)
        start = pl.multiple_of(lax.rem(kx + 4 * nx, nx) * bx + r.start, 8)
        return (pl.ds(start, bz), pl.ds(pl.multiple_of(h * half + c.start, 128), lanes))

    def obig(h, kx):
        return xblock(h, kx)

    for s in range(nx - 1):
        copies = []
        for h in range(2):
            sg = steps[h]
            src = data.at[xblock(h, ix - sg)] if s == 0 else xs.at[h, s - 1]
            c = pltpu.make_async_remote_copy(
                src_ref=src, dst_ref=xs.at[h, s], send_sem=xsend.at[h * nx + s],
                recv_sem=xrecv.at[h * nx + s], device_id=x_next[h], device_id_type=MESH_ID)
            c.start()
            copies.append(c)
        for h in range(2):
            sg = steps[h]
            copies[h].wait_recv()
            r, c = xblock(h, ix - sg * (s + 2))
            xs[h, s] = xs[h, s] + data[r, c]
            copies[h].wait_send()
    last = nx - 2
    for c in chan_one:
        c.wait_recv()
    relay[...] = part[far_at] + from_pair[1]
    chan_two = pltpu.make_async_remote_copy(
        src_ref=relay, dst_ref=from_far, send_sem=csems.at[0, 2],
        recv_sem=csems.at[1, 2], device_id=far, device_id_type=MESH_ID)
    chan_two.start()
    copies = []
    for h in range(2):
        for d in range(1, nz):
            c = pltpu.make_async_remote_copy(
                src_ref=xs.at[(h, last) + zblock(iz + d)], dst_ref=zs.at[h, d - 1],
                send_sem=zsend.at[h * nz + d], recv_sem=zrecv.at[h * nz + d],
                device_id=z_peer[d], device_id_type=MESH_ID)
            c.start()
            copies.append(c)
    own = [pltpu.make_async_copy(xs.at[(h, last) + zblock(iz)], zs.at[h, nz - 1], local.at[h]) for h in range(2)]
    for c in own:
        c.start()
    for c in own:
        c.wait()
    for c in copies:
        c.wait_recv()
    for h in range(2):
        acc = zs[h, nz - 1]
        for d in range(1, nz):
            acc = acc + zs[h, d - 1]
        zs[h, nz] = acc
    for c in copies:
        c.wait_send()
    zl = nz
    c = pltpu.make_async_remote_copy(
        src_ref=zs.at[:, zl], dst_ref=ys, send_sem=ysend.at[0], recv_sem=yrecv.at[0],
        device_id=partner, device_id_type=MESH_ID)
    c.start()
    c.wait_recv()
    for h in range(2):
        fin[h] = zs[h, zl] + ys[h]
    placed = [pltpu.make_async_copy(fin.at[h], out.at[oblock(h, ix, iz)], local.at[2 + h]) for h in range(2)]
    for p in placed:
        p.start()
    for p in placed:
        p.wait()
    c.wait_send()
    copies = []
    for h in range(2):
        loc = oblock(h, ix, iz)
        for d in range(1, nz):
            c = pltpu.make_async_remote_copy(
                src_ref=out.at[loc], dst_ref=out.at[loc], send_sem=gzsend.at[h * nz + d],
                recv_sem=gzrecv.at[h * nz + d], device_id=z_peer[d], device_id_type=MESH_ID)
            c.start()
            copies.append(c)
    for c in copies:
        c.wait_recv()
    for c in copies:
        c.wait_send()
    first = [[None, None], [None, None]]
    for h in range(2):
        loc = obig(h, ix)
        for j in range(2):
            c = pltpu.make_async_remote_copy(
                src_ref=out.at[loc], dst_ref=out.at[loc], send_sem=gxsend.at[h * nx + j],
                recv_sem=gxrecv.at[h * nx + j], device_id=x_next[j], device_id_type=MESH_ID)
            c.start()
            first[h][j] = c
    second = []
    for h in range(2):
        first[h][h].wait_recv()
        loc = obig(h, ix - steps[h])
        c = pltpu.make_async_remote_copy(
            src_ref=out.at[loc], dst_ref=out.at[loc], send_sem=gxsend.at[h * nx + 2],
            recv_sem=gxrecv.at[h * nx + 2], device_id=x_next[h], device_id_type=MESH_ID)
        c.start()
        second.append(c)
    for h in range(2):
        first[h][1 - h].wait_recv()
    for c in second:
        c.wait_recv()
    for c in first[0] + first[1] + second:
        c.wait_send()

    chan_two.wait_recv()
    total = part[me] + from_pair[0] + from_far[...]
    grad_out[...] = (cot[...].astype(jnp.float32) + total).astype(grad_out.dtype)
    for c in chan_one:
        c.wait_send()
    chan_two.wait_send()

def row_group_allreduce(pieces, nx, nz, part, cot):
    cols = pieces[0].shape[-1]
    layout = []
    at = 0
    for piece in pieces:
        layout.append((at, piece.shape[0]))
        at += piece.shape[0]
    quantum = 8 * nx * (nz // 2)
    rows = -(-at // quantum) * quantum
    used = at
    count = len(pieces)
    half = cols // 2
    bx = rows // nx
    bz = bx // (nz // 2)
    sems = [pltpu.SemaphoreType.DMA((2 * nx,)), pltpu.SemaphoreType.DMA((2 * nx,)),
            pltpu.SemaphoreType.DMA((2 * nz,)), pltpu.SemaphoreType.DMA((2 * nz,)),
            pltpu.SemaphoreType.DMA((1,)), pltpu.SemaphoreType.DMA((1,)),
            pltpu.SemaphoreType.DMA((2 * nz,)), pltpu.SemaphoreType.DMA((2 * nz,)),
            pltpu.SemaphoreType.DMA((2 * nx,)), pltpu.SemaphoreType.DMA((2 * nx,)),
            pltpu.SemaphoreType.DMA((2, 3)), pltpu.SemaphoreType.DMA((4,)),
            pltpu.SemaphoreType.DMA((2 * count,))]
    block = part.shape[1:]

    def body(*refs):
        ins, outs = refs[:count], refs[count + 2 : 2 * count + 2]
        part, cot, grad_out = refs[count], refs[count + 1], refs[2 * count + 2]
        data, out, xs, zs, ys, fin, from_pair, from_far, relay = refs[2 * count + 3 : 2 * count + 12]
        s = refs[2 * count + 12 :]
        moves = s[-1]
        packs = [pltpu.make_async_copy(ref, data.at[pl.ds(at, size)], moves.at[i])
                 for i, (ref, (at, size)) in enumerate(zip(ins, layout))]
        for c in packs:
            c.start()
        data[used:] = jnp.zeros((rows - used, cols), jnp.float32)
        for c in packs:
            c.wait()
        _sum_kernel(nx, nz, data, part, cot, out, grad_out, xs, zs, ys, fin, from_pair, from_far, relay, s[:-1])
        unpacks = [pltpu.make_async_copy(out.at[pl.ds(at, size)], ref, moves.at[count + i])
                   for i, (ref, (at, size)) in enumerate(zip(outs, layout))]
        for c in unpacks:
            c.start()
        for c in unpacks:
            c.wait()

    return pl.pallas_call(
        body,
        out_shape=tuple(jax.ShapeDtypeStruct(p.shape, jnp.float32) for p in pieces)
        + (jax.ShapeDtypeStruct(cot.shape, cot.dtype),),
        in_specs=[pl.BlockSpec(memory_space=pltpu.VMEM)] * (count + 2),
        out_specs=(pl.BlockSpec(memory_space=pltpu.VMEM),) * (count + 1),
        scratch_shapes=[
            pltpu.VMEM((rows, cols), jnp.float32),
            pltpu.VMEM((rows, cols), jnp.float32),
            pltpu.VMEM((2, nx - 1, bx, half), jnp.float32),
            pltpu.VMEM((2, nz + 1, bz, half // 2), jnp.float32),
            pltpu.VMEM((2, bz, half // 2), jnp.float32),
            pltpu.VMEM((2, bz, half // 2), jnp.float32),
            pltpu.VMEM((2,) + block, jnp.float32),
            pltpu.VMEM(block, jnp.float32),
            pltpu.VMEM(block, jnp.float32),
        ] + sems,
        compiler_params=pltpu.CompilerParams(collective_id=0, has_side_effects=True,
                                             vmem_limit_bytes=48 * 1024 * 1024),
    )(*pieces, part, cot)


def _chan_gather_kernel(first, second, out_first, out_second, sems):
    coords = [lax.axis_index(a) for a in ALL_AXES]
    hi, core = coords[3], coords[4]

    def dev(h, c):
        return (coords[0], coords[1], coords[2], h, c)

    me = hi * 2 + core
    across = hi * 2 + (1 - core)
    over = (1 - hi) * 2 + core
    pair, far = dev(hi, 1 - core), dev(1 - hi, core)

    barrier = pltpu.get_barrier_semaphore()
    for d in (pair, far):
        pl.semaphore_signal(barrier, inc=1, device_id=d, device_id_type=MESH_ID)
    pl.semaphore_wait(barrier, 2)

    sources = (first, second)
    outs = (out_first, out_second)
    step_one = []
    for k in range(2):
        for j, target in enumerate((pair, far)):
            c = pltpu.make_async_remote_copy(
                src_ref=sources[k], dst_ref=outs[k].at[me], send_sem=sems.at[0, k, j],
                recv_sem=sems.at[1, k, j], device_id=target, device_id_type=MESH_ID)
            c.start()
            step_one.append(c)
    for k in range(2):
        outs[k][me] = sources[k][...]
    relay = []
    for k in range(2):
        step_one[2 * k + 1].wait_recv()
        c = pltpu.make_async_remote_copy(
            src_ref=outs[k].at[over], dst_ref=outs[k].at[over], send_sem=sems.at[0, k, 2],
            recv_sem=sems.at[1, k, 2], device_id=pair, device_id_type=MESH_ID)
        c.start()
        relay.append(c)
    for k in range(2):
        step_one[2 * k].wait_recv()
    for c in relay:
        c.wait_recv()
    for c in step_one + relay:
        c.wait_send()


def chan_gather(first, second):
    shape = (4,) + first.shape
    result = pl.pallas_call(
        _chan_gather_kernel,
        out_shape=(jax.ShapeDtypeStruct(shape, first.dtype), jax.ShapeDtypeStruct(shape, second.dtype)),
        in_specs=[pl.BlockSpec(memory_space=pltpu.VMEM)] * 2,
        out_specs=(pl.BlockSpec(memory_space=pltpu.VMEM),) * 2,
        scratch_shapes=[pltpu.SemaphoreType.DMA((2, 2, 3))],
        compiler_params=pltpu.CompilerParams(collective_id=1, has_side_effects=True),
    )(first, second)
    return tuple(r.reshape((-1,) + first.shape[1:]) for r in result)


def extended(block, sides, width):
    for axis, dim in sides:
        count = 1
        for name in axis:
            count *= lax.axis_size(name)
        forward = [(i, i + 1) for i in range(count - 1)]
        backward = [(target, source) for source, target in forward]
        low = lax.ppermute(
            lax.slice_in_dim(block, block.shape[dim] - width, None, axis=dim), axis, forward
        )
        high = lax.ppermute(lax.slice_in_dim(block, 0, width, axis=dim), axis, backward)
        block = jnp.concatenate([low, block, high], axis=dim)
    return block


def gelu_parts(pre):
    cdf = 0.5 * (1.0 + lax.erf(pre * 0.7071067811865476))
    dens = jnp.exp(-0.5 * pre * pre) * 0.3989422804014327
    return (pre * cdf, cdf + pre * dens)


def shards(inputs, cotangent, expand_w, expand_b, depth_k, depth_b, project_w):
    rows_in, rows_cot = chan_gather(inputs, cotangent)
    nrows, ncols, cin = rows_in.shape
    hslice = expand_w.shape[1]
    flat_inputs = rows_in.reshape(nrows * ncols, cin)
    flat_cotan = rows_cot.reshape(nrows * ncols, cin)
    pre_one = (
        jnp.dot(flat_inputs, expand_w, preferred_element_type=jnp.float32).reshape(
            nrows, ncols, hslice
        )
        + expand_b
    )
    hidden, slope_one = gelu_parts(pre_one)
    hidden = hidden.astype(jnp.bfloat16)
    rimmed = extended(hidden, ((ROW_AXES, 0),), 2)
    padded = jnp.pad(rimmed, ((0, 0), (2, 2), (0, 0))).astype(jnp.float32)
    pre_two = jnp.zeros((nrows, ncols, hslice), jnp.float32) + depth_b
    for row_tap in range(5):
        for col_tap in range(5):
            pre_two = (
                pre_two
                + depth_k[5 * row_tap + col_tap]
                * padded[row_tap : row_tap + nrows, col_tap : col_tap + ncols]
            )
    mixed, slope_two = gelu_parts(pre_two)
    mixed = mixed.astype(jnp.bfloat16).reshape(nrows * ncols, hslice)
    grad_w2 = jnp.dot(mixed.T, flat_cotan, preferred_element_type=jnp.float32)
    grad_mixed = jnp.dot(flat_cotan, project_w.T, preferred_element_type=jnp.float32).reshape(
        nrows, ncols, hslice
    )
    grad_pre = (grad_mixed * slope_two).astype(jnp.bfloat16)
    grad_pre_f = grad_pre.astype(jnp.float32)
    grad_bd = jnp.sum(grad_pre_f, axis=(0, 1))
    grad_rimmed = extended(grad_pre, ((ROW_AXES, 0),), 2)
    grad_pad = jnp.pad(grad_rimmed, ((0, 0), (2, 2), (0, 0))).astype(jnp.float32)
    taps = []
    grad_hidden = jnp.zeros((nrows, ncols, hslice), jnp.float32)
    for row_tap in range(5):
        for col_tap in range(5):
            taps.append(
                jnp.sum(
                    padded[row_tap : row_tap + nrows, col_tap : col_tap + ncols] * grad_pre_f,
                    axis=(0, 1),
                )
            )
            grad_hidden = (
                grad_hidden
                + depth_k[5 * row_tap + col_tap]
                * grad_pad[4 - row_tap : 4 - row_tap + nrows, 4 - col_tap : 4 - col_tap + ncols]
            )
    grad_k = jnp.stack(taps, axis=0)
    grad_act = (grad_hidden * slope_one).astype(jnp.bfloat16)
    flat_act = grad_act.reshape(nrows * ncols, hslice)
    grad_b1 = jnp.sum(flat_act.astype(jnp.float32), axis=0)
    grad_w1 = jnp.dot(flat_inputs.T, flat_act, preferred_element_type=jnp.float32)
    part = jnp.einsum("rwh,ch->rwc", grad_act, expand_w, preferred_element_type=jnp.float32)
    part = part.reshape((4, -1) + part.shape[1:])
    small = jnp.concatenate([grad_k, grad_b1[None], grad_bd[None]], axis=0)
    taps_count = grad_k.shape[0]
    small = jnp.pad(small, ((0, -small.shape[0] % 8), (0, 0)))
    nx, nz = lax.axis_size("x"), lax.axis_size("z")
    w1, w2, small, input_grad = row_group_allreduce([grad_w1, grad_w2, small], nx, nz, part, cotangent)
    summed = [w1, small[taps_count], small[:taps_count], small[taps_count + 1], w2]
    return (input_grad, summed[0], summed[1], summed[2], summed[3], summed[4])


def solution(mesh):
    fine = Mesh(mesh.devices.reshape(2, 8, 4, 2, 2), ROW_AXES + CHAN_AXES)
    rows = ROW_AXES + CHAN_AXES
    in_specs = (
        P(rows, None, None),
        P(rows, None, None),
        P(None, CHAN_AXES),
        P(CHAN_AXES),
        P(None, CHAN_AXES),
        P(CHAN_AXES),
        P(CHAN_AXES, None),
    )
    out_specs = (
        P(rows, None, None),
        P(None, CHAN_AXES),
        P(CHAN_AXES),
        P(None, CHAN_AXES),
        P(CHAN_AXES),
        P(CHAN_AXES, None),
    )
    return jax.shard_map(shards, mesh=fine, in_specs=in_specs, out_specs=out_specs, check_vma=False)
```

```python
import jax
import jax.numpy as jnp
from jax import lax
from jax.experimental import pallas as pl
from jax.experimental.pallas import tpu as pltpu
from jax.sharding import Mesh, PartitionSpec as P

MESH_ID = pl.DeviceIdType.MESH
ALL_AXES = ("y_lo", "z", "x", "y_hi", "core")
ROW_AXES = ("y_lo", "z", "x")
CHAN_AXES = ("y_hi", "core")


def _sum_kernel(nx, nz, data, part, cot, out, grad_out, xs, zs, ys, fin, from_pair, from_far, relay, sems):
    (xsend, xrecv, zsend, zrecv, ysend, yrecv, gzsend, gzrecv, gxsend, gxrecv, csems, local) = sems
    coords = [lax.axis_index(a) for a in ALL_AXES]
    iy, iz, ix = coords[0], coords[1], coords[2]
    hi, core = coords[3], coords[4]
    me = hi * 2 + core
    pair_at = hi * 2 + (1 - core)
    far_at = (1 - hi) * 2 + core
    diag_at = (1 - hi) * 2 + (1 - core)
    pair = (iy, iz, ix, hi, 1 - core)
    far = (iy, iz, ix, 1 - hi, core)

    def dev(y=None, z=None, x=None):
        c = list(coords)
        if y is not None:
            c[0] = y
        if z is not None:
            c[1] = z
        if x is not None:
            c[2] = x
        return tuple(c)

    x_next = [dev(x=lax.rem(ix + 1, nx)), dev(x=lax.rem(ix + nx - 1, nx))]
    z_next = [dev(z=lax.rem(iz + 1, nz)), dev(z=lax.rem(iz + nz - 1, nz))]
    partner = dev(y=1 - iy)

    barrier = pltpu.get_barrier_semaphore()
    z_peer = [None] + [dev(z=lax.rem(iz + d, nz)) for d in range(1, nz)]
    peers = [x_next[0], x_next[1], partner, pair, far] + z_peer[1:]
    if nx == 2:
        peers = peers[1:]
    for d in peers:
        pl.semaphore_signal(barrier, inc=1, device_id=d, device_id_type=MESH_ID)
    pl.semaphore_wait(barrier, len(peers))

    chan_one = []
    for j, src in enumerate((part.at[pair_at], part.at[diag_at])):
        c = pltpu.make_async_remote_copy(
            src_ref=src, dst_ref=from_pair.at[j], send_sem=csems.at[0, j],
            recv_sem=csems.at[1, j], device_id=pair, device_id_type=MESH_ID)
        c.start()
        chan_one.append(c)

    rows, cols = data.shape
    half = cols // 2
    bx = rows // nx
    bz = bx // (nz // 2)
    lanes = half // 2
    steps = (1, -1)

    def xblock(h, k):
        return (pl.ds(pl.multiple_of(lax.rem(k + 4 * nx, nx) * bx, 8), bx), pl.ds(h * half, half))

    def zblock(k):
        k = lax.rem(k + 4 * nz, nz)
        return (pl.ds(pl.multiple_of((k // 2) * bz, 8), bz), pl.ds(pl.multiple_of(lax.rem(k, 2) * lanes, 128), lanes))

    def oblock(h, kx, kz):
        r, c = zblock(kz)
        start = pl.multiple_of(lax.rem(kx + 4 * nx, nx) * bx + r.start, 8)
        return (pl.ds(start, bz), pl.ds(pl.multiple_of(h * half + c.start, 128), lanes))

    def obig(h, kx):
        return xblock(h, kx)

    rs_one = [[None, None], [None, None]]
    for h in range(2):
        sg = steps[h]
        for j, (k, target) in enumerate(((ix + 2 * sg, x_next[h]), (ix - sg, x_next[1 - h]))):
            c = pltpu.make_async_remote_copy(
                src_ref=data.at[xblock(h, k)], dst_ref=xs.at[h, j], send_sem=xsend.at[h * nx + j],
                recv_sem=xrecv.at[h * nx + j], device_id=target, device_id_type=MESH_ID)
            c.start()
            rs_one[h][j] = c
    rs_two = []
    for h in range(2):
        sg = steps[h]
        rs_one[h][0].wait_recv()
        r, c = xblock(h, ix + sg)
        xs[h, 0] = xs[h, 0] + data[r, c]
        copy = pltpu.make_async_remote_copy(
            src_ref=xs.at[h, 0], dst_ref=xs.at[h, 2], send_sem=xsend.at[h * nx + 2],
            recv_sem=xrecv.at[h * nx + 2], device_id=x_next[h], device_id_type=MESH_ID)
        copy.start()
        rs_two.append(copy)
    for h in range(2):
        rs_one[h][1].wait_recv()
        rs_two[h].wait_recv()
        r, c = xblock(h, ix)
        xs[h, 2] = xs[h, 2] + xs[h, 1] + data[r, c]
    for c in rs_one[0] + rs_one[1] + rs_two:
        c.wait_send()
    last = nx - 2
    for c in chan_one:
        c.wait_recv()
    relay[...] = part[far_at] + from_pair[1]
    chan_two = pltpu.make_async_remote_copy(
        src_ref=relay, dst_ref=from_far, send_sem=csems.at[0, 2],
        recv_sem=csems.at[1, 2], device_id=far, device_id_type=MESH_ID)
    chan_two.start()
    copies = []
    for h in range(2):
        for d in range(1, nz):
            c = pltpu.make_async_remote_copy(
                src_ref=xs.at[(h, last) + zblock(iz + d)], dst_ref=zs.at[h, d - 1],
                send_sem=zsend.at[h * nz + d], recv_sem=zrecv.at[h * nz + d],
                device_id=z_peer[d], device_id_type=MESH_ID)
            c.start()
            copies.append(c)
    own = [pltpu.make_async_copy(xs.at[(h, last) + zblock(iz)], zs.at[h, nz - 1], local.at[h]) for h in range(2)]
    for c in own:
        c.start()
    for c in own:
        c.wait()
    for c in copies:
        c.wait_recv()
    for h in range(2):
        acc = zs[h, nz - 1]
        for d in range(1, nz):
            acc = acc + zs[h, d - 1]
        zs[h, nz] = acc
    for c in copies:
        c.wait_send()
    zl = nz
    c = pltpu.make_async_remote_copy(
        src_ref=zs.at[:, zl], dst_ref=ys, send_sem=ysend.at[0], recv_sem=yrecv.at[0],
        device_id=partner, device_id_type=MESH_ID)
    c.start()
    c.wait_recv()
    for h in range(2):
        fin[h] = zs[h, zl] + ys[h]
    placed = [pltpu.make_async_copy(fin.at[h], out.at[oblock(h, ix, iz)], local.at[2 + h]) for h in range(2)]
    for p in placed:
        p.start()
    for p in placed:
        p.wait()
    c.wait_send()
    copies = []
    for h in range(2):
        loc = oblock(h, ix, iz)
        for d in range(1, nz):
            c = pltpu.make_async_remote_copy(
                src_ref=out.at[loc], dst_ref=out.at[loc], send_sem=gzsend.at[h * nz + d],
                recv_sem=gzrecv.at[h * nz + d], device_id=z_peer[d], device_id_type=MESH_ID)
            c.start()
            copies.append(c)
    for c in copies:
        c.wait_recv()
    for c in copies:
        c.wait_send()
    first = [[None, None], [None, None]]
    for h in range(2):
        loc = obig(h, ix)
        for j in range(2):
            c = pltpu.make_async_remote_copy(
                src_ref=out.at[loc], dst_ref=out.at[loc], send_sem=gxsend.at[h * nx + j],
                recv_sem=gxrecv.at[h * nx + j], device_id=x_next[j], device_id_type=MESH_ID)
            c.start()
            first[h][j] = c
    second = []
    for h in range(2):
        first[h][h].wait_recv()
        loc = obig(h, ix - steps[h])
        c = pltpu.make_async_remote_copy(
            src_ref=out.at[loc], dst_ref=out.at[loc], send_sem=gxsend.at[h * nx + 2],
            recv_sem=gxrecv.at[h * nx + 2], device_id=x_next[h], device_id_type=MESH_ID)
        c.start()
        second.append(c)
    for h in range(2):
        first[h][1 - h].wait_recv()
    for c in second:
        c.wait_recv()
    for c in first[0] + first[1] + second:
        c.wait_send()

    chan_two.wait_recv()
    total = part[me] + from_pair[0] + from_far[...]
    grad_out[...] = (cot[...].astype(jnp.float32) + total).astype(grad_out.dtype)
    for c in chan_one:
        c.wait_send()
    chan_two.wait_send()

def row_group_allreduce(pieces, nx, nz, part, cot):
    cols = pieces[0].shape[-1]
    layout = []
    at = 0
    for piece in pieces:
        layout.append((at, piece.shape[0]))
        at += piece.shape[0]
    quantum = 8 * nx * (nz // 2)
    rows = -(-at // quantum) * quantum
    used = at
    count = len(pieces)
    half = cols // 2
    bx = rows // nx
    bz = bx // (nz // 2)
    sems = [pltpu.SemaphoreType.DMA((2 * nx,)), pltpu.SemaphoreType.DMA((2 * nx,)),
            pltpu.SemaphoreType.DMA((2 * nz,)), pltpu.SemaphoreType.DMA((2 * nz,)),
            pltpu.SemaphoreType.DMA((1,)), pltpu.SemaphoreType.DMA((1,)),
            pltpu.SemaphoreType.DMA((2 * nz,)), pltpu.SemaphoreType.DMA((2 * nz,)),
            pltpu.SemaphoreType.DMA((2 * nx,)), pltpu.SemaphoreType.DMA((2 * nx,)),
            pltpu.SemaphoreType.DMA((2, 3)), pltpu.SemaphoreType.DMA((4,)),
            pltpu.SemaphoreType.DMA((2 * count,))]
    block = part.shape[1:]

    def body(*refs):
        ins, outs = refs[:count], refs[count + 2 : 2 * count + 2]
        part, cot, grad_out = refs[count], refs[count + 1], refs[2 * count + 2]
        data, out, xs, zs, ys, fin, from_pair, from_far, relay = refs[2 * count + 3 : 2 * count + 12]
        s = refs[2 * count + 12 :]
        moves = s[-1]
        packs = [pltpu.make_async_copy(ref, data.at[pl.ds(at, size)], moves.at[i])
                 for i, (ref, (at, size)) in enumerate(zip(ins, layout))]
        for c in packs:
            c.start()
        data[used:] = jnp.zeros((rows - used, cols), jnp.float32)
        for c in packs:
            c.wait()
        _sum_kernel(nx, nz, data, part, cot, out, grad_out, xs, zs, ys, fin, from_pair, from_far, relay, s[:-1])
        unpacks = [pltpu.make_async_copy(out.at[pl.ds(at, size)], ref, moves.at[count + i])
                   for i, (ref, (at, size)) in enumerate(zip(outs, layout))]
        for c in unpacks:
            c.start()
        for c in unpacks:
            c.wait()

    return pl.pallas_call(
        body,
        out_shape=tuple(jax.ShapeDtypeStruct(p.shape, jnp.float32) for p in pieces)
        + (jax.ShapeDtypeStruct(cot.shape, cot.dtype),),
        in_specs=[pl.BlockSpec(memory_space=pltpu.VMEM)] * (count + 2),
        out_specs=(pl.BlockSpec(memory_space=pltpu.VMEM),) * (count + 1),
        scratch_shapes=[
            pltpu.VMEM((rows, cols), jnp.float32),
            pltpu.VMEM((rows, cols), jnp.float32),
            pltpu.VMEM((2, nx - 1, bx, half), jnp.float32),
            pltpu.VMEM((2, nz + 1, bz, half // 2), jnp.float32),
            pltpu.VMEM((2, bz, half // 2), jnp.float32),
            pltpu.VMEM((2, bz, half // 2), jnp.float32),
            pltpu.VMEM((2,) + block, jnp.float32),
            pltpu.VMEM(block, jnp.float32),
            pltpu.VMEM(block, jnp.float32),
        ] + sems,
        compiler_params=pltpu.CompilerParams(collective_id=0, has_side_effects=True,
                                             vmem_limit_bytes=48 * 1024 * 1024),
    )(*pieces, part, cot)


def _chan_gather_kernel(first, second, out_first, out_second, sems):
    coords = [lax.axis_index(a) for a in ALL_AXES]
    hi, core = coords[3], coords[4]

    def dev(h, c):
        return (coords[0], coords[1], coords[2], h, c)

    me = hi * 2 + core
    across = hi * 2 + (1 - core)
    over = (1 - hi) * 2 + core
    pair, far = dev(hi, 1 - core), dev(1 - hi, core)

    barrier = pltpu.get_barrier_semaphore()
    for d in (pair, far):
        pl.semaphore_signal(barrier, inc=1, device_id=d, device_id_type=MESH_ID)
    pl.semaphore_wait(barrier, 2)

    sources = (first, second)
    outs = (out_first, out_second)
    step_one = []
    for k in range(2):
        for j, target in enumerate((pair, far)):
            c = pltpu.make_async_remote_copy(
                src_ref=sources[k], dst_ref=outs[k].at[me], send_sem=sems.at[0, k, j],
                recv_sem=sems.at[1, k, j], device_id=target, device_id_type=MESH_ID)
            c.start()
            step_one.append(c)
    for k in range(2):
        outs[k][me] = sources[k][...]
    relay = []
    for k in range(2):
        step_one[2 * k + 1].wait_recv()
        c = pltpu.make_async_remote_copy(
            src_ref=outs[k].at[over], dst_ref=outs[k].at[over], send_sem=sems.at[0, k, 2],
            recv_sem=sems.at[1, k, 2], device_id=pair, device_id_type=MESH_ID)
        c.start()
        relay.append(c)
    for k in range(2):
        step_one[2 * k].wait_recv()
    for c in relay:
        c.wait_recv()
    for c in step_one + relay:
        c.wait_send()


def chan_gather(first, second):
    shape = (4,) + first.shape
    result = pl.pallas_call(
        _chan_gather_kernel,
        out_shape=(jax.ShapeDtypeStruct(shape, first.dtype), jax.ShapeDtypeStruct(shape, second.dtype)),
        in_specs=[pl.BlockSpec(memory_space=pltpu.VMEM)] * 2,
        out_specs=(pl.BlockSpec(memory_space=pltpu.VMEM),) * 2,
        scratch_shapes=[pltpu.SemaphoreType.DMA((2, 2, 3))],
        compiler_params=pltpu.CompilerParams(collective_id=1, has_side_effects=True),
    )(first, second)
    return tuple(r.reshape((-1,) + first.shape[1:]) for r in result)


def extended(block, sides, width):
    for axis, dim in sides:
        count = 1
        for name in axis:
            count *= lax.axis_size(name)
        forward = [(i, i + 1) for i in range(count - 1)]
        backward = [(target, source) for source, target in forward]
        low = lax.ppermute(
            lax.slice_in_dim(block, block.shape[dim] - width, None, axis=dim), axis, forward
        )
        high = lax.ppermute(lax.slice_in_dim(block, 0, width, axis=dim), axis, backward)
        block = jnp.concatenate([low, block, high], axis=dim)
    return block


def gelu_parts(pre):
    cdf = 0.5 * (1.0 + lax.erf(pre * 0.7071067811865476))
    dens = jnp.exp(-0.5 * pre * pre) * 0.3989422804014327
    return (pre * cdf, cdf + pre * dens)


def shards(inputs, cotangent, expand_w, expand_b, depth_k, depth_b, project_w):
    rows_in, rows_cot = chan_gather(inputs, cotangent)
    nrows, ncols, cin = rows_in.shape
    hslice = expand_w.shape[1]
    flat_inputs = rows_in.reshape(nrows * ncols, cin)
    flat_cotan = rows_cot.reshape(nrows * ncols, cin)
    pre_one = (
        jnp.dot(flat_inputs, expand_w, preferred_element_type=jnp.float32).reshape(
            nrows, ncols, hslice
        )
        + expand_b
    )
    hidden, slope_one = gelu_parts(pre_one)
    hidden = hidden.astype(jnp.bfloat16)
    rimmed = extended(hidden, ((ROW_AXES, 0),), 2)
    padded = jnp.pad(rimmed, ((0, 0), (2, 2), (0, 0))).astype(jnp.float32)
    pre_two = jnp.zeros((nrows, ncols, hslice), jnp.float32) + depth_b
    for row_tap in range(5):
        for col_tap in range(5):
            pre_two = (
                pre_two
                + depth_k[5 * row_tap + col_tap]
                * padded[row_tap : row_tap + nrows, col_tap : col_tap + ncols]
            )
    mixed, slope_two = gelu_parts(pre_two)
    mixed = mixed.astype(jnp.bfloat16).reshape(nrows * ncols, hslice)
    grad_w2 = jnp.dot(mixed.T, flat_cotan, preferred_element_type=jnp.float32)
    grad_mixed = jnp.dot(flat_cotan, project_w.T, preferred_element_type=jnp.float32).reshape(
        nrows, ncols, hslice
    )
    grad_pre = (grad_mixed * slope_two).astype(jnp.bfloat16)
    grad_pre_f = grad_pre.astype(jnp.float32)
    grad_bd = jnp.sum(grad_pre_f, axis=(0, 1))
    grad_rimmed = extended(grad_pre, ((ROW_AXES, 0),), 2)
    grad_pad = jnp.pad(grad_rimmed, ((0, 0), (2, 2), (0, 0))).astype(jnp.float32)
    taps = []
    grad_hidden = jnp.zeros((nrows, ncols, hslice), jnp.float32)
    for row_tap in range(5):
        for col_tap in range(5):
            taps.append(
                jnp.sum(
                    padded[row_tap : row_tap + nrows, col_tap : col_tap + ncols] * grad_pre_f,
                    axis=(0, 1),
                )
            )
            grad_hidden = (
                grad_hidden
                + depth_k[5 * row_tap + col_tap]
                * grad_pad[4 - row_tap : 4 - row_tap + nrows, 4 - col_tap : 4 - col_tap + ncols]
            )
    grad_k = jnp.stack(taps, axis=0)
    grad_act = (grad_hidden * slope_one).astype(jnp.bfloat16)
    flat_act = grad_act.reshape(nrows * ncols, hslice)
    grad_b1 = jnp.sum(flat_act.astype(jnp.float32), axis=0)
    grad_w1 = jnp.dot(flat_inputs.T, flat_act, preferred_element_type=jnp.float32)
    part = jnp.einsum("rwh,ch->rwc", grad_act, expand_w, preferred_element_type=jnp.float32)
    part = part.reshape((4, -1) + part.shape[1:])
    small = jnp.concatenate([grad_k, grad_b1[None], grad_bd[None]], axis=0)
    taps_count = grad_k.shape[0]
    small = jnp.pad(small, ((0, -small.shape[0] % 8), (0, 0)))
    nx, nz = lax.axis_size("x"), lax.axis_size("z")
    w1, w2, small, input_grad = row_group_allreduce([grad_w1, grad_w2, small], nx, nz, part, cotangent)
    summed = [w1, small[taps_count], small[:taps_count], small[taps_count + 1], w2]
    return (input_grad, summed[0], summed[1], summed[2], summed[3], summed[4])


def solution(mesh):
    fine = Mesh(mesh.devices.reshape(2, 8, 4, 2, 2), ROW_AXES + CHAN_AXES)
    rows = ROW_AXES + CHAN_AXES
    in_specs = (
        P(rows, None, None),
        P(rows, None, None),
        P(None, CHAN_AXES),
        P(CHAN_AXES),
        P(None, CHAN_AXES),
        P(CHAN_AXES),
        P(CHAN_AXES, None),
    )
    out_specs = (
        P(rows, None, None),
        P(None, CHAN_AXES),
        P(CHAN_AXES),
        P(None, CHAN_AXES),
        P(CHAN_AXES),
        P(CHAN_AXES, None),
    )
    return jax.shard_map(shards, mesh=fine, in_specs=in_specs, out_specs=out_specs, check_vma=False)
```

```python
import jax
import jax.numpy as jnp
from jax import lax
from jax.experimental import pallas as pl
from jax.experimental.pallas import tpu as pltpu
from jax.sharding import Mesh, PartitionSpec as P

MESH_ID = pl.DeviceIdType.MESH
ALL_AXES = ("y_lo", "z", "x", "y_hi", "core")
ROW_AXES = ("y_lo", "z", "x")
CHAN_AXES = ("y_hi", "core")


def _sum_kernel(nx, nz, data, part, cot, out, grad_out, xs, zs, ys, fin, from_pair, from_far, relay, sems):
    (xsend, xrecv, zsend, zrecv, ysend, yrecv, gzsend, gzrecv, gxsend, gxrecv, csems, local) = sems
    coords = [lax.axis_index(a) for a in ALL_AXES]
    iy, iz, ix = coords[0], coords[1], coords[2]
    hi, core = coords[3], coords[4]
    me = hi * 2 + core
    pair_at = hi * 2 + (1 - core)
    far_at = (1 - hi) * 2 + core
    diag_at = (1 - hi) * 2 + (1 - core)
    pair = (iy, iz, ix, hi, 1 - core)
    far = (iy, iz, ix, 1 - hi, core)

    def dev(y=None, z=None, x=None):
        c = list(coords)
        if y is not None:
            c[0] = y
        if z is not None:
            c[1] = z
        if x is not None:
            c[2] = x
        return tuple(c)

    x_next = [dev(x=lax.rem(ix + 1, nx)), dev(x=lax.rem(ix + nx - 1, nx))]
    z_next = [dev(z=lax.rem(iz + 1, nz)), dev(z=lax.rem(iz + nz - 1, nz))]
    partner = dev(y=1 - iy)

    barrier = pltpu.get_barrier_semaphore()
    z_peer = [None] + [dev(z=lax.rem(iz + d, nz)) for d in range(1, nz)]
    peers = [x_next[0], x_next[1], partner, pair, far] + z_peer[1:]
    if nx == 2:
        peers = peers[1:]
    for d in peers:
        pl.semaphore_signal(barrier, inc=1, device_id=d, device_id_type=MESH_ID)
    pl.semaphore_wait(barrier, len(peers))

    chan_one = []
    for j, src in enumerate((part.at[pair_at], part.at[diag_at])):
        c = pltpu.make_async_remote_copy(
            src_ref=src, dst_ref=from_pair.at[j], send_sem=csems.at[0, j],
            recv_sem=csems.at[1, j], device_id=pair, device_id_type=MESH_ID)
        c.start()
        chan_one.append(c)

    rows, cols = data.shape
    half = cols // 2
    bx = rows // nx
    bz = bx // (nz // 2)
    lanes = half // 2
    steps = (1, -1)

    def xblock(h, k):
        return (pl.ds(pl.multiple_of(lax.rem(k + 4 * nx, nx) * bx, 8), bx), pl.ds(h * half, half))

    def zblock(k):
        k = lax.rem(k + 4 * nz, nz)
        return (pl.ds(pl.multiple_of((k // 2) * bz, 8), bz), pl.ds(pl.multiple_of(lax.rem(k, 2) * lanes, 128), lanes))

    def oblock(h, kx, kz):
        r, c = zblock(kz)
        start = pl.multiple_of(lax.rem(kx + 4 * nx, nx) * bx + r.start, 8)
        return (pl.ds(start, bz), pl.ds(pl.multiple_of(h * half + c.start, 128), lanes))

    def obig(h, kx):
        return xblock(h, kx)

    for s in range(nx - 1):
        copies = []
        for h in range(2):
            sg = steps[h]
            src = data.at[xblock(h, ix - sg)] if s == 0 else xs.at[h, s - 1]
            c = pltpu.make_async_remote_copy(
                src_ref=src, dst_ref=xs.at[h, s], send_sem=xsend.at[h * nx + s],
                recv_sem=xrecv.at[h * nx + s], device_id=x_next[h], device_id_type=MESH_ID)
            c.start()
            copies.append(c)
        for h in range(2):
            sg = steps[h]
            copies[h].wait_recv()
            r, c = xblock(h, ix - sg * (s + 2))
            xs[h, s] = xs[h, s] + data[r, c]
            copies[h].wait_send()
    last = nx - 2
    for c in chan_one:
        c.wait_recv()
    relay[...] = part[far_at] + from_pair[1]
    chan_two = pltpu.make_async_remote_copy(
        src_ref=relay, dst_ref=from_far, send_sem=csems.at[0, 2],
        recv_sem=csems.at[1, 2], device_id=far, device_id_type=MESH_ID)
    chan_two.start()
    copies = []
    for h in range(2):
        for d in range(1, nz):
            c = pltpu.make_async_remote_copy(
                src_ref=xs.at[(h, last) + zblock(iz + d)], dst_ref=zs.at[h, d - 1],
                send_sem=zsend.at[h * nz + d], recv_sem=zrecv.at[h * nz + d],
                device_id=z_peer[d], device_id_type=MESH_ID)
            c.start()
            copies.append(c)
    own = [pltpu.make_async_copy(xs.at[(h, last) + zblock(iz)], zs.at[h, nz - 1], local.at[h]) for h in range(2)]
    for c in own:
        c.start()
    for c in own:
        c.wait()
    for c in copies:
        c.wait_recv()
    for h in range(2):
        acc = zs[h, nz - 1]
        for d in range(1, nz):
            acc = acc + zs[h, d - 1]
        zs[h, nz] = acc
    for c in copies:
        c.wait_send()
    zl = nz
    chan_two.wait_recv()
    total = part[me] + from_pair[0] + from_far[...]
    grad_out[...] = (cot[...].astype(jnp.float32) + total).astype(grad_out.dtype)
    c = pltpu.make_async_remote_copy(
        src_ref=zs.at[:, zl], dst_ref=ys, send_sem=ysend.at[0], recv_sem=yrecv.at[0],
        device_id=partner, device_id_type=MESH_ID)
    c.start()
    c.wait_recv()
    for h in range(2):
        fin[h] = zs[h, zl] + ys[h]
    placed = [pltpu.make_async_copy(fin.at[h], out.at[oblock(h, ix, iz)], local.at[2 + h]) for h in range(2)]
    for p in placed:
        p.start()
    for p in placed:
        p.wait()
    c.wait_send()
    copies = []
    for h in range(2):
        loc = oblock(h, ix, iz)
        for d in range(1, nz):
            c = pltpu.make_async_remote_copy(
                src_ref=out.at[loc], dst_ref=out.at[loc], send_sem=gzsend.at[h * nz + d],
                recv_sem=gzrecv.at[h * nz + d], device_id=z_peer[d], device_id_type=MESH_ID)
            c.start()
            copies.append(c)
    for c in copies:
        c.wait_recv()
    for c in copies:
        c.wait_send()
    first = [[None, None], [None, None]]
    for h in range(2):
        loc = obig(h, ix)
        for j in range(2):
            c = pltpu.make_async_remote_copy(
                src_ref=out.at[loc], dst_ref=out.at[loc], send_sem=gxsend.at[h * nx + j],
                recv_sem=gxrecv.at[h * nx + j], device_id=x_next[j], device_id_type=MESH_ID)
            c.start()
            first[h][j] = c
    second = []
    for h in range(2):
        first[h][h].wait_recv()
        loc = obig(h, ix - steps[h])
        c = pltpu.make_async_remote_copy(
            src_ref=out.at[loc], dst_ref=out.at[loc], send_sem=gxsend.at[h * nx + 2],
            recv_sem=gxrecv.at[h * nx + 2], device_id=x_next[h], device_id_type=MESH_ID)
        c.start()
        second.append(c)
    for h in range(2):
        first[h][1 - h].wait_recv()
    for c in second:
        c.wait_recv()
    for c in first[0] + first[1] + second:
        c.wait_send()

    for c in chan_one:
        c.wait_send()
    chan_two.wait_send()

def row_group_allreduce(pieces, nx, nz, part, cot):
    cols = pieces[0].shape[-1]
    layout = []
    at = 0
    for piece in pieces:
        layout.append((at, piece.shape[0]))
        at += piece.shape[0]
    quantum = 8 * nx * (nz // 2)
    rows = -(-at // quantum) * quantum
    used = at
    count = len(pieces)
    half = cols // 2
    bx = rows // nx
    bz = bx // (nz // 2)
    sems = [pltpu.SemaphoreType.DMA((2 * nx,)), pltpu.SemaphoreType.DMA((2 * nx,)),
            pltpu.SemaphoreType.DMA((2 * nz,)), pltpu.SemaphoreType.DMA((2 * nz,)),
            pltpu.SemaphoreType.DMA((1,)), pltpu.SemaphoreType.DMA((1,)),
            pltpu.SemaphoreType.DMA((2 * nz,)), pltpu.SemaphoreType.DMA((2 * nz,)),
            pltpu.SemaphoreType.DMA((2 * nx,)), pltpu.SemaphoreType.DMA((2 * nx,)),
            pltpu.SemaphoreType.DMA((2, 3)), pltpu.SemaphoreType.DMA((4,)),
            pltpu.SemaphoreType.DMA((2 * count,))]
    block = part.shape[1:]

    def body(*refs):
        ins, outs = refs[:count], refs[count + 2 : 2 * count + 2]
        part, cot, grad_out = refs[count], refs[count + 1], refs[2 * count + 2]
        data, out, xs, zs, ys, fin, from_pair, from_far, relay = refs[2 * count + 3 : 2 * count + 12]
        s = refs[2 * count + 12 :]
        moves = s[-1]
        packs = [pltpu.make_async_copy(ref, data.at[pl.ds(at, size)], moves.at[i])
                 for i, (ref, (at, size)) in enumerate(zip(ins, layout))]
        for c in packs:
            c.start()
        data[used:] = jnp.zeros((rows - used, cols), jnp.float32)
        for c in packs:
            c.wait()
        _sum_kernel(nx, nz, data, part, cot, out, grad_out, xs, zs, ys, fin, from_pair, from_far, relay, s[:-1])
        unpacks = [pltpu.make_async_copy(out.at[pl.ds(at, size)], ref, moves.at[count + i])
                   for i, (ref, (at, size)) in enumerate(zip(outs, layout))]
        for c in unpacks:
            c.start()
        for c in unpacks:
            c.wait()

    return pl.pallas_call(
        body,
        out_shape=tuple(jax.ShapeDtypeStruct(p.shape, jnp.float32) for p in pieces)
        + (jax.ShapeDtypeStruct(cot.shape, cot.dtype),),
        in_specs=[pl.BlockSpec(memory_space=pltpu.VMEM)] * (count + 2),
        out_specs=(pl.BlockSpec(memory_space=pltpu.VMEM),) * (count + 1),
        scratch_shapes=[
            pltpu.VMEM((rows, cols), jnp.float32),
            pltpu.VMEM((rows, cols), jnp.float32),
            pltpu.VMEM((2, nx - 1, bx, half), jnp.float32),
            pltpu.VMEM((2, nz + 1, bz, half // 2), jnp.float32),
            pltpu.VMEM((2, bz, half // 2), jnp.float32),
            pltpu.VMEM((2, bz, half // 2), jnp.float32),
            pltpu.VMEM((2,) + block, jnp.float32),
            pltpu.VMEM(block, jnp.float32),
            pltpu.VMEM(block, jnp.float32),
        ] + sems,
        compiler_params=pltpu.CompilerParams(collective_id=0, has_side_effects=True,
                                             vmem_limit_bytes=48 * 1024 * 1024),
    )(*pieces, part, cot)


def _chan_gather_kernel(first, second, out_first, out_second, sems):
    coords = [lax.axis_index(a) for a in ALL_AXES]
    hi, core = coords[3], coords[4]

    def dev(h, c):
        return (coords[0], coords[1], coords[2], h, c)

    me = hi * 2 + core
    across = hi * 2 + (1 - core)
    over = (1 - hi) * 2 + core
    pair, far = dev(hi, 1 - core), dev(1 - hi, core)

    barrier = pltpu.get_barrier_semaphore()
    for d in (pair, far):
        pl.semaphore_signal(barrier, inc=1, device_id=d, device_id_type=MESH_ID)
    pl.semaphore_wait(barrier, 2)

    sources = (first, second)
    outs = (out_first, out_second)
    step_one = []
    for k in range(2):
        for j, target in enumerate((pair, far)):
            c = pltpu.make_async_remote_copy(
                src_ref=sources[k], dst_ref=outs[k].at[me], send_sem=sems.at[0, k, j],
                recv_sem=sems.at[1, k, j], device_id=target, device_id_type=MESH_ID)
            c.start()
            step_one.append(c)
    for k in range(2):
        outs[k][me] = sources[k][...]
    relay = []
    for k in range(2):
        step_one[2 * k + 1].wait_recv()
        c = pltpu.make_async_remote_copy(
            src_ref=outs[k].at[over], dst_ref=outs[k].at[over], send_sem=sems.at[0, k, 2],
            recv_sem=sems.at[1, k, 2], device_id=pair, device_id_type=MESH_ID)
        c.start()
        relay.append(c)
    for k in range(2):
        step_one[2 * k].wait_recv()
    for c in relay:
        c.wait_recv()
    for c in step_one + relay:
        c.wait_send()


def chan_gather(first, second):
    shape = (4,) + first.shape
    result = pl.pallas_call(
        _chan_gather_kernel,
        out_shape=(jax.ShapeDtypeStruct(shape, first.dtype), jax.ShapeDtypeStruct(shape, second.dtype)),
        in_specs=[pl.BlockSpec(memory_space=pltpu.VMEM)] * 2,
        out_specs=(pl.BlockSpec(memory_space=pltpu.VMEM),) * 2,
        scratch_shapes=[pltpu.SemaphoreType.DMA((2, 2, 3))],
        compiler_params=pltpu.CompilerParams(collective_id=1, has_side_effects=True),
    )(first, second)
    return tuple(r.reshape((-1,) + first.shape[1:]) for r in result)


def extended(block, sides, width):
    for axis, dim in sides:
        count = 1
        for name in axis:
            count *= lax.axis_size(name)
        forward = [(i, i + 1) for i in range(count - 1)]
        backward = [(target, source) for source, target in forward]
        low = lax.ppermute(
            lax.slice_in_dim(block, block.shape[dim] - width, None, axis=dim), axis, forward
        )
        high = lax.ppermute(lax.slice_in_dim(block, 0, width, axis=dim), axis, backward)
        block = jnp.concatenate([low, block, high], axis=dim)
    return block


def gelu_parts(pre):
    cdf = 0.5 * (1.0 + lax.erf(pre * 0.7071067811865476))
    dens = jnp.exp(-0.5 * pre * pre) * 0.3989422804014327
    return (pre * cdf, cdf + pre * dens)


def shards(inputs, cotangent, expand_w, expand_b, depth_k, depth_b, project_w):
    rows_in, rows_cot = chan_gather(inputs, cotangent)
    nrows, ncols, cin = rows_in.shape
    hslice = expand_w.shape[1]
    flat_inputs = rows_in.reshape(nrows * ncols, cin)
    flat_cotan = rows_cot.reshape(nrows * ncols, cin)
    pre_one = (
        jnp.dot(flat_inputs, expand_w, preferred_element_type=jnp.float32).reshape(
            nrows, ncols, hslice
        )
        + expand_b
    )
    hidden, slope_one = gelu_parts(pre_one)
    hidden = hidden.astype(jnp.bfloat16)
    rimmed = extended(hidden, ((ROW_AXES, 0),), 2)
    padded = jnp.pad(rimmed, ((0, 0), (2, 2), (0, 0))).astype(jnp.float32)
    pre_two = jnp.zeros((nrows, ncols, hslice), jnp.float32) + depth_b
    for row_tap in range(5):
        for col_tap in range(5):
            pre_two = (
                pre_two
                + depth_k[5 * row_tap + col_tap]
                * padded[row_tap : row_tap + nrows, col_tap : col_tap + ncols]
            )
    mixed, slope_two = gelu_parts(pre_two)
    mixed = mixed.astype(jnp.bfloat16).reshape(nrows * ncols, hslice)
    grad_w2 = jnp.dot(mixed.T, flat_cotan, preferred_element_type=jnp.float32)
    grad_mixed = jnp.dot(flat_cotan, project_w.T, preferred_element_type=jnp.float32).reshape(
        nrows, ncols, hslice
    )
    grad_pre = (grad_mixed * slope_two).astype(jnp.bfloat16)
    grad_pre_f = grad_pre.astype(jnp.float32)
    grad_bd = jnp.sum(grad_pre_f, axis=(0, 1))
    grad_rimmed = extended(grad_pre, ((ROW_AXES, 0),), 2)
    grad_pad = jnp.pad(grad_rimmed, ((0, 0), (2, 2), (0, 0))).astype(jnp.float32)
    taps = []
    grad_hidden = jnp.zeros((nrows, ncols, hslice), jnp.float32)
    for row_tap in range(5):
        for col_tap in range(5):
            taps.append(
                jnp.sum(
                    padded[row_tap : row_tap + nrows, col_tap : col_tap + ncols] * grad_pre_f,
                    axis=(0, 1),
                )
            )
            grad_hidden = (
                grad_hidden
                + depth_k[5 * row_tap + col_tap]
                * grad_pad[4 - row_tap : 4 - row_tap + nrows, 4 - col_tap : 4 - col_tap + ncols]
            )
    grad_k = jnp.stack(taps, axis=0)
    grad_act = (grad_hidden * slope_one).astype(jnp.bfloat16)
    flat_act = grad_act.reshape(nrows * ncols, hslice)
    grad_b1 = jnp.sum(flat_act.astype(jnp.float32), axis=0)
    grad_w1 = jnp.dot(flat_inputs.T, flat_act, preferred_element_type=jnp.float32)
    part = jnp.einsum("rwh,ch->rwc", grad_act, expand_w, preferred_element_type=jnp.float32)
    part = part.reshape((4, -1) + part.shape[1:])
    small = jnp.concatenate([grad_k, grad_b1[None], grad_bd[None]], axis=0)
    taps_count = grad_k.shape[0]
    small = jnp.pad(small, ((0, -small.shape[0] % 8), (0, 0)))
    nx, nz = lax.axis_size("x"), lax.axis_size("z")
    w1, w2, small, input_grad = row_group_allreduce([grad_w1, grad_w2, small], nx, nz, part, cotangent)
    summed = [w1, small[taps_count], small[:taps_count], small[taps_count + 1], w2]
    return (input_grad, summed[0], summed[1], summed[2], summed[3], summed[4])


def solution(mesh):
    fine = Mesh(mesh.devices.reshape(2, 8, 4, 2, 2), ROW_AXES + CHAN_AXES)
    rows = ROW_AXES + CHAN_AXES
    in_specs = (
        P(rows, None, None),
        P(rows, None, None),
        P(None, CHAN_AXES),
        P(CHAN_AXES),
        P(None, CHAN_AXES),
        P(CHAN_AXES),
        P(CHAN_AXES, None),
    )
    out_specs = (
        P(rows, None, None),
        P(None, CHAN_AXES),
        P(CHAN_AXES),
        P(None, CHAN_AXES),
        P(CHAN_AXES),
        P(CHAN_AXES, None),
    )
    return jax.shard_map(shards, mesh=fine, in_specs=in_specs, out_specs=out_specs, check_vma=False)
```

```python
import jax
import jax.numpy as jnp
from jax import lax
from jax.experimental import pallas as pl
from jax.experimental.pallas import tpu as pltpu
from jax.sharding import Mesh, PartitionSpec as P

MESH_ID = pl.DeviceIdType.MESH
ALL_AXES = ("y_lo", "z", "x", "y_hi", "core")
ROW_AXES = ("y_lo", "z", "x")
CHAN_AXES = ("y_hi", "core")


def _sum_kernel(nx, nz, data, part, cot, out, grad_out, xs, zs, ys, fin, from_pair, from_far, relay, sems):
    (xsend, xrecv, zsend, zrecv, ysend, yrecv, gzsend, gzrecv, gxsend, gxrecv, csems, local) = sems
    coords = [lax.axis_index(a) for a in ALL_AXES]
    iy, iz, ix = coords[0], coords[1], coords[2]
    hi, core = coords[3], coords[4]
    me = hi * 2 + core
    pair_at = hi * 2 + (1 - core)
    far_at = (1 - hi) * 2 + core
    diag_at = (1 - hi) * 2 + (1 - core)
    pair = (iy, iz, ix, hi, 1 - core)
    far = (iy, iz, ix, 1 - hi, core)

    def dev(y=None, z=None, x=None):
        c = list(coords)
        if y is not None:
            c[0] = y
        if z is not None:
            c[1] = z
        if x is not None:
            c[2] = x
        return tuple(c)

    x_next = [dev(x=lax.rem(ix + 1, nx)), dev(x=lax.rem(ix + nx - 1, nx))]
    z_next = [dev(z=lax.rem(iz + 1, nz)), dev(z=lax.rem(iz + nz - 1, nz))]
    partner = dev(y=1 - iy)

    barrier = pltpu.get_barrier_semaphore()
    z_peer = [None] + [dev(z=lax.rem(iz + d, nz)) for d in range(1, nz)]
    peers = [x_next[0], x_next[1], partner, pair, far] + z_peer[1:]
    if nx == 2:
        peers = peers[1:]
    for d in peers:
        pl.semaphore_signal(barrier, inc=1, device_id=d, device_id_type=MESH_ID)
    pl.semaphore_wait(barrier, len(peers))

    chan_one = []
    for j, src in enumerate((part.at[pair_at], part.at[diag_at])):
        c = pltpu.make_async_remote_copy(
            src_ref=src, dst_ref=from_pair.at[j], send_sem=csems.at[0, j],
            recv_sem=csems.at[1, j], device_id=pair, device_id_type=MESH_ID)
        c.start()
        chan_one.append(c)

    rows, cols = data.shape
    half = cols // 2
    bx = rows // nx
    bz = bx // (nz // 2)
    lanes = half // 2
    steps = (1, -1)

    def xblock(h, k):
        return (pl.ds(pl.multiple_of(lax.rem(k + 4 * nx, nx) * bx, 8), bx), pl.ds(h * half, half))

    def zblock(k):
        k = lax.rem(k + 4 * nz, nz)
        return (pl.ds(pl.multiple_of((k // 2) * bz, 8), bz), pl.ds(pl.multiple_of(lax.rem(k, 2) * lanes, 128), lanes))

    def oblock(h, kx, kz):
        r, c = zblock(kz)
        start = pl.multiple_of(lax.rem(kx + 4 * nx, nx) * bx + r.start, 8)
        return (pl.ds(start, bz), pl.ds(pl.multiple_of(h * half + c.start, 128), lanes))

    def obig(h, kx):
        return xblock(h, kx)

    for s in range(nx - 1):
        copies = []
        for h in range(2):
            sg = steps[h]
            src = data.at[xblock(h, ix - sg)] if s == 0 else xs.at[h, s - 1]
            c = pltpu.make_async_remote_copy(
                src_ref=src, dst_ref=xs.at[h, s], send_sem=xsend.at[h * nx + s],
                recv_sem=xrecv.at[h * nx + s], device_id=x_next[h], device_id_type=MESH_ID)
            c.start()
            copies.append(c)
        for h in range(2):
            sg = steps[h]
            copies[h].wait_recv()
            r, c = xblock(h, ix - sg * (s + 2))
            xs[h, s] = xs[h, s] + data[r, c]
            copies[h].wait_send()
    last = nx - 2
    for c in chan_one:
        c.wait_recv()
    relay[...] = part[far_at] + from_pair[1]
    chan_two = pltpu.make_async_remote_copy(
        src_ref=relay, dst_ref=from_far, send_sem=csems.at[0, 2],
        recv_sem=csems.at[1, 2], device_id=far, device_id_type=MESH_ID)
    chan_two.start()
    copies = []
    for h in range(2):
        for d in range(1, nz):
            c = pltpu.make_async_remote_copy(
                src_ref=xs.at[(h, last) + zblock(iz + d)], dst_ref=zs.at[h, d - 1],
                send_sem=zsend.at[h * nz + d], recv_sem=zrecv.at[h * nz + d],
                device_id=z_peer[d], device_id_type=MESH_ID)
            c.start()
            copies.append(c)
    own = [pltpu.make_async_copy(xs.at[(h, last) + zblock(iz)], zs.at[h, nz - 1], local.at[h]) for h in range(2)]
    for c in own:
        c.start()
    for c in own:
        c.wait()
    for c in copies:
        c.wait_recv()
    for h in range(2):
        acc = zs[h, nz - 1]
        for d in range(1, nz):
            acc = acc + zs[h, d - 1]
        zs[h, nz] = acc
    for c in copies:
        c.wait_send()
    zl = nz
    chan_two.wait_recv()
    total = part[me] + from_pair[0] + from_far[...]
    grad_out[...] = (cot[...].astype(jnp.float32) + total).astype(grad_out.dtype)
    c = pltpu.make_async_remote_copy(
        src_ref=zs.at[:, zl], dst_ref=ys, send_sem=ysend.at[0], recv_sem=yrecv.at[0],
        device_id=partner, device_id_type=MESH_ID)
    c.start()
    c.wait_recv()
    for h in range(2):
        fin[h] = zs[h, zl] + ys[h]
    placed = [pltpu.make_async_copy(fin.at[h], out.at[oblock(h, ix, iz)], local.at[2 + h]) for h in range(2)]
    for p in placed:
        p.start()
    for p in placed:
        p.wait()
    c.wait_send()
    copies = []
    for h in range(2):
        loc = oblock(h, ix, iz)
        for d in range(1, nz):
            c = pltpu.make_async_remote_copy(
                src_ref=out.at[loc], dst_ref=out.at[loc], send_sem=gzsend.at[h * nz + d],
                recv_sem=gzrecv.at[h * nz + d], device_id=z_peer[d], device_id_type=MESH_ID)
            c.start()
            copies.append(c)
    for c in copies:
        c.wait_recv()
    for c in copies:
        c.wait_send()
    first = [[None, None], [None, None]]
    for h in range(2):
        loc = obig(h, ix)
        for j in range(2):
            c = pltpu.make_async_remote_copy(
                src_ref=out.at[loc], dst_ref=out.at[loc], send_sem=gxsend.at[h * nx + j],
                recv_sem=gxrecv.at[h * nx + j], device_id=x_next[j], device_id_type=MESH_ID)
            c.start()
            first[h][j] = c
    second = []
    for h in range(2):
        first[h][h].wait_recv()
        loc = obig(h, ix - steps[h])
        c = pltpu.make_async_remote_copy(
            src_ref=out.at[loc], dst_ref=out.at[loc], send_sem=gxsend.at[h * nx + 2],
            recv_sem=gxrecv.at[h * nx + 2], device_id=x_next[h], device_id_type=MESH_ID)
        c.start()
        second.append(c)
    for h in range(2):
        first[h][1 - h].wait_recv()
    for c in second:
        c.wait_recv()
    for c in first[0] + first[1] + second:
        c.wait_send()

    for c in chan_one:
        c.wait_send()
    chan_two.wait_send()

def row_group_allreduce(pieces, nx, nz, part, cot):
    cols = pieces[0].shape[-1]
    layout = []
    at = 0
    for piece in pieces:
        layout.append((at, piece.shape[0]))
        at += piece.shape[0]
    quantum = 8 * nx * (nz // 2)
    rows = -(-at // quantum) * quantum
    used = at
    count = len(pieces)
    half = cols // 2
    bx = rows // nx
    bz = bx // (nz // 2)
    sems = [pltpu.SemaphoreType.DMA((2 * nx,)), pltpu.SemaphoreType.DMA((2 * nx,)),
            pltpu.SemaphoreType.DMA((2 * nz,)), pltpu.SemaphoreType.DMA((2 * nz,)),
            pltpu.SemaphoreType.DMA((1,)), pltpu.SemaphoreType.DMA((1,)),
            pltpu.SemaphoreType.DMA((2 * nz,)), pltpu.SemaphoreType.DMA((2 * nz,)),
            pltpu.SemaphoreType.DMA((2 * nx,)), pltpu.SemaphoreType.DMA((2 * nx,)),
            pltpu.SemaphoreType.DMA((2, 3)), pltpu.SemaphoreType.DMA((4,)),
            pltpu.SemaphoreType.DMA((2 * count,))]
    block = part.shape[1:]

    def body(*refs):
        ins, outs = refs[:count], refs[count + 2 : 2 * count + 2]
        part, cot, grad_out = refs[count], refs[count + 1], refs[2 * count + 2]
        data, out, xs, zs, ys, fin, from_pair, from_far, relay = refs[2 * count + 3 : 2 * count + 12]
        s = refs[2 * count + 12 :]
        moves = s[-1]
        packs = [pltpu.make_async_copy(ref, data.at[pl.ds(at, size)], moves.at[i])
                 for i, (ref, (at, size)) in enumerate(zip(ins, layout))]
        for c in packs:
            c.start()
        data[used:] = jnp.zeros((rows - used, cols), jnp.float32)
        for c in packs:
            c.wait()
        _sum_kernel(nx, nz, data, part, cot, out, grad_out, xs, zs, ys, fin, from_pair, from_far, relay, s[:-1])
        unpacks = [pltpu.make_async_copy(out.at[pl.ds(at, size)], ref, moves.at[count + i])
                   for i, (ref, (at, size)) in enumerate(zip(outs, layout))]
        for c in unpacks:
            c.start()
        for c in unpacks:
            c.wait()

    return pl.pallas_call(
        body,
        out_shape=tuple(jax.ShapeDtypeStruct(p.shape, jnp.float32) for p in pieces)
        + (jax.ShapeDtypeStruct(cot.shape, cot.dtype),),
        in_specs=[pl.BlockSpec(memory_space=pltpu.VMEM)] * (count + 2),
        out_specs=(pl.BlockSpec(memory_space=pltpu.VMEM),) * (count + 1),
        scratch_shapes=[
            pltpu.VMEM((rows, cols), jnp.float32),
            pltpu.VMEM((rows, cols), jnp.float32),
            pltpu.VMEM((2, nx - 1, bx, half), jnp.float32),
            pltpu.VMEM((2, nz + 1, bz, half // 2), jnp.float32),
            pltpu.VMEM((2, bz, half // 2), jnp.float32),
            pltpu.VMEM((2, bz, half // 2), jnp.float32),
            pltpu.VMEM((2,) + block, jnp.float32),
            pltpu.VMEM(block, jnp.float32),
            pltpu.VMEM(block, jnp.float32),
        ] + sems,
        compiler_params=pltpu.CompilerParams(collective_id=0, has_side_effects=True,
                                             vmem_limit_bytes=48 * 1024 * 1024),
    )(*pieces, part, cot)


def _chan_gather_kernel(first, second, out_first, out_second, sems):
    coords = [lax.axis_index(a) for a in ALL_AXES]
    hi, core = coords[3], coords[4]

    def dev(h, c):
        return (coords[0], coords[1], coords[2], h, c)

    me = hi * 2 + core
    across = hi * 2 + (1 - core)
    over = (1 - hi) * 2 + core
    pair, far = dev(hi, 1 - core), dev(1 - hi, core)

    barrier = pltpu.get_barrier_semaphore()
    for d in (pair, far):
        pl.semaphore_signal(barrier, inc=1, device_id=d, device_id_type=MESH_ID)
    pl.semaphore_wait(barrier, 2)

    sources = (first, second)
    outs = (out_first, out_second)
    step_one = [None] * 4
    for j, target in ((1, far), (0, pair)):
        for k in range(2):
            c = pltpu.make_async_remote_copy(
                src_ref=sources[k], dst_ref=outs[k].at[me], send_sem=sems.at[0, k, j],
                recv_sem=sems.at[1, k, j], device_id=target, device_id_type=MESH_ID)
            c.start()
            step_one[2 * k + j] = c
    for k in range(2):
        outs[k][me] = sources[k][...]
    relay = []
    for k in range(2):
        step_one[2 * k + 1].wait_recv()
        c = pltpu.make_async_remote_copy(
            src_ref=outs[k].at[over], dst_ref=outs[k].at[over], send_sem=sems.at[0, k, 2],
            recv_sem=sems.at[1, k, 2], device_id=pair, device_id_type=MESH_ID)
        c.start()
        relay.append(c)
    for k in range(2):
        step_one[2 * k].wait_recv()
    for c in relay:
        c.wait_recv()
    for c in step_one + relay:
        c.wait_send()


def chan_gather(first, second):
    shape = (4,) + first.shape
    result = pl.pallas_call(
        _chan_gather_kernel,
        out_shape=(jax.ShapeDtypeStruct(shape, first.dtype), jax.ShapeDtypeStruct(shape, second.dtype)),
        in_specs=[pl.BlockSpec(memory_space=pltpu.VMEM)] * 2,
        out_specs=(pl.BlockSpec(memory_space=pltpu.VMEM),) * 2,
        scratch_shapes=[pltpu.SemaphoreType.DMA((2, 2, 3))],
        compiler_params=pltpu.CompilerParams(collective_id=1, has_side_effects=True),
    )(first, second)
    return tuple(r.reshape((-1,) + first.shape[1:]) for r in result)


def extended(block, sides, width):
    for axis, dim in sides:
        count = 1
        for name in axis:
            count *= lax.axis_size(name)
        forward = [(i, i + 1) for i in range(count - 1)]
        backward = [(target, source) for source, target in forward]
        low = lax.ppermute(
            lax.slice_in_dim(block, block.shape[dim] - width, None, axis=dim), axis, forward
        )
        high = lax.ppermute(lax.slice_in_dim(block, 0, width, axis=dim), axis, backward)
        block = jnp.concatenate([low, block, high], axis=dim)
    return block


def gelu_parts(pre):
    cdf = 0.5 * (1.0 + lax.erf(pre * 0.7071067811865476))
    dens = jnp.exp(-0.5 * pre * pre) * 0.3989422804014327
    return (pre * cdf, cdf + pre * dens)


def shards(inputs, cotangent, expand_w, expand_b, depth_k, depth_b, project_w):
    rows_in, rows_cot = chan_gather(inputs, cotangent)
    nrows, ncols, cin = rows_in.shape
    hslice = expand_w.shape[1]
    flat_inputs = rows_in.reshape(nrows * ncols, cin)
    flat_cotan = rows_cot.reshape(nrows * ncols, cin)
    pre_one = (
        jnp.dot(flat_inputs, expand_w, preferred_element_type=jnp.float32).reshape(
            nrows, ncols, hslice
        )
        + expand_b
    )
    hidden, slope_one = gelu_parts(pre_one)
    hidden = hidden.astype(jnp.bfloat16)
    rimmed = extended(hidden, ((ROW_AXES, 0),), 2)
    padded = jnp.pad(rimmed, ((0, 0), (2, 2), (0, 0))).astype(jnp.float32)
    pre_two = jnp.zeros((nrows, ncols, hslice), jnp.float32) + depth_b
    for row_tap in range(5):
        for col_tap in range(5):
            pre_two = (
                pre_two
                + depth_k[5 * row_tap + col_tap]
                * padded[row_tap : row_tap + nrows, col_tap : col_tap + ncols]
            )
    mixed, slope_two = gelu_parts(pre_two)
    mixed = mixed.astype(jnp.bfloat16).reshape(nrows * ncols, hslice)
    grad_w2 = jnp.dot(mixed.T, flat_cotan, preferred_element_type=jnp.float32)
    grad_mixed = jnp.dot(flat_cotan, project_w.T, preferred_element_type=jnp.float32).reshape(
        nrows, ncols, hslice
    )
    grad_pre = (grad_mixed * slope_two).astype(jnp.bfloat16)
    grad_pre_f = grad_pre.astype(jnp.float32)
    grad_bd = jnp.sum(grad_pre_f, axis=(0, 1))
    grad_rimmed = extended(grad_pre, ((ROW_AXES, 0),), 2)
    grad_pad = jnp.pad(grad_rimmed, ((0, 0), (2, 2), (0, 0))).astype(jnp.float32)
    taps = []
    grad_hidden = jnp.zeros((nrows, ncols, hslice), jnp.float32)
    for row_tap in range(5):
        for col_tap in range(5):
            taps.append(
                jnp.sum(
                    padded[row_tap : row_tap + nrows, col_tap : col_tap + ncols] * grad_pre_f,
                    axis=(0, 1),
                )
            )
            grad_hidden = (
                grad_hidden
                + depth_k[5 * row_tap + col_tap]
                * grad_pad[4 - row_tap : 4 - row_tap + nrows, 4 - col_tap : 4 - col_tap + ncols]
            )
    grad_k = jnp.stack(taps, axis=0)
    grad_act = (grad_hidden * slope_one).astype(jnp.bfloat16)
    flat_act = grad_act.reshape(nrows * ncols, hslice)
    grad_b1 = jnp.sum(flat_act.astype(jnp.float32), axis=0)
    grad_w1 = jnp.dot(flat_inputs.T, flat_act, preferred_element_type=jnp.float32)
    part = jnp.einsum("rwh,ch->rwc", grad_act, expand_w, preferred_element_type=jnp.float32)
    part = part.reshape((4, -1) + part.shape[1:])
    small = jnp.concatenate([grad_k, grad_b1[None], grad_bd[None]], axis=0)
    taps_count = grad_k.shape[0]
    small = jnp.pad(small, ((0, -small.shape[0] % 8), (0, 0)))
    nx, nz = lax.axis_size("x"), lax.axis_size("z")
    w1, w2, small, input_grad = row_group_allreduce([grad_w1, grad_w2, small], nx, nz, part, cotangent)
    summed = [w1, small[taps_count], small[:taps_count], small[taps_count + 1], w2]
    return (input_grad, summed[0], summed[1], summed[2], summed[3], summed[4])


def solution(mesh):
    fine = Mesh(mesh.devices.reshape(2, 8, 4, 2, 2), ROW_AXES + CHAN_AXES)
    rows = ROW_AXES + CHAN_AXES
    in_specs = (
        P(rows, None, None),
        P(rows, None, None),
        P(None, CHAN_AXES),
        P(CHAN_AXES),
        P(None, CHAN_AXES),
        P(CHAN_AXES),
        P(CHAN_AXES, None),
    )
    out_specs = (
        P(rows, None, None),
        P(None, CHAN_AXES),
        P(CHAN_AXES),
        P(None, CHAN_AXES),
        P(CHAN_AXES),
        P(CHAN_AXES, None),
    )
    return jax.shard_map(shards, mesh=fine, in_specs=in_specs, out_specs=out_specs, check_vma=False)
```

```python
import jax
import jax.numpy as jnp
from jax import lax
from jax.experimental import pallas as pl
from jax.experimental.pallas import tpu as pltpu
from jax.sharding import Mesh, PartitionSpec as P

MESH_ID = pl.DeviceIdType.MESH
ALL_AXES = ("y_lo", "z", "x", "y_hi", "core")
ROW_AXES = ("y_lo", "z", "x")
CHAN_AXES = ("y_hi", "core")


def _sum_kernel(nx, nz, data, part, cot, out, grad_out, xs, zs, ys, fin, from_pair, from_far, relay, sems):
    (xsend, xrecv, zsend, zrecv, ysend, yrecv, gzsend, gzrecv, gxsend, gxrecv, csems, local) = sems
    coords = [lax.axis_index(a) for a in ALL_AXES]
    iy, iz, ix = coords[0], coords[1], coords[2]
    hi, core = coords[3], coords[4]
    me = hi * 2 + core
    pair_at = hi * 2 + (1 - core)
    far_at = (1 - hi) * 2 + core
    diag_at = (1 - hi) * 2 + (1 - core)
    pair = (iy, iz, ix, hi, 1 - core)
    far = (iy, iz, ix, 1 - hi, core)

    def dev(y=None, z=None, x=None):
        c = list(coords)
        if y is not None:
            c[0] = y
        if z is not None:
            c[1] = z
        if x is not None:
            c[2] = x
        return tuple(c)

    x_next = [dev(x=lax.rem(ix + 1, nx)), dev(x=lax.rem(ix + nx - 1, nx))]
    z_next = [dev(z=lax.rem(iz + 1, nz)), dev(z=lax.rem(iz + nz - 1, nz))]
    partner = dev(y=1 - iy)

    barrier = pltpu.get_barrier_semaphore()
    z_peer = [None] + [dev(z=lax.rem(iz + d, nz)) for d in range(1, nz)]
    peers = [x_next[0], x_next[1], partner, pair, far] + z_peer[1:]
    if nx == 2:
        peers = peers[1:]
    for d in peers:
        pl.semaphore_signal(barrier, inc=1, device_id=d, device_id_type=MESH_ID)
    pl.semaphore_wait(barrier, len(peers))

    chan_one = []
    for j, src in enumerate((part.at[pair_at], part.at[diag_at])):
        c = pltpu.make_async_remote_copy(
            src_ref=src, dst_ref=from_pair.at[j], send_sem=csems.at[0, j],
            recv_sem=csems.at[1, j], device_id=pair, device_id_type=MESH_ID)
        c.start()
        chan_one.append(c)

    rows, cols = data.shape
    half = cols // 2
    bx = rows // nx
    bz = bx // (nz // 2)
    lanes = half // 2
    steps = (1, -1)

    def xblock(h, k):
        return (pl.ds(pl.multiple_of(lax.rem(k + 4 * nx, nx) * bx, 8), bx), pl.ds(h * half, half))

    def zblock(k):
        k = lax.rem(k + 4 * nz, nz)
        return (pl.ds(pl.multiple_of((k // 2) * bz, 8), bz), pl.ds(pl.multiple_of(lax.rem(k, 2) * lanes, 128), lanes))

    def oblock(h, kx, kz):
        r, c = zblock(kz)
        start = pl.multiple_of(lax.rem(kx + 4 * nx, nx) * bx + r.start, 8)
        return (pl.ds(start, bz), pl.ds(pl.multiple_of(h * half + c.start, 128), lanes))

    def obig(h, kx):
        return xblock(h, kx)

    for s in range(nx - 1):
        copies = []
        for h in range(2):
            sg = steps[h]
            src = data.at[xblock(h, ix - sg)] if s == 0 else xs.at[h, s - 1]
            c = pltpu.make_async_remote_copy(
                src_ref=src, dst_ref=xs.at[h, s], send_sem=xsend.at[h * nx + s],
                recv_sem=xrecv.at[h * nx + s], device_id=x_next[h], device_id_type=MESH_ID)
            c.start()
            copies.append(c)
        for h in range(2):
            sg = steps[h]
            copies[h].wait_recv()
            r, c = xblock(h, ix - sg * (s + 2))
            xs[h, s] = xs[h, s] + data[r, c]
            copies[h].wait_send()
    last = nx - 2
    for c in chan_one:
        c.wait_recv()
    relay[...] = part[far_at] + from_pair[1]
    chan_two = pltpu.make_async_remote_copy(
        src_ref=relay, dst_ref=from_far, send_sem=csems.at[0, 2],
        recv_sem=csems.at[1, 2], device_id=far, device_id_type=MESH_ID)
    chan_two.start()
    copies = []
    for h in range(2):
        for d in range(1, nz):
            c = pltpu.make_async_remote_copy(
                src_ref=xs.at[(h, last) + zblock(iz + d)], dst_ref=zs.at[h, d - 1],
                send_sem=zsend.at[h * nz + d], recv_sem=zrecv.at[h * nz + d],
                device_id=z_peer[d], device_id_type=MESH_ID)
            c.start()
            copies.append(c)
    own = [pltpu.make_async_copy(xs.at[(h, last) + zblock(iz)], zs.at[h, nz - 1], local.at[h]) for h in range(2)]
    for c in own:
        c.start()
    for c in own:
        c.wait()
    for h in range(2):
        for c in copies[h * (nz - 1) : (h + 1) * (nz - 1)]:
            c.wait_recv()
        acc = zs[h, nz - 1]
        for d in range(1, nz):
            acc = acc + zs[h, d - 1]
        zs[h, nz] = acc
    for c in copies:
        c.wait_send()
    zl = nz
    chan_two.wait_recv()
    total = part[me] + from_pair[0] + from_far[...]
    grad_out[...] = (cot[...].astype(jnp.float32) + total).astype(grad_out.dtype)
    c = pltpu.make_async_remote_copy(
        src_ref=zs.at[:, zl], dst_ref=ys, send_sem=ysend.at[0], recv_sem=yrecv.at[0],
        device_id=partner, device_id_type=MESH_ID)
    c.start()
    c.wait_recv()
    for h in range(2):
        fin[h] = zs[h, zl] + ys[h]
    placed = [pltpu.make_async_copy(fin.at[h], out.at[oblock(h, ix, iz)], local.at[2 + h]) for h in range(2)]
    for p in placed:
        p.start()
    for p in placed:
        p.wait()
    c.wait_send()
    copies = []
    for h in range(2):
        loc = oblock(h, ix, iz)
        for d in range(1, nz):
            c = pltpu.make_async_remote_copy(
                src_ref=out.at[loc], dst_ref=out.at[loc], send_sem=gzsend.at[h * nz + d],
                recv_sem=gzrecv.at[h * nz + d], device_id=z_peer[d], device_id_type=MESH_ID)
            c.start()
            copies.append(c)
    for c in copies:
        c.wait_recv()
    for c in copies:
        c.wait_send()
    first = [[None, None], [None, None]]
    for h in range(2):
        loc = obig(h, ix)
        for j in range(2):
            c = pltpu.make_async_remote_copy(
                src_ref=out.at[loc], dst_ref=out.at[loc], send_sem=gxsend.at[h * nx + j],
                recv_sem=gxrecv.at[h * nx + j], device_id=x_next[j], device_id_type=MESH_ID)
            c.start()
            first[h][j] = c
    second = []
    for h in range(2):
        first[h][h].wait_recv()
        loc = obig(h, ix - steps[h])
        c = pltpu.make_async_remote_copy(
            src_ref=out.at[loc], dst_ref=out.at[loc], send_sem=gxsend.at[h * nx + 2],
            recv_sem=gxrecv.at[h * nx + 2], device_id=x_next[h], device_id_type=MESH_ID)
        c.start()
        second.append(c)
    for h in range(2):
        first[h][1 - h].wait_recv()
    for c in second:
        c.wait_recv()
    for c in first[0] + first[1] + second:
        c.wait_send()

    for c in chan_one:
        c.wait_send()
    chan_two.wait_send()

def row_group_allreduce(pieces, nx, nz, part, cot):
    cols = pieces[0].shape[-1]
    layout = []
    at = 0
    for piece in pieces:
        layout.append((at, piece.shape[0]))
        at += piece.shape[0]
    quantum = 8 * nx * (nz // 2)
    rows = -(-at // quantum) * quantum
    used = at
    count = len(pieces)
    half = cols // 2
    bx = rows // nx
    bz = bx // (nz // 2)
    sems = [pltpu.SemaphoreType.DMA((2 * nx,)), pltpu.SemaphoreType.DMA((2 * nx,)),
            pltpu.SemaphoreType.DMA((2 * nz,)), pltpu.SemaphoreType.DMA((2 * nz,)),
            pltpu.SemaphoreType.DMA((1,)), pltpu.SemaphoreType.DMA((1,)),
            pltpu.SemaphoreType.DMA((2 * nz,)), pltpu.SemaphoreType.DMA((2 * nz,)),
            pltpu.SemaphoreType.DMA((2 * nx,)), pltpu.SemaphoreType.DMA((2 * nx,)),
            pltpu.SemaphoreType.DMA((2, 3)), pltpu.SemaphoreType.DMA((4,)),
            pltpu.SemaphoreType.DMA((2 * count,))]
    block = part.shape[1:]

    def body(*refs):
        ins, outs = refs[:count], refs[count + 2 : 2 * count + 2]
        part, cot, grad_out = refs[count], refs[count + 1], refs[2 * count + 2]
        data, out, xs, zs, ys, fin, from_pair, from_far, relay = refs[2 * count + 3 : 2 * count + 12]
        s = refs[2 * count + 12 :]
        moves = s[-1]
        packs = [pltpu.make_async_copy(ref, data.at[pl.ds(at, size)], moves.at[i])
                 for i, (ref, (at, size)) in enumerate(zip(ins, layout))]
        for c in packs:
            c.start()
        data[used:] = jnp.zeros((rows - used, cols), jnp.float32)
        for c in packs:
            c.wait()
        _sum_kernel(nx, nz, data, part, cot, out, grad_out, xs, zs, ys, fin, from_pair, from_far, relay, s[:-1])
        unpacks = [pltpu.make_async_copy(out.at[pl.ds(at, size)], ref, moves.at[count + i])
                   for i, (ref, (at, size)) in enumerate(zip(outs, layout))]
        for c in unpacks:
            c.start()
        for c in unpacks:
            c.wait()

    return pl.pallas_call(
        body,
        out_shape=tuple(jax.ShapeDtypeStruct(p.shape, jnp.float32) for p in pieces)
        + (jax.ShapeDtypeStruct(cot.shape, cot.dtype),),
        in_specs=[pl.BlockSpec(memory_space=pltpu.VMEM)] * (count + 2),
        out_specs=(pl.BlockSpec(memory_space=pltpu.VMEM),) * (count + 1),
        scratch_shapes=[
            pltpu.VMEM((rows, cols), jnp.float32),
            pltpu.VMEM((rows, cols), jnp.float32),
            pltpu.VMEM((2, nx - 1, bx, half), jnp.float32),
            pltpu.VMEM((2, nz + 1, bz, half // 2), jnp.float32),
            pltpu.VMEM((2, bz, half // 2), jnp.float32),
            pltpu.VMEM((2, bz, half // 2), jnp.float32),
            pltpu.VMEM((2,) + block, jnp.float32),
            pltpu.VMEM(block, jnp.float32),
            pltpu.VMEM(block, jnp.float32),
        ] + sems,
        compiler_params=pltpu.CompilerParams(collective_id=0, has_side_effects=True,
                                             vmem_limit_bytes=48 * 1024 * 1024),
    )(*pieces, part, cot)


def _chan_gather_kernel(first, second, out_first, out_second, sems):
    coords = [lax.axis_index(a) for a in ALL_AXES]
    hi, core = coords[3], coords[4]

    def dev(h, c):
        return (coords[0], coords[1], coords[2], h, c)

    me = hi * 2 + core
    across = hi * 2 + (1 - core)
    over = (1 - hi) * 2 + core
    pair, far = dev(hi, 1 - core), dev(1 - hi, core)

    barrier = pltpu.get_barrier_semaphore()
    for d in (pair, far):
        pl.semaphore_signal(barrier, inc=1, device_id=d, device_id_type=MESH_ID)
    pl.semaphore_wait(barrier, 2)

    sources = (first, second)
    outs = (out_first, out_second)
    step_one = [None] * 4
    for j, target in ((1, far), (0, pair)):
        for k in range(2):
            c = pltpu.make_async_remote_copy(
                src_ref=sources[k], dst_ref=outs[k].at[me], send_sem=sems.at[0, k, j],
                recv_sem=sems.at[1, k, j], device_id=target, device_id_type=MESH_ID)
            c.start()
            step_one[2 * k + j] = c
    for k in range(2):
        outs[k][me] = sources[k][...]
    relay = []
    for k in range(2):
        step_one[2 * k + 1].wait_recv()
        c = pltpu.make_async_remote_copy(
            src_ref=outs[k].at[over], dst_ref=outs[k].at[over], send_sem=sems.at[0, k, 2],
            recv_sem=sems.at[1, k, 2], device_id=pair, device_id_type=MESH_ID)
        c.start()
        relay.append(c)
    for k in range(2):
        step_one[2 * k].wait_recv()
    for c in relay:
        c.wait_recv()
    for c in step_one + relay:
        c.wait_send()


def chan_gather(first, second):
    shape = (4,) + first.shape
    result = pl.pallas_call(
        _chan_gather_kernel,
        out_shape=(jax.ShapeDtypeStruct(shape, first.dtype), jax.ShapeDtypeStruct(shape, second.dtype)),
        in_specs=[pl.BlockSpec(memory_space=pltpu.VMEM)] * 2,
        out_specs=(pl.BlockSpec(memory_space=pltpu.VMEM),) * 2,
        scratch_shapes=[pltpu.SemaphoreType.DMA((2, 2, 3))],
        compiler_params=pltpu.CompilerParams(collective_id=1, has_side_effects=True),
    )(first, second)
    return tuple(r.reshape((-1,) + first.shape[1:]) for r in result)


def extended(block, sides, width):
    for axis, dim in sides:
        count = 1
        for name in axis:
            count *= lax.axis_size(name)
        forward = [(i, i + 1) for i in range(count - 1)]
        backward = [(target, source) for source, target in forward]
        low = lax.ppermute(
            lax.slice_in_dim(block, block.shape[dim] - width, None, axis=dim), axis, forward
        )
        high = lax.ppermute(lax.slice_in_dim(block, 0, width, axis=dim), axis, backward)
        block = jnp.concatenate([low, block, high], axis=dim)
    return block


def gelu_parts(pre):
    cdf = 0.5 * (1.0 + lax.erf(pre * 0.7071067811865476))
    dens = jnp.exp(-0.5 * pre * pre) * 0.3989422804014327
    return (pre * cdf, cdf + pre * dens)


def shards(inputs, cotangent, expand_w, expand_b, depth_k, depth_b, project_w):
    rows_in, rows_cot = chan_gather(inputs, cotangent)
    nrows, ncols, cin = rows_in.shape
    hslice = expand_w.shape[1]
    flat_inputs = rows_in.reshape(nrows * ncols, cin)
    flat_cotan = rows_cot.reshape(nrows * ncols, cin)
    pre_one = (
        jnp.dot(flat_inputs, expand_w, preferred_element_type=jnp.float32).reshape(
            nrows, ncols, hslice
        )
        + expand_b
    )
    hidden, slope_one = gelu_parts(pre_one)
    hidden = hidden.astype(jnp.bfloat16)
    rimmed = extended(hidden, ((ROW_AXES, 0),), 2)
    padded = jnp.pad(rimmed, ((0, 0), (2, 2), (0, 0))).astype(jnp.float32)
    pre_two = jnp.zeros((nrows, ncols, hslice), jnp.float32) + depth_b
    for row_tap in range(5):
        for col_tap in range(5):
            pre_two = (
                pre_two
                + depth_k[5 * row_tap + col_tap]
                * padded[row_tap : row_tap + nrows, col_tap : col_tap + ncols]
            )
    mixed, slope_two = gelu_parts(pre_two)
    mixed = mixed.astype(jnp.bfloat16).reshape(nrows * ncols, hslice)
    grad_w2 = jnp.dot(mixed.T, flat_cotan, preferred_element_type=jnp.float32)
    grad_mixed = jnp.dot(flat_cotan, project_w.T, preferred_element_type=jnp.float32).reshape(
        nrows, ncols, hslice
    )
    grad_pre = (grad_mixed * slope_two).astype(jnp.bfloat16)
    grad_pre_f = grad_pre.astype(jnp.float32)
    grad_bd = jnp.sum(grad_pre_f, axis=(0, 1))
    grad_rimmed = extended(grad_pre, ((ROW_AXES, 0),), 2)
    grad_pad = jnp.pad(grad_rimmed, ((0, 0), (2, 2), (0, 0))).astype(jnp.float32)
    taps = []
    grad_hidden = jnp.zeros((nrows, ncols, hslice), jnp.float32)
    for row_tap in range(5):
        for col_tap in range(5):
            taps.append(
                jnp.sum(
                    padded[row_tap : row_tap + nrows, col_tap : col_tap + ncols] * grad_pre_f,
                    axis=(0, 1),
                )
            )
            grad_hidden = (
                grad_hidden
                + depth_k[5 * row_tap + col_tap]
                * grad_pad[4 - row_tap : 4 - row_tap + nrows, 4 - col_tap : 4 - col_tap + ncols]
            )
    grad_k = jnp.stack(taps, axis=0)
    grad_act = (grad_hidden * slope_one).astype(jnp.bfloat16)
    flat_act = grad_act.reshape(nrows * ncols, hslice)
    grad_b1 = jnp.sum(flat_act.astype(jnp.float32), axis=0)
    grad_w1 = jnp.dot(flat_inputs.T, flat_act, preferred_element_type=jnp.float32)
    part = jnp.einsum("rwh,ch->rwc", grad_act, expand_w, preferred_element_type=jnp.float32)
    part = part.reshape((4, -1) + part.shape[1:])
    small = jnp.concatenate([grad_k, grad_b1[None], grad_bd[None]], axis=0)
    taps_count = grad_k.shape[0]
    small = jnp.pad(small, ((0, -small.shape[0] % 8), (0, 0)))
    nx, nz = lax.axis_size("x"), lax.axis_size("z")
    w1, w2, small, input_grad = row_group_allreduce([grad_w1, grad_w2, small], nx, nz, part, cotangent)
    summed = [w1, small[taps_count], small[:taps_count], small[taps_count + 1], w2]
    return (input_grad, summed[0], summed[1], summed[2], summed[3], summed[4])


def solution(mesh):
    fine = Mesh(mesh.devices.reshape(2, 8, 4, 2, 2), ROW_AXES + CHAN_AXES)
    rows = ROW_AXES + CHAN_AXES
    in_specs = (
        P(rows, None, None),
        P(rows, None, None),
        P(None, CHAN_AXES),
        P(CHAN_AXES),
        P(None, CHAN_AXES),
        P(CHAN_AXES),
        P(CHAN_AXES, None),
    )
    out_specs = (
        P(rows, None, None),
        P(None, CHAN_AXES),
        P(CHAN_AXES),
        P(None, CHAN_AXES),
        P(CHAN_AXES),
        P(CHAN_AXES, None),
    )
    return jax.shard_map(shards, mesh=fine, in_specs=in_specs, out_specs=out_specs, check_vma=False)
```

```python
import jax
import jax.numpy as jnp
from jax import lax
from jax.experimental import pallas as pl
from jax.experimental.pallas import tpu as pltpu
from jax.sharding import Mesh, PartitionSpec as P

MESH_ID = pl.DeviceIdType.MESH
ALL_AXES = ("y_lo", "z", "x", "y_hi", "core")
ROW_AXES = ("y_lo", "z", "x")
CHAN_AXES = ("y_hi", "core")


def _sum_kernel(nx, nz, data, part, cot, out, grad_out, xs, zs, ys, fin, from_pair, from_far, relay, sems):
    (xsend, xrecv, zsend, zrecv, ysend, yrecv, gzsend, gzrecv, gxsend, gxrecv, csems, local) = sems
    coords = [lax.axis_index(a) for a in ALL_AXES]
    iy, iz, ix = coords[0], coords[1], coords[2]
    hi, core = coords[3], coords[4]
    me = hi * 2 + core
    pair_at = hi * 2 + (1 - core)
    far_at = (1 - hi) * 2 + core
    diag_at = (1 - hi) * 2 + (1 - core)
    pair = (iy, iz, ix, hi, 1 - core)
    far = (iy, iz, ix, 1 - hi, core)

    def dev(y=None, z=None, x=None):
        c = list(coords)
        if y is not None:
            c[0] = y
        if z is not None:
            c[1] = z
        if x is not None:
            c[2] = x
        return tuple(c)

    x_next = [dev(x=lax.rem(ix + 1, nx)), dev(x=lax.rem(ix + nx - 1, nx))]
    z_next = [dev(z=lax.rem(iz + 1, nz)), dev(z=lax.rem(iz + nz - 1, nz))]
    partner = dev(y=1 - iy)

    barrier = pltpu.get_barrier_semaphore()
    z_peer = [None] + [dev(z=lax.rem(iz + d, nz)) for d in range(1, nz)]
    peers = [x_next[0], x_next[1], partner, pair, far] + z_peer[1:]
    if nx == 2:
        peers = peers[1:]
    for d in peers:
        pl.semaphore_signal(barrier, inc=1, device_id=d, device_id_type=MESH_ID)
    pl.semaphore_wait(barrier, len(peers))


    rows, cols = data.shape
    half = cols // 2
    bx = rows // nx
    bz = bx // (nz // 2)
    lanes = half // 2
    steps = (1, -1)

    def xblock(h, k):
        return (pl.ds(pl.multiple_of(lax.rem(k + 4 * nx, nx) * bx, 8), bx), pl.ds(h * half, half))

    def zblock(k):
        k = lax.rem(k + 4 * nz, nz)
        return (pl.ds(pl.multiple_of((k // 2) * bz, 8), bz), pl.ds(pl.multiple_of(lax.rem(k, 2) * lanes, 128), lanes))

    def oblock(h, kx, kz):
        r, c = zblock(kz)
        start = pl.multiple_of(lax.rem(kx + 4 * nx, nx) * bx + r.start, 8)
        return (pl.ds(start, bz), pl.ds(pl.multiple_of(h * half + c.start, 128), lanes))

    def obig(h, kx):
        return xblock(h, kx)

    for s in range(nx - 1):
        copies = []
        for h in range(2):
            sg = steps[h]
            src = data.at[xblock(h, ix - sg)] if s == 0 else xs.at[h, s - 1]
            c = pltpu.make_async_remote_copy(
                src_ref=src, dst_ref=xs.at[h, s], send_sem=xsend.at[h * nx + s],
                recv_sem=xrecv.at[h * nx + s], device_id=x_next[h], device_id_type=MESH_ID)
            c.start()
            copies.append(c)
        if s == 0:
            chan_one = []
            for j, src in enumerate((part.at[pair_at], part.at[diag_at])):
                c = pltpu.make_async_remote_copy(
                    src_ref=src, dst_ref=from_pair.at[j], send_sem=csems.at[0, j],
                    recv_sem=csems.at[1, j], device_id=pair, device_id_type=MESH_ID)
                c.start()
                chan_one.append(c)
        for h in range(2):
            sg = steps[h]
            copies[h].wait_recv()
            r, c = xblock(h, ix - sg * (s + 2))
            xs[h, s] = xs[h, s] + data[r, c]
            copies[h].wait_send()
    last = nx - 2
    for c in chan_one:
        c.wait_recv()
    relay[...] = part[far_at] + from_pair[1]
    chan_two = pltpu.make_async_remote_copy(
        src_ref=relay, dst_ref=from_far, send_sem=csems.at[0, 2],
        recv_sem=csems.at[1, 2], device_id=far, device_id_type=MESH_ID)
    chan_two.start()
    copies = []
    for h in range(2):
        for d in range(1, nz):
            c = pltpu.make_async_remote_copy(
                src_ref=xs.at[(h, last) + zblock(iz + d)], dst_ref=zs.at[h, d - 1],
                send_sem=zsend.at[h * nz + d], recv_sem=zrecv.at[h * nz + d],
                device_id=z_peer[d], device_id_type=MESH_ID)
            c.start()
            copies.append(c)
    own = [pltpu.make_async_copy(xs.at[(h, last) + zblock(iz)], zs.at[h, nz - 1], local.at[h]) for h in range(2)]
    for c in own:
        c.start()
    for c in own:
        c.wait()
    for h in range(2):
        for c in copies[h * (nz - 1) : (h + 1) * (nz - 1)]:
            c.wait_recv()
        acc = zs[h, nz - 1]
        for d in range(1, nz):
            acc = acc + zs[h, d - 1]
        zs[h, nz] = acc
    for c in copies:
        c.wait_send()
    zl = nz
    chan_two.wait_recv()
    total = part[me] + from_pair[0] + from_far[...]
    grad_out[...] = (cot[...].astype(jnp.float32) + total).astype(grad_out.dtype)
    c = pltpu.make_async_remote_copy(
        src_ref=zs.at[:, zl], dst_ref=ys, send_sem=ysend.at[0], recv_sem=yrecv.at[0],
        device_id=partner, device_id_type=MESH_ID)
    c.start()
    c.wait_recv()
    for h in range(2):
        fin[h] = zs[h, zl] + ys[h]
    placed = [pltpu.make_async_copy(fin.at[h], out.at[oblock(h, ix, iz)], local.at[2 + h]) for h in range(2)]
    for p in placed:
        p.start()
    for p in placed:
        p.wait()
    c.wait_send()
    copies = []
    for h in range(2):
        loc = oblock(h, ix, iz)
        for d in range(1, nz):
            c = pltpu.make_async_remote_copy(
                src_ref=out.at[loc], dst_ref=out.at[loc], send_sem=gzsend.at[h * nz + d],
                recv_sem=gzrecv.at[h * nz + d], device_id=z_peer[d], device_id_type=MESH_ID)
            c.start()
            copies.append(c)
    for c in copies:
        c.wait_recv()
    for c in copies:
        c.wait_send()
    first = [[None, None], [None, None]]
    for h in range(2):
        loc = obig(h, ix)
        for j in range(2):
            c = pltpu.make_async_remote_copy(
                src_ref=out.at[loc], dst_ref=out.at[loc], send_sem=gxsend.at[h * nx + j],
                recv_sem=gxrecv.at[h * nx + j], device_id=x_next[j], device_id_type=MESH_ID)
            c.start()
            first[h][j] = c
    second = []
    for h in range(2):
        first[h][h].wait_recv()
        loc = obig(h, ix - steps[h])
        c = pltpu.make_async_remote_copy(
            src_ref=out.at[loc], dst_ref=out.at[loc], send_sem=gxsend.at[h * nx + 2],
            recv_sem=gxrecv.at[h * nx + 2], device_id=x_next[h], device_id_type=MESH_ID)
        c.start()
        second.append(c)
    for h in range(2):
        first[h][1 - h].wait_recv()
    for c in second:
        c.wait_recv()
    for c in first[0] + first[1] + second:
        c.wait_send()

    for c in chan_one:
        c.wait_send()
    chan_two.wait_send()

def row_group_allreduce(pieces, nx, nz, part, cot):
    cols = pieces[0].shape[-1]
    layout = []
    at = 0
    for piece in pieces:
        layout.append((at, piece.shape[0]))
        at += piece.shape[0]
    quantum = 8 * nx * (nz // 2)
    rows = -(-at // quantum) * quantum
    used = at
    count = len(pieces)
    half = cols // 2
    bx = rows // nx
    bz = bx // (nz // 2)
    sems = [pltpu.SemaphoreType.DMA((2 * nx,)), pltpu.SemaphoreType.DMA((2 * nx,)),
            pltpu.SemaphoreType.DMA((2 * nz,)), pltpu.SemaphoreType.DMA((2 * nz,)),
            pltpu.SemaphoreType.DMA((1,)), pltpu.SemaphoreType.DMA((1,)),
            pltpu.SemaphoreType.DMA((2 * nz,)), pltpu.SemaphoreType.DMA((2 * nz,)),
            pltpu.SemaphoreType.DMA((2 * nx,)), pltpu.SemaphoreType.DMA((2 * nx,)),
            pltpu.SemaphoreType.DMA((2, 3)), pltpu.SemaphoreType.DMA((4,)),
            pltpu.SemaphoreType.DMA((2 * count,))]
    block = part.shape[1:]

    def body(*refs):
        ins, outs = refs[:count], refs[count + 2 : 2 * count + 2]
        part, cot, grad_out = refs[count], refs[count + 1], refs[2 * count + 2]
        data, out, xs, zs, ys, fin, from_pair, from_far, relay = refs[2 * count + 3 : 2 * count + 12]
        s = refs[2 * count + 12 :]
        moves = s[-1]
        packs = [pltpu.make_async_copy(ref, data.at[pl.ds(at, size)], moves.at[i])
                 for i, (ref, (at, size)) in enumerate(zip(ins, layout))]
        for c in packs:
            c.start()
        data[used:] = jnp.zeros((rows - used, cols), jnp.float32)
        for c in packs:
            c.wait()
        _sum_kernel(nx, nz, data, part, cot, out, grad_out, xs, zs, ys, fin, from_pair, from_far, relay, s[:-1])
        unpacks = [pltpu.make_async_copy(out.at[pl.ds(at, size)], ref, moves.at[count + i])
                   for i, (ref, (at, size)) in enumerate(zip(outs, layout))]
        for c in unpacks:
            c.start()
        for c in unpacks:
            c.wait()

    return pl.pallas_call(
        body,
        out_shape=tuple(jax.ShapeDtypeStruct(p.shape, jnp.float32) for p in pieces)
        + (jax.ShapeDtypeStruct(cot.shape, cot.dtype),),
        in_specs=[pl.BlockSpec(memory_space=pltpu.VMEM)] * (count + 2),
        out_specs=(pl.BlockSpec(memory_space=pltpu.VMEM),) * (count + 1),
        scratch_shapes=[
            pltpu.VMEM((rows, cols), jnp.float32),
            pltpu.VMEM((rows, cols), jnp.float32),
            pltpu.VMEM((2, nx - 1, bx, half), jnp.float32),
            pltpu.VMEM((2, nz + 1, bz, half // 2), jnp.float32),
            pltpu.VMEM((2, bz, half // 2), jnp.float32),
            pltpu.VMEM((2, bz, half // 2), jnp.float32),
            pltpu.VMEM((2,) + block, jnp.float32),
            pltpu.VMEM(block, jnp.float32),
            pltpu.VMEM(block, jnp.float32),
        ] + sems,
        compiler_params=pltpu.CompilerParams(collective_id=0, has_side_effects=True,
                                             vmem_limit_bytes=48 * 1024 * 1024),
    )(*pieces, part, cot)


def _chan_gather_kernel(first, second, out_first, out_second, sems):
    coords = [lax.axis_index(a) for a in ALL_AXES]
    hi, core = coords[3], coords[4]

    def dev(h, c):
        return (coords[0], coords[1], coords[2], h, c)

    me = hi * 2 + core
    across = hi * 2 + (1 - core)
    over = (1 - hi) * 2 + core
    pair, far = dev(hi, 1 - core), dev(1 - hi, core)

    barrier = pltpu.get_barrier_semaphore()
    for d in (pair, far):
        pl.semaphore_signal(barrier, inc=1, device_id=d, device_id_type=MESH_ID)
    pl.semaphore_wait(barrier, 2)

    sources = (first, second)
    outs = (out_first, out_second)
    step_one = [None] * 4
    for j, target in ((1, far), (0, pair)):
        for k in range(2):
            c = pltpu.make_async_remote_copy(
                src_ref=sources[k], dst_ref=outs[k].at[me], send_sem=sems.at[0, k, j],
                recv_sem=sems.at[1, k, j], device_id=target, device_id_type=MESH_ID)
            c.start()
            step_one[2 * k + j] = c
    for k in range(2):
        outs[k][me] = sources[k][...]
    relay = []
    for k in range(2):
        step_one[2 * k + 1].wait_recv()
        c = pltpu.make_async_remote_copy(
            src_ref=outs[k].at[over], dst_ref=outs[k].at[over], send_sem=sems.at[0, k, 2],
            recv_sem=sems.at[1, k, 2], device_id=pair, device_id_type=MESH_ID)
        c.start()
        relay.append(c)
    for k in range(2):
        step_one[2 * k].wait_recv()
    for c in relay:
        c.wait_recv()
    for c in step_one + relay:
        c.wait_send()


def chan_gather(first, second):
    shape = (4,) + first.shape
    result = pl.pallas_call(
        _chan_gather_kernel,
        out_shape=(jax.ShapeDtypeStruct(shape, first.dtype), jax.ShapeDtypeStruct(shape, second.dtype)),
        in_specs=[pl.BlockSpec(memory_space=pltpu.VMEM)] * 2,
        out_specs=(pl.BlockSpec(memory_space=pltpu.VMEM),) * 2,
        scratch_shapes=[pltpu.SemaphoreType.DMA((2, 2, 3))],
        compiler_params=pltpu.CompilerParams(collective_id=1, has_side_effects=True),
    )(first, second)
    return tuple(r.reshape((-1,) + first.shape[1:]) for r in result)


def extended(block, sides, width):
    for axis, dim in sides:
        count = 1
        for name in axis:
            count *= lax.axis_size(name)
        forward = [(i, i + 1) for i in range(count - 1)]
        backward = [(target, source) for source, target in forward]
        low = lax.ppermute(
            lax.slice_in_dim(block, block.shape[dim] - width, None, axis=dim), axis, forward
        )
        high = lax.ppermute(lax.slice_in_dim(block, 0, width, axis=dim), axis, backward)
        block = jnp.concatenate([low, block, high], axis=dim)
    return block


def gelu_parts(pre):
    cdf = 0.5 * (1.0 + lax.erf(pre * 0.7071067811865476))
    dens = jnp.exp(-0.5 * pre * pre) * 0.3989422804014327
    return (pre * cdf, cdf + pre * dens)


def shards(inputs, cotangent, expand_w, expand_b, depth_k, depth_b, project_w):
    rows_in, rows_cot = chan_gather(inputs, cotangent)
    nrows, ncols, cin = rows_in.shape
    hslice = expand_w.shape[1]
    flat_inputs = rows_in.reshape(nrows * ncols, cin)
    flat_cotan = rows_cot.reshape(nrows * ncols, cin)
    pre_one = (
        jnp.dot(flat_inputs, expand_w, preferred_element_type=jnp.float32).reshape(
            nrows, ncols, hslice
        )
        + expand_b
    )
    hidden, slope_one = gelu_parts(pre_one)
    hidden = hidden.astype(jnp.bfloat16)
    rimmed = extended(hidden, ((ROW_AXES, 0),), 2)
    padded = jnp.pad(rimmed, ((0, 0), (2, 2), (0, 0))).astype(jnp.float32)
    pre_two = jnp.zeros((nrows, ncols, hslice), jnp.float32) + depth_b
    for row_tap in range(5):
        for col_tap in range(5):
            pre_two = (
                pre_two
                + depth_k[5 * row_tap + col_tap]
                * padded[row_tap : row_tap + nrows, col_tap : col_tap + ncols]
            )
    mixed, slope_two = gelu_parts(pre_two)
    mixed = mixed.astype(jnp.bfloat16).reshape(nrows * ncols, hslice)
    grad_w2 = jnp.dot(mixed.T, flat_cotan, preferred_element_type=jnp.float32)
    grad_mixed = jnp.dot(flat_cotan, project_w.T, preferred_element_type=jnp.float32).reshape(
        nrows, ncols, hslice
    )
    grad_pre = (grad_mixed * slope_two).astype(jnp.bfloat16)
    grad_pre_f = grad_pre.astype(jnp.float32)
    grad_bd = jnp.sum(grad_pre_f, axis=(0, 1))
    grad_rimmed = extended(grad_pre, ((ROW_AXES, 0),), 2)
    grad_pad = jnp.pad(grad_rimmed, ((0, 0), (2, 2), (0, 0))).astype(jnp.float32)
    taps = []
    grad_hidden = jnp.zeros((nrows, ncols, hslice), jnp.float32)
    for row_tap in range(5):
        for col_tap in range(5):
            taps.append(
                jnp.sum(
                    padded[row_tap : row_tap + nrows, col_tap : col_tap + ncols] * grad_pre_f,
                    axis=(0, 1),
                )
            )
            grad_hidden = (
                grad_hidden
                + depth_k[5 * row_tap + col_tap]
                * grad_pad[4 - row_tap : 4 - row_tap + nrows, 4 - col_tap : 4 - col_tap + ncols]
            )
    grad_k = jnp.stack(taps, axis=0)
    grad_act = (grad_hidden * slope_one).astype(jnp.bfloat16)
    flat_act = grad_act.reshape(nrows * ncols, hslice)
    grad_b1 = jnp.sum(flat_act.astype(jnp.float32), axis=0)
    grad_w1 = jnp.dot(flat_inputs.T, flat_act, preferred_element_type=jnp.float32)
    part = jnp.einsum("rwh,ch->rwc", grad_act, expand_w, preferred_element_type=jnp.float32)
    part = part.reshape((4, -1) + part.shape[1:])
    small = jnp.concatenate([grad_k, grad_b1[None], grad_bd[None]], axis=0)
    taps_count = grad_k.shape[0]
    small = jnp.pad(small, ((0, -small.shape[0] % 8), (0, 0)))
    nx, nz = lax.axis_size("x"), lax.axis_size("z")
    w1, w2, small, input_grad = row_group_allreduce([grad_w1, grad_w2, small], nx, nz, part, cotangent)
    summed = [w1, small[taps_count], small[:taps_count], small[taps_count + 1], w2]
    return (input_grad, summed[0], summed[1], summed[2], summed[3], summed[4])


def solution(mesh):
    fine = Mesh(mesh.devices.reshape(2, 8, 4, 2, 2), ROW_AXES + CHAN_AXES)
    rows = ROW_AXES + CHAN_AXES
    in_specs = (
        P(rows, None, None),
        P(rows, None, None),
        P(None, CHAN_AXES),
        P(CHAN_AXES),
        P(None, CHAN_AXES),
        P(CHAN_AXES),
        P(CHAN_AXES, None),
    )
    out_specs = (
        P(rows, None, None),
        P(None, CHAN_AXES),
        P(CHAN_AXES),
        P(None, CHAN_AXES),
        P(CHAN_AXES),
        P(CHAN_AXES, None),
    )
    return jax.shard_map(shards, mesh=fine, in_specs=in_specs, out_specs=out_specs, check_vma=False)
```
